32 devices in a mesh: dp: 8 (over z, y), tensor: 4 (over x, core).
Axes of the slice: x: 2, y: 2, z: 4, core: 2. Of those that a mesh axis runs over, the one named last changes fastest.
Arguments:
- hidden_in: bfloat16 [1024, 24, 768], P('tensor', 'dp'), may hold values from -6 to 6
- doc_ids: int32 [1024, 24], P(None, 'dp'), may hold values from -1 to 7, as said below
- first_gain: bfloat16 [768], replicated, may hold values from 0.5 to 1.5
- first_shift: bfloat16 [768], replicated, may hold values from -1 to 1
- qkv_weight: bfloat16 [768, 3, 768], P(None, None, 'tensor'), may hold values from -0.3125 to 0.3125
- qv_bias: bfloat16 [2, 768], P(None, 'tensor'), may hold values from -1 to 1
- proj_weight: bfloat16 [768, 768], P('tensor'), may hold values from -0.75 to 0.75
- proj_bias: bfloat16 [768], replicated, may hold values from -1 to 1
- second_gain: bfloat16 [768], replicated, may hold values from 0.5 to 1.5
- second_shift: bfloat16 [768], replicated, may hold values from -1 to 1
- up_weight: bfloat16 [768, 3072], P(None, 'tensor'), may hold values from -0.21875 to 0.21875
- up_bias: bfloat16 [3072], P('tensor'), may hold values from -1 to 1
- down_weight: bfloat16 [3072, 768], P('tensor'), may hold values from -0.15625 to 0.15625
- down_bias: bfloat16 [768], replicated, may hold values from -1 to 1
- out_grad: bfloat16 [1024, 24, 768], P('tensor', 'dp'), may hold values from -6 to 6
Outputs:
- block_out: bfloat16 [1024, 24, 768], P('tensor', 'dp')
- in_grad: bfloat16 [1024, 24, 768], P('tensor', 'dp')
- first_gain_grad: float32 [768], replicated
- first_shift_grad: float32 [768], replicated
- qkv_weight_grad: float32 [768, 3, 768], P(None, None, 'tensor')
- qv_bias_grad: float32 [2, 768], P(None, 'tensor')
- proj_weight_grad: float32 [768, 768], P('tensor')
- proj_bias_grad: float32 [768], replicated
- second_gain_grad: float32 [768], replicated
- second_shift_grad: float32 [768], replicated
- up_weight_grad: float32 [768, 3072], P(None, 'tensor')
- up_bias_grad: float32 [3072], P('tensor')
- down_weight_grad: float32 [3072, 768], P('tensor')
- down_bias_grad: float32 [768], replicated
The draws below stay inside these ranges and needn't reach their ends.
Inputs may be any that keep to these rules, and one draw needn't show every extreme that they name: `doc_ids`: each sequence's 1024 positions hold exactly 8 documents with ids 0 to 7 in rising order, each id on a run of consecutive positions, followed by a tail of one to 128 positions that holds -1 (padding).
All inputs are finite; a program needn't handle non-finite values.
Results may differ from the reference program's by a relative error of at most 0.019.
Values may be sent and summed in bfloat16 or wider, within the bound.
No kernel may reach another device: no remote copies, remote signals or barrier semaphores. Data moves between devices by JAX's collectives and lax.ppermute only.
A program may use at most 128 MiB of HBM per device.

```python
import jax
import jax.numpy as jnp
from jax import lax

D = 768
HEADS = 12
HEAD_DIM = 64
FF = 3072
LEN = 1024
ROWS_DEV = 3
QBLOCK = 512
ROWS = 24
N_DP = 8


def draw_doc_ids(key, part):
    start_key, tail_key = jax.random.split(key)
    span = LEN - LEN // 8 - 1
    row_keys = jax.random.split(start_key, ROWS)

    def row_starts(row_key):
        return jax.random.permutation(row_key, span)[:7].astype(jnp.int32) + 1
    starts = jax.vmap(row_starts)(row_keys)
    position = jnp.arange(LEN, dtype=jnp.int32)[None, :]
    doc_number = jnp.sum((position[:, :, None] >= starts[:, None, :]).astype(jnp.int32), axis=2)
    tail_size = jax.random.randint(tail_key, (ROWS, 1), 1, LEN // 8 + 1)
    doc_number = jnp.where(position >= LEN - tail_size, -1, doc_number)
    return jnp.transpose(doc_number).astype(jnp.int32)


def block_levels(rng, extent, cuts, smallest, high):
    gain = 1.0
    for axis_at, blocks in cuts:
        heights = jax.random.uniform(jax.random.fold_in(jax.random.fold_in(rng, 6), axis_at), (blocks,), jnp.float32, smallest / len(cuts), high / len(cuts))
        gain = gain * jnp.repeat(jnp.exp(heights), extent[axis_at] // blocks).reshape((-1,) + (1,) * (len(extent) - 1 - axis_at))
    return gain


def centred(key, shape, spread, reach, cuts=(), held_as=jnp.bfloat16):
    level = block_levels(key, shape, cuts, -0.22, 0.18) if cuts else 1.0
    values = jax.random.normal(key, shape, jnp.float32) * spread * level
    return jnp.minimum(jnp.maximum(values, -reach), reach).astype(held_as)


def setup_inputs(seed: int = 0) -> dict:
    key_of = jax.random.split(jax.random.key(seed), 16)
    hidden_in = centred(key_of[0], (LEN, ROWS, D), 1.0, 6.0, ((0, 4), (1, 8)))
    doc_ids = draw_doc_ids(jax.random.fold_in(key_of[15], 71), 0)
    first_gain = jnp.clip(1.0 + 0.1 * jax.random.normal(key_of[2], (D,), jnp.float32), 0.5, 1.5).astype(jnp.bfloat16)
    first_shift = centred(key_of[3], (D,), 0.2, 1.0)
    qkv_weight = centred(key_of[4], (D, 3, D), (D // 2) ** -0.5, 0.3125, ((2, 4),))
    qv_bias = centred(key_of[5], (2, D), 0.2, 1.0, ((1, 4),))
    proj_weight = centred(key_of[6], (D, D), (D // 12) ** -0.5, 0.75, ((0, 4),))
    proj_bias = centred(key_of[7], (D,), 0.2, 1.0)
    second_gain = jnp.clip(1.0 + 0.1 * jax.random.normal(key_of[8], (D,), jnp.float32), 0.5, 1.5).astype(jnp.bfloat16)
    second_shift = centred(key_of[9], (D,), 0.2, 1.0)
    up_weight = centred(key_of[10], (D, FF), D ** -0.5, 0.21875, ((1, 4),))
    up_bias = centred(key_of[11], (FF,), 0.2, 1.0, ((0, 4),))
    down_weight = centred(key_of[12], (FF, D), (FF // 2) ** -0.5, 0.15625, ((0, 4),))
    down_bias = centred(key_of[13], (D,), 0.2, 1.0)
    out_grad = centred(key_of[14], (LEN, ROWS, D), 1.0, 6.0, ((0, 4), (1, 8)))
    return {"hidden_in": hidden_in, "doc_ids": doc_ids, "first_gain": first_gain, "first_shift": first_shift, "qkv_weight": qkv_weight, "qv_bias": qv_bias, "proj_weight": proj_weight, "proj_bias": proj_bias, "second_gain": second_gain, "second_shift": second_shift, "up_weight": up_weight, "up_bias": up_bias, "down_weight": down_weight, "down_bias": down_bias, "out_grad": out_grad}


@jax.custom_vjp
def low(v):
    return lax.optimization_barrier(v.astype(jnp.bfloat16)).astype(jnp.float32)

@jax.custom_vjp
def low_back(v):
    return v

def low_keep(v):
    return (low(v), None)

def low_pass(kept, grad):
    return (grad,)

def back_keep(v):
    return (v, None)

def back_low(kept, grad):
    return (low(grad),)
low.defvjp(low_keep, low_pass)
low_back.defvjp(back_keep, back_low)
NORM_EPS = 1e-05
MASKED = -1e+30
HIGHEST = lax.Precision.HIGHEST

def layer_norm(inputs, norm_gain, norm_shift):
    average = lax.optimization_barrier(jnp.mean(inputs, axis=-1, keepdims=True))
    centered = inputs - average
    variance = lax.optimization_barrier(jnp.mean(centered * centered, axis=-1, keepdims=True))
    return centered * lax.rsqrt(variance + NORM_EPS) * norm_gain + norm_shift

def allowed(query_ids, key_ids, first_row):
    query_pos = first_row + jnp.arange(query_ids.shape[0], dtype=jnp.int32)[:, None]
    key_pos = jnp.arange(key_ids.shape[0], dtype=jnp.int32)[None, :]
    same_doc = (query_ids[:, None] == key_ids[None, :]) & (query_ids[:, None] >= 0) & (key_pos < query_pos)
    return same_doc | (key_pos == query_pos)

def attend_row(query_rows, key_rows, value_rows, row_ids):
    length = query_rows.shape[0]
    blocks = length // QBLOCK
    scale = HEAD_DIM ** (-0.5)
    firsts = jnp.arange(blocks, dtype=jnp.int32) * QBLOCK

    def one_block(operands):
        query_block, id_block, first_row = operands
        scores = jnp.einsum('qhd,khd->hqk', query_block, key_rows, precision=HIGHEST) * scale
        scores = low_back(jnp.where(allowed(id_block, row_ids, first_row)[None], scores, MASKED))
        probability = low(jax.nn.softmax(scores, axis=-1))
        return jnp.einsum('hqk,khd->qhd', probability, value_rows, precision=HIGHEST)
    attended = lax.map(jax.checkpoint(one_block), (query_rows.reshape(blocks, QBLOCK, HEADS, HEAD_DIM), row_ids.reshape(blocks, QBLOCK), firsts))
    return attended.reshape(length, HEADS * HEAD_DIM)

def block_forward(stream, group_ids, params):
    first_gain, first_shift, qkv_weight, qv_bias, proj_weight, proj_bias, second_gain, second_shift, up_weight, up_bias, down_weight, down_bias = params
    length, row_count = (stream.shape[0], stream.shape[1])
    normed = low(layer_norm(stream, first_gain, first_shift))
    packed = jnp.einsum('lrd,dce->lrce', normed, qkv_weight, precision=HIGHEST)
    query_all = low(low_back(packed[:, :, 0] + qv_bias[0]))
    key_all = low(low_back(packed[:, :, 1]))
    value_all = low(low_back(packed[:, :, 2] + qv_bias[1]))

    def by_row(tensor_in):
        return jnp.moveaxis(tensor_in, 1, 0).reshape(row_count, length, HEADS, HEAD_DIM)
    attended = jax.vmap(attend_row)(by_row(query_all), by_row(key_all), by_row(value_all), jnp.transpose(group_ids))
    attended = low(low_back(jnp.moveaxis(attended, 0, 1)))
    attn_branch = low_back(jnp.einsum('lrd,de->lre', attended, proj_weight, precision=HIGHEST) + proj_bias)
    residual = stream + attn_branch
    normed_mid = low(layer_norm(residual, second_gain, second_shift))
    hidden = low_back(jnp.einsum('lrd,df->lrf', normed_mid, up_weight, precision=HIGHEST) + up_bias)
    activated = low(jax.nn.gelu(hidden, approximate=True))
    mlp_branch = low_back(jnp.einsum('lrf,fd->lrd', activated, down_weight, precision=HIGHEST) + down_bias)
    return residual + mlp_branch

def reference(hidden_in, doc_ids, first_gain, first_shift, qkv_weight, qv_bias, proj_weight, proj_bias, second_gain, second_shift, up_weight, up_bias, down_weight, down_bias, out_grad):
    params = tuple((param.astype(jnp.float32) for param in (first_gain, first_shift, qkv_weight, qv_bias, proj_weight, proj_bias, second_gain, second_shift, up_weight, up_bias, down_weight, down_bias)))

    def grouped(array):
        shaped = array.reshape((LEN, N_DP, ROWS_DEV) + array.shape[2:])
        return jnp.moveaxis(shaped, 1, 0)

    def ungrouped(array):
        shaped = jnp.moveaxis(array, 0, 1)
        return shaped.reshape((LEN, ROWS) + array.shape[3:])

    def one_group(totals, operands):
        stream, group_ids, group_grad = operands
        valid_mask = (group_ids >= 0).astype(jnp.float32)
        output, pullback = jax.vjp(lambda inputs, weights: block_forward(inputs, group_ids, weights), stream, params)
        stream_grad, param_grads = pullback(group_grad * valid_mask[:, :, None])
        totals = tuple((total + extra for total, extra in zip(totals, param_grads)))
        return (totals, (output.astype(jnp.bfloat16), stream_grad.astype(jnp.bfloat16)))
    zeros = tuple((jnp.zeros_like(param) for param in params))
    totals, (outputs, stream_grads) = lax.scan(one_group, zeros, (grouped(hidden_in.astype(jnp.float32)), grouped(doc_ids), grouped(out_grad.astype(jnp.float32))))
    return (ungrouped(outputs), ungrouped(stream_grads), totals[0], totals[1], totals[2], totals[3], totals[4], totals[5], totals[6], totals[7], totals[8], totals[9], totals[10], totals[11])
```

```python
import functools

import jax
import jax.numpy as jnp
from jax import lax
from jax.experimental import pallas as pl
from jax.experimental.pallas import tpu as pltpu
from jax.sharding import PartitionSpec as P

HEAD_DIM = 64
NORM_EPS = 1e-05
MASKED = -1e30
BF = jnp.bfloat16
F32 = jnp.float32
VMEM_LIMIT = 56 * 1024 * 1024

SLOT = ((0, 2, 4, 5), (1, 3, 6, 7))
SLOT_ROW = (0, 1, 0, 1, 0, 0)
SLOT_K = (0, 0, 1, 1, 2, 3)
X_SWAP = ((0, 2), (1, 3), (2, 0), (3, 1))
CORE_SWAP = ((0, 1), (1, 0), (2, 3), (3, 2))


def x_swap(value):
    return lax.ppermute(value, "tensor", X_SWAP)


def core_swap(value):
    return lax.ppermute(value, "tensor", CORE_SWAP)


def params(semantics=None):
    return pltpu.CompilerParams(vmem_limit_bytes=VMEM_LIMIT)


def fixed(shape):
    return pl.BlockSpec(shape, lambda *ids: (0,) * len(shape), pipeline_mode=pl.Buffered(1))


def nt(left, right):
    return lax.dot_general(left, right, (((1,), (1,)), ((), ())), preferred_element_type=F32)


def nn(left, right):
    return lax.dot_general(left, right, (((1,), (0,)), ((), ())), preferred_element_type=F32)


def tn(left, right):
    return lax.dot_general(left, right, (((0,), (0,)), ((), ())), preferred_element_type=F32)


def swapped_slot(slot):
    return jnp.where(slot < 4, slot ^ 2, slot ^ 1)


def key_mask(start_row, key_first, size, diagonal):
    keys = lax.broadcasted_iota(jnp.int32, (size, size), 0)
    mask = keys >= start_row - key_first
    if diagonal:
        mask = mask & (keys <= lax.broadcasted_iota(jnp.int32, (size, size), 1))
    return mask


def attend_forward_kernel(size, table, start_ref, q_ref, k_ref, v_ref, out_ref, lse_ref):
    slot = pl.program_id(1)
    row, block, low = table[0, slot], table[1, slot], table[2, slot]
    start_row = start_ref[0:1, :]
    lane = lax.broadcasted_iota(jnp.int32, (size, 2 * HEAD_DIM), 1)
    query = q_ref[...] * jnp.asarray(HEAD_DIM**-0.5, BF)
    zero = jnp.zeros_like(query)
    heads = (jnp.where(lane < HEAD_DIM, query, zero), jnp.where(lane < HEAD_DIM, zero, query))

    def load(key_block):
        at = pl.multiple_of(table[3 + row, key_block] * size, size)
        return k_ref[pl.ds(at, size), :], jnp.transpose(v_ref[pl.ds(at, size), :])

    key, value_t = load(block)
    mask = key_mask(start_row, block * size, size, True)
    carry = []
    for head in range(2):
        scores = jnp.where(mask, nt(key, heads[head]), MASKED)
        top = jnp.max(scores, axis=0, keepdims=True)
        weight = jnp.exp(scores - top)
        total = jnp.sum(weight, axis=0, keepdims=True)
        acc = nn(value_t[head * HEAD_DIM : (head + 1) * HEAD_DIM], weight.astype(BF))
        carry += [top, total, acc]

    def earlier(step, carry):
        key_block = block - 1 - step
        key, value_t = load(key_block)
        mask = key_mask(start_row, key_block * size, size, False)
        new = []
        for head in range(2):
            top, total, acc = carry[3 * head : 3 * head + 3]
            scores = jnp.where(mask, nt(key, heads[head]), MASKED)
            higher = jnp.maximum(top, jnp.max(scores, axis=0, keepdims=True))
            shrink = jnp.exp(top - higher)
            weight = jnp.exp(scores - higher)
            total = total * shrink + jnp.sum(weight, axis=0, keepdims=True)
            acc = acc * shrink + nn(
                value_t[head * HEAD_DIM : (head + 1) * HEAD_DIM], weight.astype(BF)
            )
            new += [higher, total, acc]
        return tuple(new)

    carry = lax.fori_loop(0, block - low, earlier, tuple(carry))
    both = jnp.concatenate([carry[2] / carry[1], carry[5] / carry[4]], axis=0)
    out_ref[...] = jnp.transpose(both).astype(BF)
    lse_ref[0, 0:1, :] = carry[0] + jnp.log(carry[1])
    lse_ref[0, 1:2, :] = carry[3] + jnp.log(carry[4])


def attend_forward(qkv, table, starts, size):
    pairs = qkv.shape[1] // (6 * HEAD_DIM)
    tokens = qkv.shape[0]
    width = 2 * HEAD_DIM
    return pl.pallas_call(
        functools.partial(attend_forward_kernel, size),
        grid_spec=pltpu.PrefetchScalarGridSpec(
            num_scalar_prefetch=1,
            grid=(pairs, 6),
            in_specs=[
                pl.BlockSpec((8, size), lambda p, s, *_: (0, s)),
                pl.BlockSpec((size, width), lambda p, s, *_: (s, p)),
                pl.BlockSpec((tokens, width), lambda p, s, *_: (0, pairs + p)),
                pl.BlockSpec((tokens, width), lambda p, s, *_: (0, 2 * pairs + p)),
            ],
            out_specs=[
                pl.BlockSpec((size, width), lambda p, s, *_: (s, p)),
                pl.BlockSpec((1, 8, size), lambda p, s, *_: (p, 0, s)),
            ],
        ),
        out_shape=[
            jax.ShapeDtypeStruct((6 * size, pairs * width), BF),
            jax.ShapeDtypeStruct((pairs, 8, 6 * size), F32),
        ],
        compiler_params=params(),
        cost_estimate=pl.CostEstimate(
            flops=36 * size * size * pairs * 256, bytes_accessed=tokens * width * pairs * 8, transcendentals=0
        ),
        name="attend_forward",
    )(table, starts, qkv, qkv, qkv)


def attend_backward_kernel(
    size, table, start_ref, q_ref, k_ref, v_ref, out_ref, grad_ref, lse_ref,
    dq_ref, dk_ref, dv_ref, dk_acc, dv_acc,
):
    slot = pl.program_id(1)
    row, block, low = table[0, slot], table[1, slot], table[2, slot]
    start_row = start_ref[0:1, :]
    lane = lax.broadcasted_iota(jnp.int32, (size, 2 * HEAD_DIM), 1)
    scale = jnp.asarray(HEAD_DIM**-0.5, BF)
    query = q_ref[...] * scale
    grad = grad_ref[...]
    zero = jnp.zeros_like(query)
    q_heads = (jnp.where(lane < HEAD_DIM, query, zero), jnp.where(lane < HEAD_DIM, zero, query))
    g_heads = (jnp.where(lane < HEAD_DIM, grad, zero), jnp.where(lane < HEAD_DIM, zero, grad))
    products = jnp.transpose(grad.astype(F32) * out_ref[...].astype(F32))
    deltas = (
        jnp.sum(products[:HEAD_DIM], axis=0, keepdims=True),
        jnp.sum(products[HEAD_DIM:], axis=0, keepdims=True),
    )

    @pl.when(slot == 0)
    def _():
        dk_acc[...] = jnp.zeros_like(dk_acc)
        dv_acc[...] = jnp.zeros_like(dv_acc)

    def one_block(key_block, diagonal):
        at = pl.multiple_of(table[3 + row, key_block] * size, size)
        key, value = k_ref[pl.ds(at, size), :], v_ref[pl.ds(at, size), :]
        key_t = jnp.transpose(key)
        mask = key_mask(start_row, key_block * size, size, diagonal)
        dq_parts = []
        dk_sum = None
        dv_sum = None
        for head in range(2):
            scores = nt(key, q_heads[head])
            prob = jnp.where(mask, jnp.exp(jnp.where(mask, scores, MASKED) - lse_ref[0, head : head + 1, :]), 0.0)
            prob_grad = nt(value, g_heads[head])
            score_grad = (prob * (prob_grad - deltas[head])).astype(BF)
            dk_part = nn(score_grad, q_heads[head])
            dv_part = nn(prob.astype(BF), g_heads[head])
            dk_sum = dk_part if dk_sum is None else dk_sum + dk_part
            dv_sum = dv_part if dv_sum is None else dv_sum + dv_part
            dq_parts.append(nn(key_t[head * HEAD_DIM : (head + 1) * HEAD_DIM], score_grad))
        dk_acc[pl.ds(at, size), :] += dk_sum
        dv_acc[pl.ds(at, size), :] += dv_sum
        return jnp.concatenate(dq_parts, axis=0)

    dq_t = one_block(block, True)
    dq_t = lax.fori_loop(
        0, block - low, lambda step, acc: acc + one_block(block - 1 - step, False), dq_t
    )
    dq_ref[...] = (jnp.transpose(dq_t) * HEAD_DIM**-0.5).astype(BF)

    @pl.when(slot == pl.num_programs(1) - 1)
    def _():
        dk_ref[...] = dk_acc[...].astype(BF)
        dv_ref[...] = dv_acc[...].astype(BF)


def attend_backward(qkv, attended, grad, lse, table, starts, size):
    pairs = qkv.shape[1] // (6 * HEAD_DIM)
    tokens = qkv.shape[0]
    width = 2 * HEAD_DIM
    block = pl.BlockSpec((size, width), lambda p, s, *_: (s, p))
    return pl.pallas_call(
        functools.partial(attend_backward_kernel, size),
        grid_spec=pltpu.PrefetchScalarGridSpec(
            num_scalar_prefetch=1,
            grid=(pairs, 6),
            in_specs=[
                pl.BlockSpec((8, size), lambda p, s, *_: (0, s)),
                block,
                pl.BlockSpec((tokens, width), lambda p, s, *_: (0, pairs + p)),
                pl.BlockSpec((tokens, width), lambda p, s, *_: (0, 2 * pairs + p)),
                block,
                block,
                pl.BlockSpec((1, 8, size), lambda p, s, *_: (p, 0, s)),
            ],
            out_specs=[
                block,
                pl.BlockSpec((tokens, width), lambda p, s, *_: (0, p)),
                pl.BlockSpec((tokens, width), lambda p, s, *_: (0, p)),
            ],
            scratch_shapes=[pltpu.VMEM((tokens, width), F32), pltpu.VMEM((tokens, width), F32)],
        ),
        out_shape=[
            jax.ShapeDtypeStruct((6 * size, pairs * width), BF),
            jax.ShapeDtypeStruct((tokens, pairs * width), BF),
            jax.ShapeDtypeStruct((tokens, pairs * width), BF),
        ],
        compiler_params=params(),
        cost_estimate=pl.CostEstimate(
            flops=90 * size * size * pairs * 256, bytes_accessed=tokens * width * pairs * 16, transcendentals=0
        ),
        name="attend_backward",
    )(table, starts, qkv, qkv, qkv, attended, grad, lse)


GELU_C = 0.7978845608028654
GELU_A = 0.044715


def mlp_kernel(
    x_ref, own_ref, other_ref, bg_ref, vec_ref, upb_ref, up0_ref, up1_ref, dn0_ref, dn1_ref,
    res_ref, mid_ref, act_ref, hg_ref, out_ref, midin_ref, upbg_ref,
):
    proj_bias, gain, shift = vec_ref[0:1, :], vec_ref[1:2, :], vec_ref[2:3, :]
    residual = (
        x_ref[...].astype(F32) + own_ref[...].astype(F32) + other_ref[...].astype(F32) + proj_bias
    )
    res_ref[...] = residual
    centered = residual - jnp.mean(residual, axis=-1, keepdims=True)
    variance = jnp.mean(centered * centered, axis=-1, keepdims=True)
    mid = (centered * lax.rsqrt(variance + NORM_EPS) * gain + shift).astype(BF)
    mid_ref[...] = mid
    bg = bg_ref[...]

    @pl.when(pl.program_id(0) == 0)
    def _():
        upbg_ref[...] = jnp.zeros_like(upbg_ref)

    out = None
    midin = None
    for part, (up_ref, dn_ref) in enumerate(((up0_ref, dn0_ref), (up1_ref, dn1_ref))):
        hidden = nn(mid, up_ref[...]) + upb_ref[part : part + 1, :]
        act_grad = nt(bg, dn_ref[...])
        square = hidden * hidden
        bent = jnp.tanh(GELU_C * (hidden + GELU_A * hidden * square))
        half = 0.5 * (1.0 + bent)
        act = (hidden * half).astype(BF)
        slope = half + 0.5 * hidden * (1.0 - bent * bent) * (GELU_C + 3.0 * GELU_C * GELU_A * square)
        grad = (act_grad * slope).astype(BF)
        act_ref[part] = act
        hg_ref[part] = grad
        upbg_ref[part : part + 1, :] += jnp.sum(grad.astype(F32), axis=0, keepdims=True)
        out_part = nn(act, dn_ref[...])
        midin_part = nt(grad, up_ref[...])
        out = out_part if out is None else out + out_part
        midin = midin_part if midin is None else midin + midin_part
    out_ref[...] = out.astype(BF)
    midin_ref[...] = midin.astype(BF)


def mlp(tokens, own, other, bg, vectors, up_bias, up0, up1, dn0, dn1, size):
    rows, width = own.shape
    inner = up0.shape[1]
    block = pl.BlockSpec((size, width), lambda i: (i, 0))
    wide = pl.BlockSpec((2, size, inner), lambda i: (0, i, 0))
    return pl.pallas_call(
        mlp_kernel,
        grid=(rows // size,),
        in_specs=[
            block,
            block,
            pl.BlockSpec((size, width), lambda i: (swapped_slot(i), 0)),
            block,
            fixed((8, width)),
            fixed((8, inner)),
            fixed((width, inner)),
            fixed((width, inner)),
            fixed((inner, width)),
            fixed((inner, width)),
        ],
        out_specs=[block, block, wide, wide, block, block, pl.BlockSpec((8, inner), lambda i: (0, 0))],
        out_shape=[
            jax.ShapeDtypeStruct((rows, width), F32),
            jax.ShapeDtypeStruct((rows, width), BF),
            jax.ShapeDtypeStruct((2, rows, inner), BF),
            jax.ShapeDtypeStruct((2, rows, inner), BF),
            jax.ShapeDtypeStruct((rows, width), BF),
            jax.ShapeDtypeStruct((rows, width), BF),
            jax.ShapeDtypeStruct((8, inner), F32),
        ],
        compiler_params=params(),
        cost_estimate=pl.CostEstimate(
            flops=16 * rows * width * inner, bytes_accessed=rows * width * 24, transcendentals=0
        ),
        name="mlp",
    )(tokens, own, other, bg, vectors, up_bias, up0, up1, dn0, dn1)


def mid_backward_kernel(
    res_ref, own_ref, other_ref, bg_ref, vec_ref, proj_ref, rg_ref, ag_ref, atg_ref, sum_ref
):
    gain = vec_ref[1:2, :]
    residual = res_ref[...]
    centered = residual - jnp.mean(residual, axis=-1, keepdims=True)
    rstd = lax.rsqrt(jnp.mean(centered * centered, axis=-1, keepdims=True) + NORM_EPS)
    xhat = centered * rstd
    mid_in = own_ref[...].astype(F32) + other_ref[...].astype(F32)
    gy = mid_in * gain
    through = rstd * (
        gy
        - jnp.mean(gy, axis=-1, keepdims=True)
        - xhat * jnp.mean(gy * xhat, axis=-1, keepdims=True)
    )
    total = bg_ref[...].astype(F32) + through
    rg_ref[...] = total
    low = total.astype(BF)
    ag_ref[...] = low
    atg_ref[...] = nt(low, proj_ref[...]).astype(BF)

    @pl.when(pl.program_id(0) == 0)
    def _():
        sum_ref[...] = jnp.zeros_like(sum_ref)

    sum_ref[0:1, :] += jnp.sum(mid_in * xhat, axis=0, keepdims=True)
    sum_ref[1:2, :] += jnp.sum(mid_in, axis=0, keepdims=True)
    sum_ref[2:3, :] += jnp.sum(low.astype(F32), axis=0, keepdims=True)
    sum_ref[3:4, :] += jnp.sum(bg_ref[...].astype(F32), axis=0, keepdims=True)


def mid_backward(residual, own, other, bg, vectors, proj, size):
    rows, width = own.shape
    inner = proj.shape[0]
    block = pl.BlockSpec((size, width), lambda i: (i, 0))
    return pl.pallas_call(
        mid_backward_kernel,
        grid=(rows // size,),
        in_specs=[
            block,
            block,
            pl.BlockSpec((size, width), lambda i: (swapped_slot(i), 0)),
            block,
            fixed((8, width)),
            fixed((inner, width)),
        ],
        out_specs=[
            block,
            block,
            pl.BlockSpec((size, inner), lambda i: (i, 0)),
            pl.BlockSpec((8, width), lambda i: (0, 0)),
        ],
        out_shape=[
            jax.ShapeDtypeStruct((rows, width), F32),
            jax.ShapeDtypeStruct((rows, width), BF),
            jax.ShapeDtypeStruct((rows, inner), BF),
            jax.ShapeDtypeStruct((8, width), F32),
        ],
        compiler_params=params(),
        cost_estimate=pl.CostEstimate(
            flops=2 * rows * width * inner, bytes_accessed=rows * width * 16, transcendentals=0
        ),
        name="mid_backward",
    )(residual, own, other, bg, vectors, proj)


def dp_partners(count, bit):
    return [(d, d ^ bit) for d in range(count)]


def halve(value, index, bit, count):
    rows = value.shape[0] // 2
    side = jnp.where((index & bit) != 0, 1, 0)
    keep = lax.dynamic_slice_in_dim(value, side * rows, rows, 0)
    give = lax.dynamic_slice_in_dim(value, (1 - side) * rows, rows, 0).astype(BF)
    return keep.astype(F32) + lax.ppermute(give, "dp", dp_partners(count, bit)).astype(F32)


def double(value, index, bit, count):
    got = lax.ppermute(value, "dp", dp_partners(count, bit))
    rows = value.shape[0]
    side = jnp.where((index & bit) != 0, 1, 0)
    both = jnp.zeros((2 * rows,) + value.shape[1:], value.dtype)
    both = lax.dynamic_update_slice_in_dim(both, value, side * rows, 0)
    return lax.dynamic_update_slice_in_dim(both, got, (1 - side) * rows, 0)


def sum_over_dp(value):
    count = lax.axis_size("dp")
    index = lax.axis_index("dp")
    bits = [1 << i for i in range(count.bit_length() - 1)]
    for bit in bits:
        value = halve(value, index, bit, count)
    value = value.astype(BF)
    for bit in reversed(bits):
        value = double(value, index, bit, count)
    return value


def sum_everywhere(value):
    count = lax.axis_size("dp")
    value = value + core_swap(value)
    value = value + x_swap(value)
    bit = 1
    while bit < count:
        value = value + lax.ppermute(value, "dp", dp_partners(count, bit))
        bit *= 2
    return value


def body(
    hidden_in,
    doc_ids,
    first_gain,
    first_shift,
    qkv_weight,
    qv_bias,
    proj_weight,
    proj_bias,
    second_gain,
    second_shift,
    up_weight,
    up_bias,
    down_weight,
    down_bias,
    out_grad,
):
    size, rows_dev, width = hidden_in.shape
    length = doc_ids.shape[0]
    place = lax.axis_index("tensor")
    right = place >= 2
    feats = qkv_weight.shape[2]
    inner = up_weight.shape[1]

    def split_rows(value):
        first, mid, last = value[:, 0], value[:, 1], value[:, 2]
        return jnp.where(right, last, first), mid, jnp.where(right, first, last)

    def join_rows(main, mid, other):
        return jnp.stack(
            [jnp.where(right, other, main), mid, jnp.where(right, main, other)], axis=1
        )

    main, mid, away = split_rows(hidden_in)
    home = jnp.concatenate([main, mid], axis=0)
    far = x_swap(jnp.concatenate([away, mid], axis=0))
    near = core_swap(home)
    far_near = core_swap(far)
    tokens = jnp.concatenate(
        [home, near, far[:size], far_near[:size], far[size:], far_near[size:]], axis=0
    )

    qkv_flat = jnp.concatenate([qkv_weight[:, i] for i in range(3)], axis=1)
    qkv_far = x_swap(qkv_flat)
    biases = jnp.concatenate([qv_bias.reshape(-1), up_bias])
    biases_far = x_swap(biases)
    proj_far = x_swap(proj_weight)
    up_far = x_swap(up_weight)
    down_far = x_swap(down_weight)

    local_ids = lax.dynamic_slice_in_dim(doc_ids, place * size, size, 0)
    cot = jnp.where((local_ids >= 0)[:, :, None], out_grad, jnp.zeros_like(out_grad))
    g_main, g_mid, g_away = split_rows(cot)
    g_home = jnp.concatenate([g_main, g_mid], axis=0)
    g_near = core_swap(g_home)
    g_far = x_swap(g_away)
    g_far_near = core_swap(g_far)
    branch_grad = jnp.concatenate([g_home, g_near, g_far, g_far_near], axis=0)

    ids = jnp.stack([jnp.where(right, doc_ids[:, 2], doc_ids[:, 0]), doc_ids[:, 1]])
    position = lax.broadcasted_iota(jnp.int32, ids.shape, 1)
    count_below = jnp.stack(
        [jnp.sum(((ids >= 0) & (ids < d)).astype(jnp.int32), axis=1) for d in range(8)], axis=1
    )
    which = ids[:, :, None] == jnp.arange(8, dtype=jnp.int32)[None, None, :]
    starts = jnp.sum(jnp.where(which, count_below[:, None, :], 0), axis=2)
    starts = jnp.where(ids >= 0, starts, position).reshape(2, length // size, size)
    slot_row = jnp.array(SLOT_ROW, jnp.int32)
    slot_block = jnp.array(SLOT_K, jnp.int32) ^ place
    slot_start = starts.reshape(-1, size)[slot_row * (length // size) + slot_block]
    low_block = slot_start[:, 0] // size
    where_key = jnp.array(SLOT, jnp.int32)[:, jnp.arange(4, dtype=jnp.int32) ^ place]
    table = jnp.zeros((8, 8), jnp.int32)
    table = table.at[0, :6].set(slot_row).at[1, :6].set(slot_block).at[2, :6].set(low_block)
    table = table.at[3:5, :4].set(where_key)
    start_rows = jnp.broadcast_to(slot_start.reshape(1, -1), (8, 6 * size))

    stream = tokens.astype(F32)
    centered = stream - jnp.mean(stream, axis=-1, keepdims=True)
    first_rstd = lax.rsqrt(jnp.mean(centered * centered, axis=-1, keepdims=True) + NORM_EPS)
    normed = (
        centered * first_rstd * first_gain.astype(F32) + first_shift.astype(F32)
    ).astype(BF)
    qkv_both = jnp.concatenate(
        [
            part[:, i * feats : (i + 1) * feats]
            for i in range(3)
            for part in (qkv_flat, qkv_far)
        ],
        axis=1,
    )
    no_bias = jnp.zeros((2 * feats,), F32)
    qkv_bias = jnp.concatenate(
        [
            qv_bias[0].astype(F32),
            biases_far[:feats].astype(F32),
            no_bias,
            qv_bias[1].astype(F32),
            biases_far[feats : 2 * feats].astype(F32),
        ]
    )
    qkv = (nn(normed, qkv_both) + qkv_bias).astype(BF)

    attended, lse = attend_forward(qkv, table, start_rows, size)
    proj_both = jnp.concatenate([proj_weight, proj_far], axis=0)
    attn_part = nn(attended, proj_both).astype(BF)
    attn_other = core_swap(attn_part)

    vectors = jnp.zeros((8, width), F32)
    vectors = vectors.at[0].set(proj_bias.astype(F32)).at[1].set(second_gain.astype(F32))
    vectors = vectors.at[2].set(second_shift.astype(F32))
    up_biases = jnp.zeros((8, inner), F32)
    up_biases = up_biases.at[0].set(up_bias.astype(F32))
    up_biases = up_biases.at[1].set(biases_far[2 * feats :].astype(F32))
    residual, normed_mid, act, hidden_grad, out_part, mid_part, up_sums = mlp(
        tokens, attn_part, attn_other, branch_grad, vectors, up_biases,
        up_weight, up_far, down_weight, down_far, size,
    )

    def mine(value):
        return jnp.concatenate([value[: 2 * size], value[4 * size : 5 * size]], axis=0)

    def theirs(value):
        return jnp.concatenate([value[2 * size : 4 * size], value[5 * size : 6 * size]], axis=0)

    mid_other = core_swap(mid_part)
    residual_grad, attn_grad, attended_grad, mid_sums = mid_backward(
        residual, mid_part, mid_other, branch_grad, vectors, proj_both, size
    )

    down_away = tn(act[1], branch_grad).astype(BF)
    up_away = tn(normed_mid, hidden_grad[1]).astype(BF)
    down_own = tn(act[0], branch_grad)
    up_own = tn(normed_mid, hidden_grad[0])
    down_sum = sum_over_dp(down_own + x_swap(down_away).astype(F32))
    up_sum = sum_over_dp(up_own + x_swap(up_away).astype(F32))

    out_own = (
        mine(residual)
        + mine(out_part).astype(F32)
        + core_swap(theirs(out_part)).astype(F32)
        + down_bias.astype(F32)
    ).astype(BF)
    block_out = join_rows(out_own[:size], out_own[size : 2 * size], x_swap(out_own[2 * size :]))

    dq, dk, dv = attend_backward(qkv, attended, attended_grad, lse, table, start_rows, size)

    proj_pair = tn(attended, attn_grad)
    proj_sum = sum_over_dp(proj_pair[:feats] + x_swap(proj_pair[feats:].astype(BF)).astype(F32))

    qkv_grad = jnp.concatenate(
        [jnp.concatenate([dq, jnp.zeros((2 * size, 2 * feats), BF)], axis=0), dk, dv], axis=1
    )
    qkv_pair = tn(normed, qkv_grad)
    qkv_own = jnp.concatenate(
        [qkv_pair[:, 2 * i * feats : (2 * i + 1) * feats] for i in range(3)], axis=1
    )
    qkv_away = jnp.concatenate(
        [qkv_pair[:, (2 * i + 1) * feats : (2 * i + 2) * feats] for i in range(3)], axis=1
    )
    qkv_sum = sum_over_dp(qkv_own + x_swap(qkv_away.astype(BF)).astype(F32))

    first_part = nt(qkv_grad, qkv_both)
    own_in = jnp.concatenate([mine(first_part), first_part[6 * size : 7 * size]], axis=0)
    give_in = jnp.concatenate([theirs(first_part), first_part[7 * size :]], axis=0)
    own_in = own_in + core_swap(give_in.astype(BF)).astype(F32)
    mid_extra = x_swap(own_in[3 * size :].astype(BF)).astype(F32)
    first_in = jnp.concatenate(
        [own_in[:size], own_in[size : 2 * size] + mid_extra, own_in[2 * size : 3 * size]], axis=0
    )
    xhat = mine(centered) * mine(first_rstd)
    gy = first_in * first_gain.astype(F32)
    through = mine(first_rstd) * (
        gy - jnp.mean(gy, axis=-1, keepdims=True) - xhat * jnp.mean(gy * xhat, axis=-1, keepdims=True)
    )
    in_own = (mine(residual_grad) + through).astype(BF)
    in_grad = join_rows(in_own[:size], in_own[size : 2 * size], x_swap(in_own[2 * size :]))

    core = place & 1
    up_slots = jnp.zeros((4, inner), F32)
    up_slots = lax.dynamic_update_slice_in_dim(up_slots, up_sums[0:1], place, 0)
    up_slots = lax.dynamic_update_slice_in_dim(up_slots, up_sums[1:2], place ^ 2, 0)
    q_sum = jnp.sum(dq.astype(F32), axis=0)
    v_sum = jnp.sum(dv.astype(F32), axis=0)
    qv_slots = jnp.zeros((4, 2 * feats), F32)
    qv_slots = lax.dynamic_update_slice_in_dim(
        qv_slots, jnp.concatenate([q_sum[:feats], v_sum[:feats]])[None], place, 0
    )
    qv_slots = lax.dynamic_update_slice_in_dim(
        qv_slots, jnp.concatenate([q_sum[feats:], v_sum[feats:]])[None], place ^ 2, 0
    )
    small = jnp.concatenate(
        [
            jnp.sum(first_in * xhat, axis=0)[None],
            jnp.sum(first_in, axis=0)[None],
            0.5 * mid_sums[:4],
            up_slots,
            qv_slots.reshape(-1, width),
        ],
        axis=0,
    )
    small = sum_everywhere(small)
    up_bias_grad = lax.dynamic_slice_in_dim(small, 6 + place, 1, 0)[0]
    qv_all = small[10:].reshape(4, 2, feats)
    qv_bias_grad = lax.dynamic_slice_in_dim(qv_all, place, 1, 0)[0]

    qkv_weight_grad = jnp.stack(
        [qkv_sum[:, i * feats : (i + 1) * feats] for i in range(3)], axis=1
    ).astype(F32)
    return (
        block_out,
        in_grad,
        small[0],
        small[1],
        qkv_weight_grad,
        qv_bias_grad,
        proj_sum.astype(F32),
        small[4],
        small[2],
        small[3],
        up_sum.astype(F32),
        up_bias_grad,
        down_sum.astype(F32),
        small[5],
    )


def solution(mesh):
    in_specs = (
        P("tensor", "dp", None),
        P(None, "dp"),
        P(),
        P(),
        P(None, None, "tensor"),
        P(None, "tensor"),
        P("tensor", None),
        P(),
        P(),
        P(),
        P(None, "tensor"),
        P("tensor"),
        P("tensor", None),
        P(),
        P("tensor", "dp", None),
    )
    out_specs = (
        P("tensor", "dp", None),
        P("tensor", "dp", None),
        P(),
        P(),
        P(None, None, "tensor"),
        P(None, "tensor"),
        P("tensor", None),
        P(),
        P(),
        P(),
        P(None, "tensor"),
        P("tensor"),
        P("tensor", None),
        P(),
    )
    return jax.shard_map(body, mesh=mesh, in_specs=in_specs, out_specs=out_specs, check_vma=False)
```

```python
import functools

import jax
import jax.numpy as jnp
from jax import lax
from jax.experimental import pallas as pl
from jax.experimental.pallas import tpu as pltpu
from jax.sharding import PartitionSpec as P

HEAD_DIM = 64
NORM_EPS = 1e-05
MASKED = -1e30
BF = jnp.bfloat16
F32 = jnp.float32
VMEM_LIMIT = 56 * 1024 * 1024

SLOT = ((0, 2, 4, 5), (1, 3, 6, 7))
SLOT_ROW = (0, 1, 0, 1, 0, 0)
SLOT_K = (0, 0, 1, 1, 2, 3)
X_SWAP = ((0, 2), (1, 3), (2, 0), (3, 1))
CORE_SWAP = ((0, 1), (1, 0), (2, 3), (3, 2))


def x_swap(value):
    return lax.ppermute(value, "tensor", X_SWAP)


def core_swap(value):
    return lax.ppermute(value, "tensor", CORE_SWAP)


def params(semantics=None):
    return pltpu.CompilerParams(vmem_limit_bytes=VMEM_LIMIT)


def fixed(shape):
    return pl.BlockSpec(shape, lambda *ids: (0,) * len(shape), pipeline_mode=pl.Buffered(1))


def nt(left, right):
    return lax.dot_general(left, right, (((1,), (1,)), ((), ())), preferred_element_type=F32)


def nn(left, right):
    return lax.dot_general(left, right, (((1,), (0,)), ((), ())), preferred_element_type=F32)


def tn(left, right):
    return lax.dot_general(left, right, (((0,), (0,)), ((), ())), preferred_element_type=F32)


SMALL_COST = pl.CostEstimate(flops=1, bytes_accessed=1, transcendentals=0)


def swapped_slot(slot):
    return jnp.where(slot < 4, slot ^ 2, slot ^ 1)


def own_first(step):
    return jnp.where(step == 2, 4, jnp.where((step == 3) | (step == 4), step - 1, step))


def key_mask(start_row, key_first, size, diagonal):
    keys = lax.broadcasted_iota(jnp.int32, (size, size), 0)
    mask = keys >= start_row - key_first
    if diagonal:
        mask = mask & (keys <= lax.broadcasted_iota(jnp.int32, (size, size), 1))
    return mask


def head_rows(size):
    lane = lax.broadcasted_iota(jnp.int32, (size, 2 * HEAD_DIM), 1)

    def select(value):
        zero = jnp.zeros((size, 2 * HEAD_DIM), value.dtype)
        pair = value[:, : 2 * HEAD_DIM]
        return (
            jnp.where(lane < HEAD_DIM, pair, zero),
            jnp.where(lane < HEAD_DIM, zero, pair),
            value[:, 2 * HEAD_DIM :],
        )

    return select


def pair_lanes(value, head):
    first = 2 * HEAD_DIM * (head // 2)
    return value[:, first : first + 2 * HEAD_DIM]


def attend_forward_kernel(size, table, start_ref, q_ref, k_ref, v_ref, out_ref, lse_ref):
    slot = pl.program_id(1)
    row, block, low = table[0, slot], table[1, slot], table[2, slot]
    start_row = start_ref[0:1, :]
    select = head_rows(size)
    heads = select(q_ref[...] * jnp.asarray(HEAD_DIM**-0.5, BF))

    def load(key_block):
        at = pl.multiple_of(table[3 + row, key_block] * size, size)
        return k_ref[pl.ds(at, size), :], jnp.transpose(v_ref[pl.ds(at, size), :])

    key, value_t = load(block)
    mask = key_mask(start_row, block * size, size, True)
    all_scores = [nt(pair_lanes(key, head), heads[head]) for head in range(3)]
    carry = []
    for head in range(3):
        scores = jnp.where(mask, all_scores[head], MASKED)
        top = jnp.max(scores, axis=0, keepdims=True)
        weight = jnp.exp(scores - top)
        total = jnp.sum(weight, axis=0, keepdims=True)
        acc = nn(value_t[head * HEAD_DIM : (head + 1) * HEAD_DIM], weight.astype(BF))
        carry += [top, total, acc]

    def earlier(step, carry):
        key_block = block - 1 - step
        key, value_t = load(key_block)
        mask = key_mask(start_row, key_block * size, size, False)
        all_scores = [nt(pair_lanes(key, head), heads[head]) for head in range(3)]
        new = []
        for head in range(3):
            top, total, acc = carry[3 * head : 3 * head + 3]
            scores = jnp.where(mask, all_scores[head], MASKED)
            higher = jnp.maximum(top, jnp.max(scores, axis=0, keepdims=True))
            shrink = jnp.exp(top - higher)
            weight = jnp.exp(scores - higher)
            total = total * shrink + jnp.sum(weight, axis=0, keepdims=True)
            acc = acc * shrink + nn(
                value_t[head * HEAD_DIM : (head + 1) * HEAD_DIM], weight.astype(BF)
            )
            new += [higher, total, acc]
        return tuple(new)

    carry = lax.fori_loop(0, block - low, earlier, tuple(carry))
    parts = [carry[3 * head + 2] / carry[3 * head + 1] for head in range(3)]
    parts.append(jnp.zeros_like(parts[0]))
    out_ref[...] = jnp.transpose(jnp.concatenate(parts, axis=0)).astype(BF)
    for head in range(3):
        lse_ref[0, head : head + 1, :] = carry[3 * head] + jnp.log(carry[3 * head + 1])


def attend_forward(qkv, table, starts, size):
    width = 4 * HEAD_DIM
    shards = qkv.shape[1] // (3 * width)
    tokens = qkv.shape[0]
    return pl.pallas_call(
        functools.partial(attend_forward_kernel, size),
        grid_spec=pltpu.PrefetchScalarGridSpec(
            num_scalar_prefetch=1,
            grid=(shards, 6),
            in_specs=[
                pl.BlockSpec((8, size), lambda p, s, *_: (0, s)),
                pl.BlockSpec((size, width), lambda p, s, *_: (s, 3 * p)),
                pl.BlockSpec((tokens, width), lambda p, s, *_: (0, 3 * p + 1)),
                pl.BlockSpec((tokens, width), lambda p, s, *_: (0, 3 * p + 2)),
            ],
            out_specs=[
                pl.BlockSpec((size, width), lambda p, s, *_: (s, p)),
                pl.BlockSpec((1, 8, size), lambda p, s, *_: (p, 0, s)),
            ],
        ),
        out_shape=[
            jax.ShapeDtypeStruct((6 * size, shards * width), BF),
            jax.ShapeDtypeStruct((shards, 8, 6 * size), F32),
        ],
        compiler_params=params(),
        cost_estimate=SMALL_COST,
        name="attend_forward",
    )(table, starts, qkv, qkv, qkv)


def attend_backward_kernel(
    size, table, start_ref, q_ref, k_ref, v_ref, out_ref, grad_ref, lse_ref,
    d_ref, sum_ref, dk_acc, dv_acc,
):
    slot = pl.program_id(0)
    width = 4 * HEAD_DIM
    row, block, low = table[0, slot], table[1, slot], table[2, slot]
    start_row = start_ref[0:1, :]
    select = head_rows(size)
    q_heads = select(q_ref[...] * jnp.asarray(HEAD_DIM**-0.5, BF))
    grad = grad_ref[...]
    g_heads = select(grad)
    products = jnp.transpose(grad.astype(F32) * out_ref[...].astype(F32))
    deltas = [
        jnp.sum(products[head * HEAD_DIM : (head + 1) * HEAD_DIM], axis=0, keepdims=True)
        for head in range(3)
    ]

    @pl.when(slot == 0)
    def _():
        dk_acc[...] = jnp.zeros_like(dk_acc)
        dv_acc[...] = jnp.zeros_like(dv_acc)
        sum_ref[...] = jnp.zeros_like(sum_ref)

    def one_block(key_block, diagonal):
        at = pl.multiple_of(table[3 + row, key_block] * size, size)
        key, value = k_ref[pl.ds(at, size), :], v_ref[pl.ds(at, size), :]
        key_t = jnp.transpose(key)
        mask = key_mask(start_row, key_block * size, size, diagonal)
        all_scores = [nt(pair_lanes(key, head), q_heads[head]) for head in range(3)]
        all_grads = [nt(pair_lanes(value, head), g_heads[head]) for head in range(3)]
        dq_parts, dk_parts, dv_parts = [], [], []
        for head in range(3):
            scores = jnp.where(mask, all_scores[head], MASKED)
            prob = jnp.exp(scores - lse_ref[0, head : head + 1, :])
            score_grad = (prob * (all_grads[head] - deltas[head])).astype(BF)
            dk_parts.append(nn(score_grad, q_heads[head]))
            dv_parts.append(nn(prob.astype(BF), g_heads[head]))
            dq_parts.append(nn(key_t[head * HEAD_DIM : (head + 1) * HEAD_DIM], score_grad))
        dk_acc[pl.ds(at, size), : width // 2] += dk_parts[0] + dk_parts[1]
        dk_acc[pl.ds(at, size), width // 2 :] += dk_parts[2]
        dv_acc[pl.ds(at, size), : width // 2] += dv_parts[0] + dv_parts[1]
        dv_acc[pl.ds(at, size), width // 2 :] += dv_parts[2]
        return jnp.concatenate(dq_parts, axis=0)

    dq_t = one_block(block, True)
    dq_t = lax.fori_loop(
        0, block - low, lambda step, acc: acc + one_block(block - 1 - step, False), dq_t
    )
    dq_t = jnp.concatenate([dq_t, jnp.zeros((HEAD_DIM, size), F32)], axis=0)
    dq = (jnp.transpose(dq_t) * HEAD_DIM**-0.5).astype(BF)
    d_ref[pl.ds(pl.multiple_of(slot * size, size), size), :width] = dq
    sum_ref[0:1, :] += jnp.sum(dq.astype(F32), axis=0, keepdims=True)

    @pl.when(slot == pl.num_programs(0) - 1)
    def _():
        d_ref[6 * size :, :width] = jnp.zeros((2 * size, width), BF)
        d_ref[:, width : 2 * width] = dk_acc[...].astype(BF)
        dv = dv_acc[...].astype(BF)
        d_ref[:, 2 * width :] = dv
        sum_ref[1:2, :] = jnp.sum(dv.astype(F32), axis=0, keepdims=True)


def attend_backward(qkv, attended, grad, lse, table, starts, size, shard):
    tokens = qkv.shape[0]
    width = 4 * HEAD_DIM
    block = pl.BlockSpec((size, width), lambda s, *_: (s, shard))
    return pl.pallas_call(
        functools.partial(attend_backward_kernel, size),
        grid_spec=pltpu.PrefetchScalarGridSpec(
            num_scalar_prefetch=1,
            grid=(6,),
            in_specs=[
                pl.BlockSpec((8, size), lambda s, *_: (0, s)),
                pl.BlockSpec((size, width), lambda s, *_: (s, 3 * shard)),
                pl.BlockSpec((tokens, width), lambda s, *_: (0, 3 * shard + 1)),
                pl.BlockSpec((tokens, width), lambda s, *_: (0, 3 * shard + 2)),
                block,
                block,
                pl.BlockSpec((1, 8, size), lambda s, *_: (shard, 0, s)),
            ],
            out_specs=[
                pl.BlockSpec((tokens, 3 * width), lambda s, *_: (0, 0)),
                pl.BlockSpec((8, width), lambda s, *_: (0, 0)),
            ],
            scratch_shapes=[pltpu.VMEM((tokens, width), F32), pltpu.VMEM((tokens, width), F32)],
        ),
        out_shape=[
            jax.ShapeDtypeStruct((tokens, 3 * width), BF),
            jax.ShapeDtypeStruct((8, width), F32),
        ],
        compiler_params=params(),
        cost_estimate=SMALL_COST,
        name="attend_backward",
    )(table, starts, qkv, qkv, qkv, attended, grad, lse)


GELU_C = 0.7978845608028654
GELU_A = 0.044715


def mlp_kernel(
    x_ref, own_ref, other_ref, bg_ref, vec_ref, upb_ref, up_own, up_far, dn_own, dn_far,
    res_ref, mid_ref, act_ref, hg_ref, out_ref, give_ref, midin_ref, upbg_ref,
):
    step = pl.program_id(0)
    proj_bias, gain, shift = vec_ref[0:1, :], vec_ref[1:2, :], vec_ref[2:3, :]
    residual = (
        x_ref[...].astype(F32) + own_ref[...].astype(F32) + other_ref[...].astype(F32) + proj_bias
    )
    res_ref[...] = residual
    centered = residual - jnp.mean(residual, axis=-1, keepdims=True)
    variance = jnp.mean(centered * centered, axis=-1, keepdims=True)
    mid = (centered * lax.rsqrt(variance + NORM_EPS) * gain + shift).astype(BF)
    mid_ref[...] = mid
    bg = bg_ref[...]

    @pl.when(step == 0)
    def _():
        upbg_ref[...] = jnp.zeros_like(upbg_ref)

    out = None
    midin = None
    for part, (up_w, dn_w) in enumerate(((up_own[...], dn_own[...]), (up_far[0], dn_far[0]))):
        hidden = nn(mid, up_w) + upb_ref[part : part + 1, :]
        act_grad = nt(bg, dn_w)
        square = hidden * hidden
        bent = jnp.tanh(GELU_C * (hidden + GELU_A * hidden * square))
        half = 0.5 * (1.0 + bent)
        act = (hidden * half).astype(BF)
        slope = half + 0.5 * hidden * (1.0 - bent * bent) * (GELU_C + 3.0 * GELU_C * GELU_A * square)
        grad = (act_grad * slope).astype(BF)
        act_ref[part] = act
        hg_ref[part] = grad
        upbg_ref[part : part + 1, :] += jnp.sum(grad.astype(F32), axis=0, keepdims=True)
        out_part = nn(act, dn_w)
        midin_part = nt(grad, up_w)
        out = out_part if out is None else out + out_part
        midin = midin_part if midin is None else midin + midin_part
    midin_ref[...] = midin.astype(BF)

    @pl.when(step < 3)
    def _():
        out_ref[...] = out + residual + vec_ref[3:4, :]

    @pl.when(step >= 3)
    def _():
        give_ref[...] = out.astype(BF)


def mlp(tokens, own, other, bg, vectors, up_bias, up_own, down_own, far, size):
    rows, width = own.shape
    inner = up_own.shape[1]
    block = pl.BlockSpec((size, width), lambda i: (own_first(i), 0))
    wide = pl.BlockSpec((2, size, inner), lambda i: (0, own_first(i), 0))
    return pl.pallas_call(
        mlp_kernel,
        grid=(rows // size,),
        in_specs=[
            block,
            block,
            pl.BlockSpec((size, width), lambda i: (swapped_slot(own_first(i)), 0)),
            block,
            fixed((8, width)),
            fixed((8, inner)),
            fixed((width, inner)),
            pl.BlockSpec((1, width, inner), lambda i: (0, 0, 0), pipeline_mode=pl.Buffered(1)),
            fixed((inner, width)),
            pl.BlockSpec((1, inner, width), lambda i: (1, 0, 0), pipeline_mode=pl.Buffered(1)),
        ],
        out_specs=[
            block, block, wide, wide,
            pl.BlockSpec((size, width), lambda i: (jnp.minimum(i, 2), 0)),
            pl.BlockSpec((size, width), lambda i: (jnp.maximum(i - 3, 0), 0)),
            block,
            pl.BlockSpec((8, inner), lambda i: (0, 0)),
        ],
        out_shape=[
            jax.ShapeDtypeStruct((rows, width), F32),
            jax.ShapeDtypeStruct((rows, width), BF),
            jax.ShapeDtypeStruct((2, rows, inner), BF),
            jax.ShapeDtypeStruct((2, rows, inner), BF),
            jax.ShapeDtypeStruct((rows // 2, width), F32),
            jax.ShapeDtypeStruct((rows // 2, width), BF),
            jax.ShapeDtypeStruct((rows, width), BF),
            jax.ShapeDtypeStruct((8, inner), F32),
        ],
        compiler_params=params(),
        cost_estimate=SMALL_COST,
        name="mlp",
    )(tokens, own, other, bg, vectors, up_bias, up_own, far, down_own, far)


def mid_backward_kernel(
    res_ref, own_ref, other_ref, bg_ref, vec_ref, proj_ref, rg_ref, ag_ref, atg_ref, sum_ref
):
    step = pl.program_id(0)
    gain = vec_ref[1:2, :]
    residual = res_ref[...]
    centered = residual - jnp.mean(residual, axis=-1, keepdims=True)
    rstd = lax.rsqrt(jnp.mean(centered * centered, axis=-1, keepdims=True) + NORM_EPS)
    xhat = centered * rstd
    mid_in = own_ref[...].astype(F32) + other_ref[...].astype(F32)
    gy = mid_in * gain
    through = rstd * (
        gy
        - jnp.mean(gy, axis=-1, keepdims=True)
        - xhat * jnp.mean(gy * xhat, axis=-1, keepdims=True)
    )
    total = bg_ref[...].astype(F32) + through
    low = total.astype(BF)
    ag_ref[...] = low
    atg_ref[...] = nt(low, proj_ref[...]).astype(BF)

    @pl.when(step < 3)
    def _():
        rg_ref[...] = total

    @pl.when(step == 0)
    def _():
        sum_ref[...] = jnp.zeros_like(sum_ref)

    sum_ref[0:1, :] += jnp.sum(mid_in * xhat, axis=0, keepdims=True)
    sum_ref[1:2, :] += jnp.sum(mid_in, axis=0, keepdims=True)
    sum_ref[2:3, :] += jnp.sum(low.astype(F32), axis=0, keepdims=True)
    sum_ref[3:4, :] += jnp.sum(bg_ref[...].astype(F32), axis=0, keepdims=True)


def mid_backward(residual, own, other, bg, vectors, proj, size):
    rows, width = own.shape
    inner = proj.shape[0]
    block = pl.BlockSpec((size, width), lambda i: (own_first(i), 0))
    return pl.pallas_call(
        mid_backward_kernel,
        grid=(rows // size,),
        in_specs=[
            block,
            block,
            pl.BlockSpec((size, width), lambda i: (swapped_slot(own_first(i)), 0)),
            block,
            fixed((8, width)),
            fixed((inner, width)),
        ],
        out_specs=[
            pl.BlockSpec((size, width), lambda i: (jnp.minimum(i, 2), 0)),
            block,
            pl.BlockSpec((size, inner), lambda i: (own_first(i), 0)),
            pl.BlockSpec((8, width), lambda i: (0, 0)),
        ],
        out_shape=[
            jax.ShapeDtypeStruct((rows // 2, width), F32),
            jax.ShapeDtypeStruct((rows, width), BF),
            jax.ShapeDtypeStruct((rows, inner), BF),
            jax.ShapeDtypeStruct((8, width), F32),
        ],
        compiler_params=params(),
        cost_estimate=SMALL_COST,
        name="mid_backward",
    )(residual, own, other, bg, vectors, proj)


def first_kernel(x_ref, vec_ref, far_ref, own_ref, bias_ref, normed_ref, qkv_ref):
    stream = x_ref[...].astype(F32)
    centered = stream - jnp.mean(stream, axis=-1, keepdims=True)
    variance = jnp.mean(centered * centered, axis=-1, keepdims=True)
    normed = (
        centered * lax.rsqrt(variance + NORM_EPS) * vec_ref[4:5, :] + vec_ref[5:6, :]
    ).astype(BF)
    normed_ref[...] = normed
    lanes = 4 * HEAD_DIM
    feats = far_ref.shape[0] // 3
    for shard, w_ref in enumerate((far_ref, own_ref)):
        for i in range(3):
            at = (3 * shard + i) * lanes
            part = nt(normed, w_ref[i * feats : (i + 1) * feats]) + bias_ref[
                3 * shard + i : 3 * shard + i + 1, :feats
            ]
            qkv_ref[:, at : at + feats] = part.astype(BF)
            qkv_ref[:, at + feats : at + lanes] = jnp.zeros((part.shape[0], lanes - feats), BF)


def first(tokens, vectors, far, own, bias, size):
    rows, width = tokens.shape
    outs = 6 * 4 * HEAD_DIM
    block = pl.BlockSpec((size, width), lambda i: (i, 0))
    return pl.pallas_call(
        first_kernel,
        grid=(rows // size,),
        in_specs=[block, fixed((8, width)), fixed(far.shape), fixed(own.shape), fixed(bias.shape)],
        out_specs=[block, pl.BlockSpec((size, outs), lambda i: (i, 0))],
        out_shape=[
            jax.ShapeDtypeStruct((rows, width), BF),
            jax.ShapeDtypeStruct((rows, outs), BF),
        ],
        compiler_params=params(),
        cost_estimate=SMALL_COST,
        name="first_norm_qkv",
    )(tokens, vectors, far, own, bias)


def first_in_kernel(far_d, own_d, far_w, own_w, own_ref, give_ref):
    step = pl.program_id(0)
    half = far_d.shape[0] // 2
    lanes = 4 * HEAD_DIM
    feats = far_w.shape[0] // 3
    total = None
    for d_ref, w_ref in ((far_d, far_w), (own_d, own_w)):
        for i in range(3):
            part = nn(d_ref[:, i * lanes : i * lanes + feats], w_ref[i * feats : (i + 1) * feats])
            total = part if total is None else total + part
    total = total.astype(BF)

    @pl.when(step == 0)
    def _():
        own_ref[: 2 * half] = total

    @pl.when(step == 1)
    def _():
        give_ref[: 2 * half] = total

    @pl.when(step == 2)
    def _():
        own_ref[2 * half : 3 * half] = total[:half]
        give_ref[2 * half : 3 * half] = total[half:]

    @pl.when(step == 3)
    def _():
        own_ref[3 * half :] = total[:half]
        give_ref[3 * half :] = total[half:]


def first_in(far_grad, own_grad, far, own, size):
    rows, lanes = far_grad.shape
    width = far.shape[1]
    block = pl.BlockSpec((2 * size, lanes), lambda i: (i, 0))
    whole = pl.BlockSpec((rows // 2, width), lambda i: (0, 0))
    return pl.pallas_call(
        first_in_kernel,
        grid=(4,),
        in_specs=[block, block, fixed(far.shape), fixed(own.shape)],
        out_specs=[whole, whole],
        out_shape=[jax.ShapeDtypeStruct((rows // 2, width), BF)] * 2,
        compiler_params=params(),
        cost_estimate=SMALL_COST,
        name="first_in",
    )(far_grad, own_grad, far, own)


def first_backward_kernel(x_ref, own_ref, got_ref, rg_ref, vec_ref, *refs):
    extra_ref, (in_ref, sum_ref) = (refs[0] if len(refs) == 3 else None), refs[-2:]
    stream = x_ref[...].astype(F32)
    centered = stream - jnp.mean(stream, axis=-1, keepdims=True)
    rstd = lax.rsqrt(jnp.mean(centered * centered, axis=-1, keepdims=True) + NORM_EPS)
    xhat = centered * rstd
    grad = own_ref[...].astype(F32) + got_ref[...].astype(F32)
    if extra_ref is not None:
        grad = grad + extra_ref[...].astype(F32)
    gy = grad * vec_ref[4:5, :]
    through = rstd * (
        gy
        - jnp.mean(gy, axis=-1, keepdims=True)
        - xhat * jnp.mean(gy * xhat, axis=-1, keepdims=True)
    )
    in_ref[...] = (rg_ref[...] + through).astype(BF)

    @pl.when(pl.program_id(0) == 0)
    def _():
        sum_ref[...] = jnp.zeros_like(sum_ref)

    sum_ref[0:1, :] += jnp.sum(grad * xhat, axis=0, keepdims=True)
    sum_ref[1:2, :] += jnp.sum(grad, axis=0, keepdims=True)


def first_backward(tokens, own, got, residual_grad, vectors, extra, size, owned):
    width = tokens.shape[1]
    stride = owned[1] - owned[0] if len(owned) > 1 else 1
    block = pl.BlockSpec((size, width), lambda i: (owned[0] + stride * i, 0))
    slot = pl.BlockSpec((size, width), lambda i: (owned[0] + 2 * stride * i, 0))
    more = () if extra is None else (extra,)
    return pl.pallas_call(
        first_backward_kernel,
        grid=(len(owned),),
        in_specs=[slot, block, block, block, fixed((8, width))]
        + [pl.BlockSpec((size, width), lambda i: (0, 0))] * len(more),
        out_specs=[
            pl.BlockSpec((size, width), lambda i: (i, 0)),
            pl.BlockSpec((8, width), lambda i: (0, 0)),
        ],
        out_shape=[
            jax.ShapeDtypeStruct((len(owned) * size, width), BF),
            jax.ShapeDtypeStruct((8, width), F32),
        ],
        compiler_params=params(),
        cost_estimate=SMALL_COST,
        name="first_backward",
    )(tokens, own, got, residual_grad, vectors, *more)


def dp_partners(count, bit):
    return [(d, d ^ bit) for d in range(count)]


def dp_bits():
    return [1 << i for i in range(lax.axis_size("dp").bit_length() - 1)]


def dp_swap(value, bit):
    return lax.ppermute(value, "dp", dp_partners(lax.axis_size("dp"), bit))


def upper(bit):
    return (lax.axis_index("dp") & bit) != 0


def keep_and_give(value, side, rows):
    keep = lax.dynamic_slice_in_dim(value, side * rows, rows, 0)
    give = lax.dynamic_slice_in_dim(value, (1 - side) * rows, rows, 0)
    return keep, give


def halve(value, bit):
    keep, give = keep_and_give(value, jnp.where(upper(bit), 1, 0), value.shape[0] // 2)
    return keep.astype(F32) + dp_swap(give.astype(BF), bit).astype(F32)


def double(value, bit, axis=0):
    got = dp_swap(value, bit)
    return jnp.where(
        upper(bit),
        jnp.concatenate([got, value], axis=axis),
        jnp.concatenate([value, got], axis=axis),
    )


def dp_part(value, axis):
    bits = dp_bits()
    place = sum(jnp.where(upper(bit), value.shape[axis] // (2 * bit), 0) for bit in bits)
    return lax.dynamic_slice_in_dim(value, place, value.shape[axis] // (2 * bits[-1]), axis)


def sum_everywhere(value):
    value = value + core_swap(value)
    value = value + x_swap(value)
    for bit in dp_bits():
        value = value + dp_swap(value, bit)
    return value


def after(value, *earlier):
    return lax.optimization_barrier((value,) + earlier)[0]


def body(
    hidden_in,
    doc_ids,
    first_gain,
    first_shift,
    qkv_weight,
    qv_bias,
    proj_weight,
    proj_bias,
    second_gain,
    second_shift,
    up_weight,
    up_bias,
    down_weight,
    down_bias,
    out_grad,
):
    size, rows_dev, width = hidden_in.shape
    length = doc_ids.shape[0]
    place = lax.axis_index("tensor")
    right = place >= 2
    feats = qkv_weight.shape[2]
    inner = up_weight.shape[1]

    def split_rows(value):
        first, mid, last = value[:, 0], value[:, 1], value[:, 2]
        return jnp.where(right, last, first), mid, jnp.where(right, first, last)

    def join_rows(main, mid, other):
        return jnp.stack(
            [jnp.where(right, other, main), mid, jnp.where(right, main, other)], axis=1
        )

    pieces = jnp.stack([dp_part(up_weight, 0), dp_part(down_weight, 0)])
    with jax.named_scope("mlp_weights_x"):
        far_mlp = x_swap(pieces)

    main, mid, away = split_rows(hidden_in)
    home = jnp.concatenate([main, mid], axis=0)
    with jax.named_scope("tokens"):
        far = x_swap(jnp.concatenate([away, mid], axis=0))
        near = core_swap(home)
        far_near = core_swap(far)
    tokens = jnp.concatenate(
        [home, near, far[:size], far_near[:size], far[size:], far_near[size:]], axis=0
    )

    qkv_own = jnp.transpose(qkv_weight, (1, 2, 0)).reshape(3 * feats, width)
    biases = jnp.concatenate([qv_bias, up_bias.reshape(-1, feats)], axis=0)
    with jax.named_scope("qkv_weights_x"):
        qkv_far = x_swap(qkv_own)
        biases_far = x_swap(biases)
    with jax.named_scope("proj_weight_x"):
        proj_far = x_swap(proj_weight)
    with jax.named_scope("mlp_weights_dp"):
        for bit in reversed(dp_bits()[1:]):
            far_mlp = double(far_mlp, bit, 1)
        part_mlp = far_mlp
        far_mlp = double(far_mlp, dp_bits()[0], 1)

    local_ids = lax.dynamic_slice_in_dim(doc_ids, place * size, size, 0)
    cot = jnp.where((local_ids >= 0)[:, :, None], out_grad, jnp.zeros_like(out_grad))
    g_main, g_mid, g_away = split_rows(cot)
    g_home = jnp.concatenate([g_main, g_mid], axis=0)
    with jax.named_scope("cotangent"):
        g_near = core_swap(g_home)
        g_far = x_swap(g_away)
        g_far_near = core_swap(g_far)
    branch_grad = jnp.concatenate([g_home, g_near, g_far, g_far_near], axis=0)

    ids = jnp.stack([jnp.where(right, doc_ids[:, 2], doc_ids[:, 0]), doc_ids[:, 1]])
    position = lax.broadcasted_iota(jnp.int32, ids.shape, 1)
    count_below = jnp.stack(
        [jnp.sum(((ids >= 0) & (ids < d)).astype(jnp.int32), axis=1) for d in range(8)], axis=1
    )
    which = ids[:, :, None] == jnp.arange(8, dtype=jnp.int32)[None, None, :]
    starts = jnp.sum(jnp.where(which, count_below[:, None, :], 0), axis=2)
    starts = jnp.where(ids >= 0, starts, position).reshape(2, length // size, size)
    slot_row = jnp.array(SLOT_ROW, jnp.int32)
    slot_block = jnp.array(SLOT_K, jnp.int32) ^ place
    slot_start = starts.reshape(-1, size)[slot_row * (length // size) + slot_block]
    low_block = slot_start[:, 0] // size
    where_key = jnp.array(SLOT, jnp.int32)[:, jnp.arange(4, dtype=jnp.int32) ^ place]
    table = jnp.concatenate(
        [
            jnp.pad(jnp.stack([slot_row, slot_block, low_block]), ((0, 0), (0, 2))),
            jnp.pad(where_key, ((0, 0), (0, 4))),
        ]
    )
    start_rows = jnp.broadcast_to(slot_start.reshape(1, -1), (8, 6 * size))

    vectors = jnp.stack(
        [proj_bias, second_gain, second_shift, down_bias, first_gain, first_shift]
        + [jnp.zeros_like(proj_bias)] * 2
    ).astype(F32)
    up_biases = jnp.stack(
        [up_bias, biases_far[2:].reshape(-1)] + [jnp.zeros_like(up_bias)] * 6
    ).astype(F32)

    none = jnp.zeros((1, feats), qv_bias.dtype)
    qkv_bias = jnp.concatenate(
        [biases_far[:1], none, biases_far[1:2], qv_bias[:1], none, qv_bias[1:], none, none]
    ).astype(F32)
    normed, qkv = first(tokens, vectors, qkv_far, qkv_own, qkv_bias, 2 * size)

    attended, lse = attend_forward(after(qkv, part_mlp), table, start_rows, size)
    gap = jnp.zeros((4 * HEAD_DIM - feats, width), BF)
    proj_both = jnp.concatenate([proj_far, gap, proj_weight, gap], axis=0)
    attn_part = nn(after(attended, g_far, far_mlp), proj_both).astype(BF)
    with jax.named_scope("attn_core"):
        attn_other = core_swap(attn_part)

    residual, normed_mid, act, hidden_grad, out_own, out_give, mid_part, up_sums = mlp(
        tokens, attn_part, attn_other, branch_grad, vectors, up_biases,
        up_weight, down_weight, far_mlp, size,
    )

    lanes = 4 * HEAD_DIM
    bit_y, bits_z = dp_bits()[0], dp_bits()[1:]

    def shard_rows(value):
        return jnp.concatenate([value[i * lanes : i * lanes + feats] for i in range(3)], axis=0)

    with jax.named_scope("mid_core"):
        mid_other = core_swap(mid_part)
    down_away = tn(act[1], branch_grad).astype(BF)
    with jax.named_scope("down_grad_x"):
        down_got = x_swap(down_away)
    residual_grad, attn_grad, attended_grad, mid_sums = mid_backward(
        after(residual, down_away), mid_part, mid_other, branch_grad, vectors, proj_both, size
    )

    act, hidden_grad, out_own, out_give, attended_grad = lax.optimization_barrier(
        (act, hidden_grad, out_own, out_give, attended_grad)
    )
    up_away = tn(normed_mid, hidden_grad[1]).astype(BF)
    with jax.named_scope("up_grad_x"):
        up_got = x_swap(up_away)
    d_far, sums_far = attend_backward(
        qkv, attended, after(attended_grad, up_away), lse, table, start_rows, size, 0
    )
    qkv_away = shard_rows(tn(d_far, normed)).astype(BF)
    with jax.named_scope("down_grad_dp"):
        down = tn(act[0], after(branch_grad, qkv_away)) + down_got.astype(F32)
    with jax.named_scope("qkv_grad_x"):
        qkv_got = x_swap(qkv_away)
    d_own, sums_own = attend_backward(
        qkv, attended, after(attended_grad, down), lse, table, start_rows, size, 1
    )
    with jax.named_scope("down_grad_dp"):
        down = halve(down, bit_y)
    act, hidden_grad, attended, attn_grad, d_own, down, out_give = lax.optimization_barrier(
        (act, hidden_grad, attended, attn_grad, d_own, down, out_give)
    )

    own_in, give_in = first_in(d_far, d_own, qkv_far, qkv_own, size)
    with jax.named_scope("first_core"):
        got_in = core_swap(give_in)
    with jax.named_scope("block_out"):
        out_got = core_swap(out_give)
    proj_pair = tn(attended, attn_grad)
    with jax.named_scope("proj_grad_x"):
        proj_got = x_swap(proj_pair[:feats].astype(BF))
    with jax.named_scope("up_grad_dp"):
        up = tn(normed_mid, hidden_grad[0]) + up_got.astype(F32)
    with jax.named_scope("qkv_grad_dp"):
        qkv_sum = shard_rows(tn(d_own, normed)) + qkv_got.astype(F32)
        tail = jnp.concatenate(
            [qkv_sum, proj_pair[lanes : lanes + feats] + proj_got.astype(F32)], axis=0
        )
    with jax.named_scope("first_mid_x"):
        extra = x_swap(
            (own_in[3 * size :].astype(F32) + got_in[3 * size :].astype(F32)).astype(BF)
        )
    in_main, sums_main = first_backward(
        tokens, own_in, got_in, residual_grad, vectors, None, size, (0, 2)
    )
    in_mid, sums_mid = first_backward(
        tokens, own_in, got_in, residual_grad, vectors, extra, size, (1,)
    )
    with jax.named_scope("in_grad_x"):
        in_away = x_swap(in_main[size:])
    with jax.named_scope("block_out"):
        out_full = (out_own + out_got.astype(F32)).astype(BF)
        out_away = x_swap(out_full[2 * size :])

    sums = [down, up, tail]
    stages = [1, 0, 0]
    steps = [functools.partial(halve, bit=bit) for bit in dp_bits()]
    steps += [functools.partial(double, bit=bit) for bit in reversed(dp_bits())]
    names = ("down_grad_dp", "up_grad_dp", "tail_grad_dp")
    started = 1
    while min(stages) < len(steps):
        started = min(started + 1, 3)
        for i in range(started):
            if stages[i] < len(steps):
                value = sums[i]
                if stages[i] == len(steps) // 2:
                    value = value.astype(BF)
                with jax.named_scope(names[i]):
                    sums[i] = steps[stages[i]](value)
                stages[i] += 1
        sums = list(lax.optimization_barrier(tuple(sums)))
    down_sum, up_sum, tail_sum = sums

    block_out = join_rows(out_full[:size], out_full[size : 2 * size], out_away)
    in_grad = join_rows(in_main[:size], in_mid, in_away)

    up_slots = jnp.zeros((4, inner), F32)
    up_slots = lax.dynamic_update_slice_in_dim(up_slots, up_sums[0:1], place, 0)
    up_slots = lax.dynamic_update_slice_in_dim(up_slots, up_sums[1:2], place ^ 2, 0)
    qv_own = sums_own[:2, :feats].reshape(1, -1)
    qv_far = sums_far[:2, :feats].reshape(1, -1)
    qv_slots = jnp.zeros((4, 2 * feats), F32)
    qv_slots = lax.dynamic_update_slice_in_dim(qv_slots, qv_own, place, 0)
    qv_slots = lax.dynamic_update_slice_in_dim(qv_slots, qv_far, place ^ 2, 0)
    small = jnp.concatenate(
        [
            (sums_main + sums_mid)[:2],
            0.5 * mid_sums[:4],
            up_slots,
            qv_slots.reshape(-1, width),
        ],
        axis=0,
    )
    with jax.named_scope("small_sums"):
        small = sum_everywhere(small)
    up_bias_grad = lax.dynamic_slice_in_dim(small, 6 + place, 1, 0)[0]
    qv_all = small[10:].reshape(4, 2, feats)
    qv_bias_grad = lax.dynamic_slice_in_dim(qv_all, place, 1, 0)[0]

    qkv_weight_grad = jnp.transpose(
        tail_sum[: 3 * feats].reshape(3, feats, width), (2, 0, 1)
    ).astype(F32)
    return (
        block_out,
        in_grad,
        small[0],
        small[1],
        qkv_weight_grad,
        qv_bias_grad,
        tail_sum[3 * feats :].astype(F32),
        small[4],
        small[2],
        small[3],
        up_sum.astype(F32),
        up_bias_grad,
        down_sum.astype(F32),
        small[5],
    )


def solution(mesh):
    in_specs = (
        P("tensor", "dp", None),
        P(None, "dp"),
        P(),
        P(),
        P(None, None, "tensor"),
        P(None, "tensor"),
        P("tensor", None),
        P(),
        P(),
        P(),
        P(None, "tensor"),
        P("tensor"),
        P("tensor", None),
        P(),
        P("tensor", "dp", None),
    )
    out_specs = (
        P("tensor", "dp", None),
        P("tensor", "dp", None),
        P(),
        P(),
        P(None, None, "tensor"),
        P(None, "tensor"),
        P("tensor", None),
        P(),
        P(),
        P(),
        P(None, "tensor"),
        P("tensor"),
        P("tensor", None),
        P(),
    )
    return jax.shard_map(body, mesh=mesh, in_specs=in_specs, out_specs=out_specs, check_vma=False)
```

```python
import functools

import jax
import jax.numpy as jnp
from jax import lax
from jax.experimental import pallas as pl
from jax.experimental.pallas import tpu as pltpu
from jax.sharding import PartitionSpec as P

HEAD_DIM = 64
NORM_EPS = 1e-05
MASKED = -1e30
BF = jnp.bfloat16
F32 = jnp.float32
VMEM_LIMIT = 56 * 1024 * 1024

SLOT = ((0, 2, 4, 5), (1, 3, 6, 7))
SLOT_ROW = (0, 1, 0, 1, 0, 0)
SLOT_K = (0, 0, 1, 1, 2, 3)
X_SWAP = ((0, 2), (1, 3), (2, 0), (3, 1))
CORE_SWAP = ((0, 1), (1, 0), (2, 3), (3, 2))


def x_swap(value):
    return lax.ppermute(value, "tensor", X_SWAP)


def core_swap(value):
    return lax.ppermute(value, "tensor", CORE_SWAP)


def params(semantics=None):
    return pltpu.CompilerParams(vmem_limit_bytes=VMEM_LIMIT)


def fixed(shape):
    return pl.BlockSpec(shape, lambda *ids: (0,) * len(shape), pipeline_mode=pl.Buffered(1))


def nt(left, right):
    return lax.dot_general(left, right, (((1,), (1,)), ((), ())), preferred_element_type=F32)


def nn(left, right):
    return lax.dot_general(left, right, (((1,), (0,)), ((), ())), preferred_element_type=F32)


def tn(left, right):
    return lax.dot_general(left, right, (((0,), (0,)), ((), ())), preferred_element_type=F32)


SMALL_COST = pl.CostEstimate(flops=1, bytes_accessed=1, transcendentals=0)


def key_mask(start_row, key_first, size, diagonal):
    keys = lax.broadcasted_iota(jnp.int32, (size, size), 0)
    mask = keys >= start_row - key_first
    if diagonal:
        mask = mask & (keys <= lax.broadcasted_iota(jnp.int32, (size, size), 1))
    return mask


def head_rows(size):
    lane = lax.broadcasted_iota(jnp.int32, (size, 2 * HEAD_DIM), 1)

    def select(value):
        zero = jnp.zeros((size, 2 * HEAD_DIM), value.dtype)
        pair = value[:, : 2 * HEAD_DIM]
        return (
            jnp.where(lane < HEAD_DIM, pair, zero),
            jnp.where(lane < HEAD_DIM, zero, pair),
            value[:, 2 * HEAD_DIM :],
        )

    return select


def pair_lanes(value, head):
    first = 2 * HEAD_DIM * (head // 2)
    return value[:, first : first + 2 * HEAD_DIM]


def attend_forward_kernel(size, table, start_ref, q_ref, k_ref, v_ref, out_ref, lse_ref):
    slot = pl.program_id(1)
    row, block, low = table[0, slot], table[1, slot], table[2, slot]
    start_row = start_ref[0:1, :]
    select = head_rows(size)
    heads = select(q_ref[...] * jnp.asarray(HEAD_DIM**-0.5, BF))

    def load(key_block):
        at = pl.multiple_of(table[3 + row, key_block] * size, size)
        return k_ref[pl.ds(at, size), :], jnp.transpose(v_ref[pl.ds(at, size), :])

    key, value_t = load(block)
    mask = key_mask(start_row, block * size, size, True)
    all_scores = [nt(pair_lanes(key, head), heads[head]) for head in range(3)]
    carry = []
    for head in range(3):
        scores = jnp.where(mask, all_scores[head], MASKED)
        top = jnp.max(scores, axis=0, keepdims=True)
        weight = jnp.exp(scores - top)
        total = jnp.sum(weight, axis=0, keepdims=True)
        acc = nn(value_t[head * HEAD_DIM : (head + 1) * HEAD_DIM], weight.astype(BF))
        carry += [top, total, acc]

    def earlier(step, carry):
        key_block = block - 1 - step
        key, value_t = load(key_block)
        mask = key_mask(start_row, key_block * size, size, False)
        all_scores = [nt(pair_lanes(key, head), heads[head]) for head in range(3)]
        new = []
        for head in range(3):
            top, total, acc = carry[3 * head : 3 * head + 3]
            scores = jnp.where(mask, all_scores[head], MASKED)
            higher = jnp.maximum(top, jnp.max(scores, axis=0, keepdims=True))
            shrink = jnp.exp(top - higher)
            weight = jnp.exp(scores - higher)
            total = total * shrink + jnp.sum(weight, axis=0, keepdims=True)
            acc = acc * shrink + nn(
                value_t[head * HEAD_DIM : (head + 1) * HEAD_DIM], weight.astype(BF)
            )
            new += [higher, total, acc]
        return tuple(new)

    carry = lax.fori_loop(0, block - low, earlier, tuple(carry))
    parts = [carry[3 * head + 2] / carry[3 * head + 1] for head in range(3)]
    parts.append(jnp.zeros_like(parts[0]))
    out_ref[...] = jnp.transpose(jnp.concatenate(parts, axis=0)).astype(BF)
    for head in range(3):
        lse_ref[head : head + 1, :] = carry[3 * head] + jnp.log(carry[3 * head + 1])


def attend_forward(qkv, table, starts, size):
    width = 4 * HEAD_DIM
    tokens = qkv.shape[0]
    return pl.pallas_call(
        functools.partial(attend_forward_kernel, size),
        grid_spec=pltpu.PrefetchScalarGridSpec(
            num_scalar_prefetch=1,
            grid=(2, 6),
            in_specs=[
                pl.BlockSpec((8, size), lambda p, s, *_: (0, s)),
                pl.BlockSpec((size, width), lambda p, s, *_: (s, 3 * p)),
                pl.BlockSpec((tokens, width), lambda p, s, *_: (0, 3 * p + 1)),
                pl.BlockSpec((tokens, width), lambda p, s, *_: (0, 3 * p + 2)),
            ],
            out_specs=[
                pl.BlockSpec((size, width), lambda p, s, *_: (s, p)),
                pl.BlockSpec((8, size), lambda p, s, *_: (p, s)),
            ],
        ),
        out_shape=[
            jax.ShapeDtypeStruct((6 * size, 2 * width), BF),
            jax.ShapeDtypeStruct((16, 6 * size), F32),
        ],
        compiler_params=params(),
        cost_estimate=SMALL_COST,
        name="attend_forward",
    )(table, starts, qkv, qkv, qkv)


def attend_backward_kernel(
    size, table, start_ref, q_ref, k_ref, v_ref, out_ref, grad_ref, lse_ref,
    d_ref, sum_ref, dk_acc, dv_acc,
):
    slot = pl.program_id(0)
    width = 4 * HEAD_DIM
    row, block, low = table[0, slot], table[1, slot], table[2, slot]
    start_row = start_ref[0:1, :]
    select = head_rows(size)
    q_heads = select(q_ref[...] * jnp.asarray(HEAD_DIM**-0.5, BF))
    grad = grad_ref[...]
    g_heads = select(grad)
    products = jnp.transpose(grad.astype(F32) * out_ref[...].astype(F32))
    deltas = [
        jnp.sum(products[head * HEAD_DIM : (head + 1) * HEAD_DIM], axis=0, keepdims=True)
        for head in range(3)
    ]

    @pl.when(slot == 0)
    def _():
        dk_acc[...] = jnp.zeros_like(dk_acc)
        dv_acc[...] = jnp.zeros_like(dv_acc)
        sum_ref[...] = jnp.zeros_like(sum_ref)

    def one_block(key_block, diagonal):
        at = pl.multiple_of(table[3 + row, key_block] * size, size)
        key, value = k_ref[pl.ds(at, size), :], v_ref[pl.ds(at, size), :]
        key_t = jnp.transpose(key)
        mask = key_mask(start_row, key_block * size, size, diagonal)
        all_scores = [nt(pair_lanes(key, head), q_heads[head]) for head in range(3)]
        all_grads = [nt(pair_lanes(value, head), g_heads[head]) for head in range(3)]
        dq_parts, dk_parts, dv_parts = [], [], []
        for head in range(3):
            scores = jnp.where(mask, all_scores[head], MASKED)
            prob = jnp.exp(scores - lse_ref[head : head + 1, :])
            score_grad = (prob * (all_grads[head] - deltas[head])).astype(BF)
            dk_parts.append(nn(score_grad, q_heads[head]))
            dv_parts.append(nn(prob.astype(BF), g_heads[head]))
            dq_parts.append(nn(key_t[head * HEAD_DIM : (head + 1) * HEAD_DIM], score_grad))
        dk_acc[pl.ds(at, size), : width // 2] += dk_parts[0] + dk_parts[1]
        dk_acc[pl.ds(at, size), width // 2 :] += dk_parts[2]
        dv_acc[pl.ds(at, size), : width // 2] += dv_parts[0] + dv_parts[1]
        dv_acc[pl.ds(at, size), width // 2 :] += dv_parts[2]
        return jnp.concatenate(dq_parts, axis=0)

    dq_t = one_block(block, True)
    dq_t = lax.fori_loop(
        0, block - low, lambda step, acc: acc + one_block(block - 1 - step, False), dq_t
    )
    dq_t = jnp.concatenate([dq_t, jnp.zeros((HEAD_DIM, size), F32)], axis=0)
    dq = (jnp.transpose(dq_t) * HEAD_DIM**-0.5).astype(BF)
    d_ref[pl.ds(pl.multiple_of(slot * size, size), size), :width] = dq
    sum_ref[0:1, :] += jnp.sum(dq.astype(F32), axis=0, keepdims=True)

    @pl.when(slot == pl.num_programs(0) - 1)
    def _():
        d_ref[6 * size :, :width] = jnp.zeros((2 * size, width), BF)
        d_ref[:, width : 2 * width] = dk_acc[...].astype(BF)
        dv = dv_acc[...].astype(BF)
        d_ref[:, 2 * width :] = dv
        sum_ref[1:2, :] = jnp.sum(dv.astype(F32), axis=0, keepdims=True)


def attend_backward(qkv, attended, grad, lse, table, starts, size, shard):
    tokens = qkv.shape[0]
    width = 4 * HEAD_DIM
    block = pl.BlockSpec((size, width), lambda s, *_: (s, shard))
    return pl.pallas_call(
        functools.partial(attend_backward_kernel, size),
        grid_spec=pltpu.PrefetchScalarGridSpec(
            num_scalar_prefetch=1,
            grid=(6,),
            in_specs=[
                pl.BlockSpec((8, size), lambda s, *_: (0, s)),
                pl.BlockSpec((size, width), lambda s, *_: (s, 3 * shard)),
                pl.BlockSpec((tokens, width), lambda s, *_: (0, 3 * shard + 1)),
                pl.BlockSpec((tokens, width), lambda s, *_: (0, 3 * shard + 2)),
                block,
                block,
                pl.BlockSpec((8, size), lambda s, *_: (shard, s)),
            ],
            out_specs=[
                pl.BlockSpec((tokens, 3 * width), lambda s, *_: (0, 0)),
                pl.BlockSpec((8, width), lambda s, *_: (0, 0)),
            ],
            scratch_shapes=[pltpu.VMEM((tokens, width), F32), pltpu.VMEM((tokens, width), F32)],
        ),
        out_shape=[
            jax.ShapeDtypeStruct((tokens, 3 * width), BF),
            jax.ShapeDtypeStruct((8, width), F32),
        ],
        compiler_params=params(),
        cost_estimate=SMALL_COST,
        name="attend_backward",
    )(table, starts, qkv, qkv, qkv, attended, grad, lse)


def prepare_kernel(size, place_ref, ids_ref, *refs):
    vectors, (start_ref, table_ref, vec_ref, rows_ref) = refs[:-4], refs[-4:]
    for i, ref in enumerate(vectors):
        vec_ref[i : i + 1, :] = ref[...].astype(F32).reshape(1, -1)
    vec_ref[len(vectors) :, :] = jnp.zeros((8 - len(vectors), vec_ref.shape[1]), F32)
    place = place_ref[0]
    ids = ids_ref[...]
    length = ids.shape[1]
    position = lax.broadcasted_iota(jnp.int32, ids.shape, 1)
    starts = position
    for doc in range(8):
        here = ids == doc
        first_one = jnp.min(jnp.where(here, position, length), axis=1, keepdims=True)
        starts = jnp.where(here, first_one, starts)
    rows_ref[...] = starts
    for i in range(8):
        for j in range(8):
            table_ref[i, j] = 0
    for slot in range(6):
        row, block = SLOT_ROW[slot], SLOT_K[slot] ^ place
        source = jnp.where(place >= 2, 2, 0) if row == 0 else 1
        at = pl.ds(pl.multiple_of(block * size, size), size)
        first_row, second_row, third_row = rows_ref[0:1, at], rows_ref[1:2, at], rows_ref[2:3, at]
        mine = second_row if row else jnp.where(source == 2, third_row, first_row)
        start_ref[:, slot * size : (slot + 1) * size] = jnp.broadcast_to(mine, (8, size))
        table_ref[0, slot] = row
        table_ref[1, slot] = block
        table_ref[2, slot] = jnp.min(mine) // size
    for row in range(2):
        for block in range(4):
            slots = SLOT[row]
            near = block ^ place
            table_ref[3 + row, block] = jnp.where(
                near < 2,
                jnp.where(near == 0, slots[0], slots[1]),
                jnp.where(near == 2, slots[2], slots[3]),
            )


def prepare(doc_ids, place, vectors, size):
    ids = jnp.pad(jnp.transpose(doc_ids), ((0, 5), (0, 0)), constant_values=-1)
    vmem, smem = pl.BlockSpec(memory_space=pltpu.VMEM), pl.BlockSpec(memory_space=pltpu.SMEM)
    return pl.pallas_call(
        functools.partial(prepare_kernel, size),
        in_specs=[smem, vmem] + [vmem] * len(vectors),
        out_specs=[vmem, smem, vmem],
        out_shape=[
            jax.ShapeDtypeStruct((8, 6 * size), jnp.int32),
            jax.ShapeDtypeStruct((8, 8), jnp.int32),
            jax.ShapeDtypeStruct((8, vectors[0].shape[0]), F32),
        ],
        scratch_shapes=[pltpu.VMEM(ids.shape, jnp.int32)],
        cost_estimate=SMALL_COST,
        name="prepare",
    )(place.reshape(1).astype(jnp.int32), ids, *vectors)


GELU_C = 0.7978845608028654
GELU_A = 0.044715


def two_blocks(step, refs, held_ref):
    home_ref, near_ref, far_ref, far_near_ref = refs
    half = home_ref.shape[0] // 2

    @pl.when(step == 0)
    def _():
        held_ref[...] = home_ref[...]

    @pl.when(step == 1)
    def _():
        held_ref[...] = near_ref[...]

    @pl.when(step == 2)
    def _():
        held_ref[:half] = far_ref[:half]
        held_ref[half:] = far_near_ref[:half]

    if far_ref.shape[0] > half:

        @pl.when(step == 3)
        def _():
            held_ref[:half] = far_ref[half:]
            held_ref[half:] = far_near_ref[half:]

    return held_ref[...]


def other_core(ref, step):
    value = ref[...].astype(F32)
    half = value.shape[0] // 2
    turned = jnp.concatenate([value[half:], value[:half]], axis=0)
    return jnp.where(step == 2, turned, value)


def other_pair(step):
    return jnp.where(step == 2, 2, 1 - step)


def mlp_kernel(
    x0, x1, x2, x3, own_ref, other_ref, b0, b1, b2, b3, vec_ref, upb_own, upb_far, up_own, up_far, dn_own, dn_far,
    res_ref, mid_ref, act_ref, hg_ref, out_ref, give_ref, midin_ref, upbg_ref, bg_ref, held_ref,
):
    step = pl.program_id(0)
    proj_bias, gain, shift = vec_ref[0:1, :], vec_ref[1:2, :], vec_ref[2:3, :]
    residual = two_blocks(step, (x0, x1, x2, x3), held_ref).astype(F32) + own_ref[...].astype(F32)
    residual = residual + other_core(other_ref, step) + proj_bias
    res_ref[...] = residual
    centered = residual - jnp.mean(residual, axis=-1, keepdims=True)
    variance = jnp.mean(centered * centered, axis=-1, keepdims=True)
    mid = (centered * lax.rsqrt(variance + NORM_EPS) * gain + shift).astype(BF)
    mid_ref[...] = mid
    bg = two_blocks(step, (b0, b1, b2, b3), bg_ref)

    @pl.when(step == 0)
    def _():
        upbg_ref[...] = jnp.zeros_like(upbg_ref)

    out = None
    midin = None
    weights = ((up_own[...], dn_own[...], upb_own[...]), (up_far[0], dn_far[0], upb_far[...]))
    for part, (up_w, dn_w, up_bias) in enumerate(weights):
        hidden = nn(mid, up_w) + up_bias[1:2].astype(F32)
        act_grad = nt(bg, dn_w)
        square = hidden * hidden
        bent = jnp.tanh(GELU_C * (hidden + GELU_A * hidden * square))
        half = 0.5 * (1.0 + bent)
        act = (hidden * half).astype(BF)
        slope = half + 0.5 * hidden * (1.0 - bent * bent) * (GELU_C + 3.0 * GELU_C * GELU_A * square)
        grad = (act_grad * slope).astype(BF)
        act_ref[part] = act
        hg_ref[part] = grad
        upbg_ref[part : part + 1, :] += jnp.sum(grad.astype(F32), axis=0, keepdims=True)
        out_part = nn(act, dn_w)
        midin_part = nt(grad, up_w)
        out = out_part if out is None else out + out_part
        midin = midin_part if midin is None else midin + midin_part
    midin_ref[...] = midin.astype(BF)
    size = out.shape[0] // 2

    @pl.when(step == 0)
    def _():
        out_ref[: 2 * size] = out + residual + vec_ref[3:4, :]

    @pl.when(step == 1)
    def _():
        give_ref[: 2 * size] = out.astype(BF)

    @pl.when(step == 2)
    def _():
        out_ref[2 * size :] = (out + residual)[:size] + vec_ref[3:4, :]
        give_ref[2 * size :] = out[size:].astype(BF)


def mlp(tokens, own, other, bg, vectors, qkv_own, qkv_far, up_own, down_own, far, size):
    rows, width = own.shape
    inner = up_own.shape[1]
    block = pl.BlockSpec((2 * size, width), lambda i: (i, 0))
    wide = pl.BlockSpec((2, 2 * size, inner), lambda i: (0, i, 0))
    half = pl.BlockSpec((rows // 2, width), lambda i: (0, 0))
    return pl.pallas_call(
        mlp_kernel,
        grid=(3,),
        in_specs=[fixed((2 * size, width))] * 4
        + [
            block,
            pl.BlockSpec((2 * size, width), lambda i: (other_pair(i), 0)),
        ]
        + [fixed(value.shape) for value in bg]
        + [
            fixed((8, width)),
            pl.BlockSpec((16, width), lambda i: (9 * HEAD_DIM // 16, 0)),
            pl.BlockSpec((16, width), lambda i: (9 * HEAD_DIM // 16, 0)),
            fixed((width, inner)),
            pl.BlockSpec((1, width, inner), lambda i: (0, 0, 0), pipeline_mode=pl.Buffered(1)),
            fixed((inner, width)),
            pl.BlockSpec((1, inner, width), lambda i: (1, 0, 0), pipeline_mode=pl.Buffered(1)),
        ],
        out_specs=[
            block, block, wide, wide, half, half, block,
            pl.BlockSpec((8, inner), lambda i: (0, 0)),
            block,
        ],
        out_shape=[
            jax.ShapeDtypeStruct((rows, width), F32),
            jax.ShapeDtypeStruct((rows, width), BF),
            jax.ShapeDtypeStruct((2, rows, inner), BF),
            jax.ShapeDtypeStruct((2, rows, inner), BF),
            jax.ShapeDtypeStruct((rows // 2, width), F32),
            jax.ShapeDtypeStruct((rows // 2, width), BF),
            jax.ShapeDtypeStruct((rows, width), BF),
            jax.ShapeDtypeStruct((8, inner), F32),
            jax.ShapeDtypeStruct((rows, width), BF),
        ],
        scratch_shapes=[pltpu.VMEM((2 * size, width), BF)],
        compiler_params=params(),
        cost_estimate=SMALL_COST,
        name="mlp",
    )(*tokens, own, other, *bg, vectors, qkv_own, qkv_far, up_own, far, down_own, far)


def sum_tokens_kernel(rows, has_extra, left_ref, right_ref, *refs):
    left = left_ref[0] if len(left_ref.shape) == 3 else left_ref[...]
    right = right_ref[0] if len(right_ref.shape) == 3 else right_ref[...]
    total = tn(left, right)[:rows]
    if has_extra:
        total = total + refs[0][...].astype(F32)
    refs[-1][...] = total.astype(refs[-1].dtype)


def sum_tokens(
    left, right, extra=None, dtype=BF, part=0, rows=256, first=0, count=None, room=0, into=None
):
    block = 256
    count = count or left.shape[-1] // block
    tokens, width = right.shape[-2:]

    def spec(value, lanes, at):
        if value.ndim == 3:
            return pl.BlockSpec((1, tokens, lanes), lambda i: (part, 0, at(i)))
        return pl.BlockSpec((tokens, lanes), lambda i: (0, at(i)))

    base = 0 if into is None else into.shape[0] // rows - count
    out = pl.BlockSpec((rows, width), lambda i: (base + i, 0))
    specs = [spec(left, block, lambda i: first + i), spec(right, width, lambda i: 0)]
    operands = [left, right]
    if extra is not None:
        specs.append(out)
        operands.append(extra)
    aliases = {}
    shape = jax.ShapeDtypeStruct((count * rows + room, width), dtype)
    if into is not None:
        specs.append(pl.BlockSpec(memory_space=pl.ANY))
        aliases = {len(operands): 0}
        operands.append(into)
        shape = jax.ShapeDtypeStruct(into.shape, into.dtype)
    return pl.pallas_call(
        functools.partial(sum_tokens_kernel, rows, extra is not None),
        grid=(count,),
        in_specs=specs,
        out_specs=out,
        out_shape=shape,
        input_output_aliases=aliases,
        compiler_params=params(),
        cost_estimate=SMALL_COST,
        name="sum_tokens",
    )(*operands)


def project_kernel(heads_ref, far_w, own_w, out_ref):
    lanes = 4 * HEAD_DIM
    feats = far_w.shape[0]
    total = nn(heads_ref[:, :feats], far_w[...])
    out_ref[...] = (total + nn(heads_ref[:, lanes : lanes + feats], own_w[...])).astype(BF)


def project(heads, far_w, own_w, size):
    rows, lanes = heads.shape
    width = far_w.shape[1]
    return pl.pallas_call(
        project_kernel,
        grid=(3,),
        in_specs=[
            pl.BlockSpec((2 * size, lanes), lambda i: (i, 0)), fixed(far_w.shape), fixed(own_w.shape)
        ],
        out_specs=pl.BlockSpec((2 * size, width), lambda i: (i, 0)),
        out_shape=jax.ShapeDtypeStruct((rows, width), BF),
        compiler_params=params(),
        cost_estimate=SMALL_COST,
        name="project",
    )(heads, far_w, own_w)


def mid_backward_kernel(
    res_ref, own_ref, other_ref, bg_ref, vec_ref, far_w, own_w, rg_ref, ag_ref, atg_ref, sum_ref
):
    step = pl.program_id(0)
    gain = vec_ref[1:2, :]
    residual = res_ref[...]
    centered = residual - jnp.mean(residual, axis=-1, keepdims=True)
    rstd = lax.rsqrt(jnp.mean(centered * centered, axis=-1, keepdims=True) + NORM_EPS)
    xhat = centered * rstd
    mid_in = own_ref[...].astype(F32) + other_core(other_ref, step)
    gy = mid_in * gain
    through = rstd * (
        gy
        - jnp.mean(gy, axis=-1, keepdims=True)
        - xhat * jnp.mean(gy * xhat, axis=-1, keepdims=True)
    )
    total = bg_ref[...].astype(F32) + through
    low = total.astype(BF)
    ag_ref[...] = low
    lanes = 4 * HEAD_DIM
    feats = far_w.shape[0]
    for shard, w_ref in enumerate((far_w, own_w)):
        atg_ref[:, shard * lanes : shard * lanes + feats] = nt(low, w_ref[...]).astype(BF)
        atg_ref[:, shard * lanes + feats : (shard + 1) * lanes] = jnp.zeros(
            (low.shape[0], lanes - feats), BF
        )
    size = total.shape[0] // 2

    @pl.when(step == 0)
    def _():
        rg_ref[: 2 * size] = total
        sum_ref[...] = jnp.zeros_like(sum_ref)

    @pl.when(step == 2)
    def _():
        rg_ref[2 * size :] = total[:size]

    sum_ref[0:1, :] += jnp.sum(mid_in * xhat, axis=0, keepdims=True)
    sum_ref[1:2, :] += jnp.sum(mid_in, axis=0, keepdims=True)
    sum_ref[2:3, :] += jnp.sum(low.astype(F32), axis=0, keepdims=True)
    sum_ref[3:4, :] += jnp.sum(bg_ref[...].astype(F32), axis=0, keepdims=True)


def mid_backward(residual, own, other, bg, vectors, far_w, own_w, size):
    rows, width = own.shape
    lanes = 8 * HEAD_DIM
    block = pl.BlockSpec((2 * size, width), lambda i: (i, 0))
    return pl.pallas_call(
        mid_backward_kernel,
        grid=(3,),
        in_specs=[
            block,
            block,
            pl.BlockSpec((2 * size, width), lambda i: (other_pair(i), 0)),
            block,
            fixed((8, width)),
            fixed(far_w.shape),
            fixed(own_w.shape),
        ],
        out_specs=[
            pl.BlockSpec((rows // 2, width), lambda i: (0, 0)),
            block,
            pl.BlockSpec((2 * size, lanes), lambda i: (i, 0)),
            pl.BlockSpec((8, width), lambda i: (0, 0)),
        ],
        out_shape=[
            jax.ShapeDtypeStruct((rows // 2, width), F32),
            jax.ShapeDtypeStruct((rows, width), BF),
            jax.ShapeDtypeStruct((rows, lanes), BF),
            jax.ShapeDtypeStruct((8, width), F32),
        ],
        compiler_params=params(),
        cost_estimate=SMALL_COST,
        name="mid_backward",
    )(residual, own, other, bg, vectors, far_w, own_w)


def bias_row(ref):
    return ref[9 * HEAD_DIM : 9 * HEAD_DIM + 1].astype(F32)


def pad_heads(w_ref, padded_ref):
    lanes, feats = 4 * HEAD_DIM, 3 * HEAD_DIM
    for i in range(3):
        padded_ref[i * lanes : i * lanes + feats] = w_ref[i * feats : (i + 1) * feats]
        padded_ref[i * lanes + feats : (i + 1) * lanes] = jnp.zeros(
            (lanes - feats, w_ref.shape[1]), BF
        )


def first_kernel(x0, x1, x2, x3, vec_ref, far_ref, own_ref, normed_ref, qkv_ref, far_w, own_w, held_ref):
    @pl.when(pl.program_id(0) == 0)
    def _():
        pad_heads(far_ref, far_w)
        pad_heads(own_ref, own_w)

    stream = two_blocks(pl.program_id(0), (x0, x1, x2, x3), held_ref).astype(F32)
    centered = stream - jnp.mean(stream, axis=-1, keepdims=True)
    variance = jnp.mean(centered * centered, axis=-1, keepdims=True)
    normed = (
        centered * lax.rsqrt(variance + NORM_EPS) * vec_ref[4:5, :] + vec_ref[5:6, :]
    ).astype(BF)
    normed_ref[...] = normed
    third = far_w.shape[0]
    qkv_ref[:, :third] = (nt(normed, far_w[...]) + bias_row(far_ref)).astype(BF)
    qkv_ref[:, third:] = (nt(normed, own_w[...]) + bias_row(own_ref)).astype(BF)


def first(tokens, vectors, far, own, size):
    width = tokens[0].shape[1]
    rows = 8 * size
    outs = 6 * 4 * HEAD_DIM
    block = pl.BlockSpec((2 * size, width), lambda i: (i, 0))
    return pl.pallas_call(
        first_kernel,
        grid=(4,),
        in_specs=[fixed((2 * size, width))] * 4
        + [fixed((8, width)), fixed(far.shape), fixed(own.shape)],
        out_specs=[block, pl.BlockSpec((2 * size, outs), lambda i: (i, 0))],
        out_shape=[
            jax.ShapeDtypeStruct((rows, width), BF),
            jax.ShapeDtypeStruct((rows, outs), BF),
        ],
        scratch_shapes=[pltpu.VMEM((outs // 2, width), BF)] * 2
        + [pltpu.VMEM((2 * size, width), BF)],
        compiler_params=params(),
        cost_estimate=SMALL_COST,
        name="first_norm_qkv",
    )(*tokens, vectors, far, own)


def first_in_kernel(far_d, own_d, far_ref, own_w_ref, own_ref, give_ref, far_w, own_w):
    step = pl.program_id(0)
    half = far_d.shape[0] // 2

    @pl.when(step == 0)
    def _():
        pad_heads(far_ref, far_w)
        pad_heads(own_w_ref, own_w)

    total = (nn(far_d[...], far_w[...]) + nn(own_d[...], own_w[...])).astype(BF)

    @pl.when(step == 0)
    def _():
        own_ref[: 2 * half] = total

    @pl.when(step == 1)
    def _():
        give_ref[: 2 * half] = total

    @pl.when(step == 2)
    def _():
        own_ref[2 * half : 3 * half] = total[:half]
        give_ref[2 * half : 3 * half] = total[half:]

    @pl.when(step == 3)
    def _():
        own_ref[3 * half :] = total[:half]
        give_ref[3 * half :] = total[half:]


def first_in(far_grad, own_grad, far, own, size):
    rows, lanes = far_grad.shape
    width = far.shape[1]
    block = pl.BlockSpec((2 * size, lanes), lambda i: (i, 0))
    whole = pl.BlockSpec((rows // 2, width), lambda i: (0, 0))
    return pl.pallas_call(
        first_in_kernel,
        grid=(4,),
        in_specs=[block, block, fixed(far.shape), fixed(own.shape)],
        out_specs=[whole, whole],
        out_shape=[jax.ShapeDtypeStruct((rows // 2, width), BF)] * 2,
        scratch_shapes=[pltpu.VMEM((lanes, width), BF)] * 2,
        compiler_params=params(),
        cost_estimate=SMALL_COST,
        name="first_in",
    )(far_grad, own_grad, far, own)


def first_backward_kernel(home_ref, away_ref, own_ref, got_ref, rg_ref, vec_ref, *refs):
    extra_ref, (in_ref, sum_ref) = (refs[0] if len(refs) == 3 else None), refs[-2:]
    stream = jnp.where(pl.program_id(0) == 0, home_ref[...], away_ref[...]).astype(F32)
    centered = stream - jnp.mean(stream, axis=-1, keepdims=True)
    rstd = lax.rsqrt(jnp.mean(centered * centered, axis=-1, keepdims=True) + NORM_EPS)
    xhat = centered * rstd
    grad = own_ref[...].astype(F32) + got_ref[...].astype(F32)
    if extra_ref is not None:
        grad = grad + extra_ref[...].astype(F32)
    gy = grad * vec_ref[4:5, :]
    through = rstd * (
        gy
        - jnp.mean(gy, axis=-1, keepdims=True)
        - xhat * jnp.mean(gy * xhat, axis=-1, keepdims=True)
    )
    in_ref[...] = (rg_ref[...] + through).astype(BF)

    @pl.when(pl.program_id(0) == 0)
    def _():
        sum_ref[...] = jnp.zeros_like(sum_ref)

    sum_ref[0:1, :] += jnp.sum(grad * xhat, axis=0, keepdims=True)
    sum_ref[1:2, :] += jnp.sum(grad, axis=0, keepdims=True)


def first_backward(tokens, own, got, residual_grad, vectors, extra, size, owned):
    width = tokens[0].shape[1]
    stride = owned[1] - owned[0] if len(owned) > 1 else 1
    block = pl.BlockSpec((size, width), lambda i: (owned[0] + stride * i, 0))
    home = pl.BlockSpec((size, width), lambda i: (owned[0], 0))
    away = pl.BlockSpec((size, width), lambda i: (0, 0))
    more = () if extra is None else (extra,)
    return pl.pallas_call(
        first_backward_kernel,
        grid=(len(owned),),
        in_specs=[home, away, block, block, block, fixed((8, width))]
        + [pl.BlockSpec((size, width), lambda i: (0, 0))] * len(more),
        out_specs=[
            pl.BlockSpec((size, width), lambda i: (i, 0)),
            pl.BlockSpec((8, width), lambda i: (0, 0)),
        ],
        out_shape=[
            jax.ShapeDtypeStruct((len(owned) * size, width), BF),
            jax.ShapeDtypeStruct((8, width), F32),
        ],
        compiler_params=params(),
        cost_estimate=SMALL_COST,
        name="first_backward",
    )(tokens[0], tokens[2], own, got, residual_grad, vectors, *more)


def dp_partners(count, bit):
    return [(d, d ^ bit) for d in range(count)]


def dp_bits():
    return [1 << i for i in range(lax.axis_size("dp").bit_length() - 1)]


def dp_swap(value, bit):
    return lax.ppermute(value, "dp", dp_partners(lax.axis_size("dp"), bit))


def upper(bit):
    return (lax.axis_index("dp") & bit) != 0


def in_order(value, got, bit, axis=0):
    return jnp.where(
        upper(bit),
        jnp.concatenate([got, value], axis=axis),
        jnp.concatenate([value, got], axis=axis),
    )


def double(value, bit, axis=0):
    return in_order(value, dp_swap(value, bit), bit, axis)


def dp_part(value, axis):
    bits = dp_bits()
    place = sum(jnp.where(upper(bit), value.shape[axis] // (2 * bit), 0) for bit in bits)
    return lax.dynamic_slice_in_dim(value, place, value.shape[axis] // (2 * bits[-1]), axis)


def dp_stages():
    bits = dp_bits()
    return [bits[:1]] + [bits[i : i + 2] for i in range(1, len(bits), 2)]


def masks(bits):
    if len(bits) == 1:
        return [bits[0]]
    return [bits[1], bits[0], bits[0] | bits[1]]


def member(bits):
    place = jnp.where(upper(bits[-1]), 1, 0)
    return place if len(bits) == 1 else place + jnp.where(upper(bits[0]), 2, 0)


class Step:
    def whole(self, value):
        with jax.named_scope(self.name):
            kept, give = self.split(value)
            return self.join(kept, [dp_swap(x, mask) for x, mask in zip(give, self.masks)])


class Scatter(Step):
    def __init__(self, name, bits):
        self.name, self.masks = name, masks(bits)
        self.bits = bits

    def split(self, value):
        rows = value.shape[0] // (2 ** len(self.bits))
        mine = member(self.bits)
        pieces = [
            lax.dynamic_slice_in_dim(value, (mine ^ distance) * rows, rows, 0)
            for distance in range(2 ** len(self.bits))
        ]
        return pieces[0], [piece.astype(BF) for piece in pieces[1:]]

    def join(self, kept, got):
        total = kept.astype(F32)
        for piece in got:
            total = total + piece.astype(F32)
        return total


class Gather(Step):
    def __init__(self, name, bits):
        self.name, self.masks = name, masks(bits)
        self.bits = bits

    def split(self, value):
        value = value.astype(BF)
        return value, [value] * len(self.masks)

    def join(self, kept, got):
        if len(self.bits) == 1:
            return in_order(kept, got[0], self.bits[0])
        low = in_order(kept, got[0], self.bits[1])
        return in_order(low, in_order(got[1], got[2], self.bits[1]), self.bits[0])


class GatherAndAdd(Gather):
    def split(self, value):
        pieces, total = value
        rows = -(-total.shape[0] // 16) * 16
        total_low = jnp.pad(total.astype(BF), ((0, rows - total.shape[0]), (0, 0)))
        message = jnp.concatenate([total_low, pieces], axis=0)
        return (pieces, total), [message] * len(self.masks)

    def join(self, kept, got):
        pieces, total = kept
        rows = -(-total.shape[0] // 16) * 16
        for message in got:
            total = total + message[: total.shape[0]].astype(F32)
        return super().join(pieces, [message[rows:] for message in got]), total


def exchange(values, steps, *held):
    values, held = lax.optimization_barrier((tuple(values), held))
    halves = []
    for value, step in zip(values, steps):
        with jax.named_scope(step.name):
            halves.append(step.split(value))
    halves, held = lax.optimization_barrier((halves, held))
    joined = []
    for (kept, give), step in zip(halves, steps):
        with jax.named_scope(step.name):
            got = [dp_swap(piece, mask) for piece, mask in zip(give, step.masks)]
            joined.append((kept, got))

    def finish():
        out = []
        for (kept, got), step in zip(joined, steps):
            with jax.named_scope(step.name):
                out.append(step.join(kept, got))
        return out

    return finish, held


def sum_over_tensor(value):
    diagonal = ((0, 3), (1, 2), (2, 1), (3, 0))
    return value + core_swap(value) + x_swap(value) + lax.ppermute(value, "tensor", diagonal)


def after(value, *earlier):
    return lax.optimization_barrier((value,) + earlier)[0]


def body(
    hidden_in,
    doc_ids,
    first_gain,
    first_shift,
    qkv_weight,
    qv_bias,
    proj_weight,
    proj_bias,
    second_gain,
    second_shift,
    up_weight,
    up_bias,
    down_weight,
    down_bias,
    out_grad,
):
    size, rows_dev, width = hidden_in.shape
    length = doc_ids.shape[0]
    place = lax.axis_index("tensor")
    right = place >= 2
    feats = qkv_weight.shape[2]
    inner = up_weight.shape[1]

    def split_rows(value):
        first, mid, last = value[:, 0], value[:, 1], value[:, 2]
        return jnp.where(right, last, first), mid, jnp.where(right, first, last)

    def join_rows(main, mid, other):
        return jnp.stack(
            [jnp.where(right, other, main), mid, jnp.where(right, main, other)], axis=1
        )

    def head_sums(sums_own, sums_far, up_sums):
        slots = []
        for own, away in (
            (up_sums[0:1], up_sums[1:2]),
            (sums_own[:2, :feats].reshape(1, -1), sums_far[:2, :feats].reshape(1, -1)),
        ):
            index = lax.broadcasted_iota(jnp.int32, (4, own.shape[1]), 0)
            value = jnp.where(index == place, own, jnp.where(index == place ^ 2, away, 0.0))
            slots.append(value.reshape(-1, width))
        return slots

    pieces = jnp.stack([dp_part(up_weight, 0), dp_part(down_weight, 0)])
    with jax.named_scope("mlp_weights_x"):
        far_mlp = x_swap(pieces)

    space = jnp.zeros((4 * HEAD_DIM - feats,), BF)
    biases = jnp.concatenate(
        [qv_bias[0], space, jnp.zeros((4 * HEAD_DIM,), BF), qv_bias[1], space, up_bias]
    ).reshape(2, width)
    qkv_own = jnp.concatenate(
        [
            jnp.transpose(qkv_weight, (1, 2, 0)).reshape(3 * feats, width),
            jnp.pad(biases, ((0, 14), (0, 0))),
        ],
        axis=0,
    )

    main, mid, away = split_rows(hidden_in)
    home = jnp.concatenate([main, mid], axis=0)
    with jax.named_scope("tokens"):
        far = x_swap(jnp.concatenate([away, mid], axis=0))
        near = core_swap(home)
        far_near = core_swap(far)
    tokens = (home, near, far, far_near)

    with jax.named_scope("qkv_weights_x"):
        qkv_far = x_swap(qkv_own)
    local_ids = lax.dynamic_slice_in_dim(doc_ids, place * size, size, 0)
    cot = jnp.where((local_ids >= 0)[:, :, None], out_grad, jnp.zeros_like(out_grad))
    g_main, g_mid, g_away = split_rows(cot)
    g_home = jnp.concatenate([g_main, g_mid], axis=0)
    start_rows, table, vectors = prepare(
        doc_ids,
        place,
        (proj_bias, second_gain, second_shift, down_bias, first_gain, first_shift),
        size,
    )

    with jax.named_scope("mlp_weights_dp"):
        far_mlp, qkv_own, g_home, g_away = lax.optimization_barrier(
            (far_mlp, qkv_own, g_home, g_away)
        )
        for bit in reversed(dp_bits()[1:]):
            far_mlp, table, start_rows, vectors = lax.optimization_barrier(
                (double(far_mlp, bit, 1), table, start_rows, vectors)
            )
        far_mlp, held, tokens = lax.optimization_barrier((far_mlp, qkv_far, tokens))
        got_mlp = dp_swap(far_mlp, dp_bits()[0])

    with jax.named_scope("cotangent"):
        g_near = core_swap(g_home)
        g_far = x_swap(after(g_away, held))
        g_far_near = core_swap(g_far)

    with jax.named_scope("proj_weight_x"):
        proj_far = x_swap(after(proj_weight, held))
    normed, qkv = first(tokens, vectors, held, qkv_own, size)
    attended, lse = attend_forward(qkv, table, start_rows, size)
    attn_part = project(after(attended, g_far, g_near, got_mlp), proj_far, proj_weight, size)
    with jax.named_scope("attn_core"):
        attn_other = core_swap(attn_part)
    far_mlp = in_order(far_mlp, got_mlp, dp_bits()[0], 1)

    residual, normed_mid, act, hidden_grad, out_own, out_give, mid_part, up_sums, branch_grad = mlp(
        tokens, attn_part, attn_other, (g_home, g_near, g_far, g_far_near), vectors, qkv_own, held,
        up_weight, down_weight, far_mlp, size,
    )

    stages = dp_stages()
    first_stage, high_stages = stages[0], stages[1:]

    with jax.named_scope("mid_core"):
        mid_other = core_swap(mid_part)
    down_away = sum_tokens(act, branch_grad, part=1)
    with jax.named_scope("down_grad_x"):
        down_got = x_swap(down_away)
    residual_grad, attn_grad, attended_grad, mid_sums = mid_backward(
        after(residual, down_away), mid_part, mid_other, branch_grad, vectors,
        proj_far, proj_weight, size,
    )

    act, hidden_grad, out_own, out_give, attended_grad = lax.optimization_barrier(
        (act, hidden_grad, out_own, out_give, attended_grad)
    )
    up_away = sum_tokens(normed_mid, hidden_grad, part=1, room=feats)
    up_away = sum_tokens(attended, attn_grad, rows=feats, count=1, into=up_away)
    with jax.named_scope("up_proj_grad_x"):
        up_got = x_swap(up_away)
    d_far, sums_far = attend_backward(
        qkv, attended, after(attended_grad, up_away), lse, table, start_rows, size, 0
    )
    qkv_away = sum_tokens(d_far, normed, rows=feats)
    with jax.named_scope("qkv_grad_x"):
        qkv_got = x_swap(qkv_away)
    down = sum_tokens(act, after(branch_grad, qkv_away), down_got, F32)
    with jax.named_scope("block_out"):
        out_got = core_swap(after(out_give, down))
    d_own, sums_own = attend_backward(
        qkv, attended, after(attended_grad, down), lse, table, start_rows, size, 1
    )
    d, u, t, n = "down_grad_dp", "up_proj_grad_dp", "qkv_grad_dp", "small_sums"
    finish, (attended_grad,) = exchange([down], [Scatter(d, first_stage)], attended_grad)
    d_own, sums_own = attend_backward(
        qkv, attended, attended_grad, lse, table, start_rows, size, 1
    )
    (down,) = finish()
    d_own, down, up_got, out_got = lax.optimization_barrier((d_own, down, up_got, out_got))

    singles = [[bit] for bit in dp_bits()[1:]]
    finish, (hidden_grad, up_got) = exchange(
        [down], [Scatter(d, singles[0])], hidden_grad, up_got
    )
    up = sum_tokens(normed_mid, hidden_grad, up_got, F32, room=feats)
    up = sum_tokens(attended, attn_grad, up_got, F32, rows=feats, first=1, count=1, into=up)
    with jax.named_scope("block_out"):
        out_full = (out_own + out_got.astype(F32)).astype(BF)
    (down,) = finish()
    up, down, out_full = lax.optimization_barrier((up, down, out_full))

    finish, (d_own, qkv_got, out_full) = exchange(
        [up, down], [Scatter(u, first_stage), Scatter(d, singles[1])], d_own, qkv_got, out_full
    )
    tail = sum_tokens(d_own, normed, qkv_got, F32, rows=feats)
    own_in, give_in = first_in(d_far, after(d_own, tail), held, qkv_own, size)
    up, down = finish()
    for bits in singles[2:]:
        finish, _ = exchange([down], [Scatter(d, bits)])
        (down,) = finish()

    up_gathers = [Gather(u, bits) for bits in reversed(singles)]
    down_gathers = [Gather(d, bits) for bits in reversed(singles)]
    for step in down_gathers[:-2]:
        finish, _ = exchange([down], [step])
        (down,) = finish()
    steps = [Scatter(t, first_stage), Scatter(u, high_stages[0]), down_gathers[-2]]
    finish, (own_in, give_in, out_full) = exchange(
        [tail, up, down], steps, own_in, give_in, out_full
    )
    with jax.named_scope("first_core"):
        got_in = core_swap(give_in)
    mid_sum = (own_in[3 * size :].astype(F32) + got_in[3 * size :].astype(F32)).astype(BF)
    with jax.named_scope("first_mid_x"):
        extra = x_swap(mid_sum)
    in_main, sums_main = first_backward(
        tokens, own_in, got_in, residual_grad, vectors, None, size, (0, 2)
    )
    tail, up, down = finish()
    for bits in high_stages[1:]:
        finish, _ = exchange([up], [Scatter(u, bits)])
        (up,) = finish()
    for step in up_gathers[:-2]:
        finish, _ = exchange([up], [step])
        (up,) = finish()

    steps = [Scatter(t, high_stages[0]), up_gathers[-2], down_gathers[-1]]
    finish, (in_main, extra, out_full) = exchange(
        [tail, up, down], steps, in_main, extra, out_full
    )
    with jax.named_scope("in_grad_x"):
        in_away = x_swap(in_main[size:])
    in_mid, sums_mid = first_backward(
        tokens, own_in, got_in, residual_grad, vectors, extra, size, (1,)
    )
    tail, up, down = finish()
    small = jnp.concatenate(
        [(sums_main + sums_mid)[:2], 0.5 * mid_sums[:4], *head_sums(sums_own, sums_far, up_sums)],
        axis=0,
    )
    for bits in high_stages[1:]:
        finish, _ = exchange([tail], [Scatter(t, bits)])
        (tail,) = finish()

    finish, (tail, up, small, in_away, out_full) = exchange(
        [down], [Gather(d, first_stage)], tail, up, small, in_away, out_full
    )
    with jax.named_scope("small_sums"):
        small = sum_over_tensor(small)
    with jax.named_scope("block_out"):
        out_away = x_swap(out_full[2 * size :])
    (down,) = finish()
    steps = [GatherAndAdd(t, first_stage), up_gathers[-1]]
    finish, (down, out_away) = exchange([(tail.astype(BF), small), up], steps, down, out_away)
    (tail, small), up = finish()
    last = high_stages[-1] if len(high_stages[-1]) == 2 else high_stages[-2]
    rest = [bits for bits in high_stages if bits is not last]
    for bits in reversed(rest):
        finish, _ = exchange([(tail, small)], [GatherAndAdd(t, bits)])
        ((tail, small),) = finish()
    steps = [GatherAndAdd(t, last), Gather(u, first_stage)]
    finish, _ = exchange([(tail, small), up], steps)
    (tail, small), up = finish()
    tail = tail.reshape(-1, 2, tail.shape[0] // (2 ** len(dp_bits())), width)
    tail = jnp.transpose(tail, (1, 0, 2, 3)).reshape(3 * feats, width)

    block_out = join_rows(out_full[:size], out_full[size : 2 * size], out_away)
    in_grad = join_rows(in_main[:size], in_mid, in_away)

    up_bias_grad = lax.dynamic_slice_in_dim(small, 6 + place, 1, 0)[0]
    qv_all = small[10:].reshape(4, 2, feats)
    qv_bias_grad = lax.dynamic_slice_in_dim(qv_all, place, 1, 0)[0]

    qkv_weight_grad = jnp.transpose(
        tail.reshape(3, feats, width), (2, 0, 1)
    ).astype(F32)
    return (
        block_out,
        in_grad,
        small[0],
        small[1],
        qkv_weight_grad,
        qv_bias_grad,
        up[inner:].astype(F32),
        small[4],
        small[2],
        small[3],
        up[:inner].astype(F32),
        up_bias_grad,
        down.astype(F32),
        small[5],
    )


def solution(mesh):
    in_specs = (
        P("tensor", "dp", None),
        P(None, "dp"),
        P(),
        P(),
        P(None, None, "tensor"),
        P(None, "tensor"),
        P("tensor", None),
        P(),
        P(),
        P(),
        P(None, "tensor"),
        P("tensor"),
        P("tensor", None),
        P(),
        P("tensor", "dp", None),
    )
    out_specs = (
        P("tensor", "dp", None),
        P("tensor", "dp", None),
        P(),
        P(),
        P(None, None, "tensor"),
        P(None, "tensor"),
        P("tensor", None),
        P(),
        P(),
        P(),
        P(None, "tensor"),
        P("tensor"),
        P("tensor", None),
        P(),
    )
    return jax.shard_map(body, mesh=mesh, in_specs=in_specs, out_specs=out_specs, check_vma=False)
```

```python
import functools

import jax
import jax.numpy as jnp
from jax import lax
from jax.experimental import pallas as pl
from jax.experimental.pallas import tpu as pltpu
from jax.sharding import PartitionSpec as P

HEAD_DIM = 64
NORM_EPS = 1e-05
MASKED = -1e30
BF = jnp.bfloat16
F32 = jnp.float32
VMEM_LIMIT = 56 * 1024 * 1024

SLOT = ((0, 2, 4, 5), (1, 3, 6, 7))
SLOT_ROW = (0, 1, 0, 1, 0, 0)
SLOT_K = (0, 0, 1, 1, 2, 3)
X_SWAP = ((0, 2), (1, 3), (2, 0), (3, 1))
CORE_SWAP = ((0, 1), (1, 0), (2, 3), (3, 2))


def x_swap(value):
    return lax.ppermute(value, "tensor", X_SWAP)


def core_swap(value):
    return lax.ppermute(value, "tensor", CORE_SWAP)


def params(semantics=None):
    return pltpu.CompilerParams(vmem_limit_bytes=VMEM_LIMIT)


def fixed(shape):
    return pl.BlockSpec(shape, lambda *ids: (0,) * len(shape), pipeline_mode=pl.Buffered(1))


def nt(left, right):
    return lax.dot_general(left, right, (((1,), (1,)), ((), ())), preferred_element_type=F32)


def nn(left, right):
    return lax.dot_general(left, right, (((1,), (0,)), ((), ())), preferred_element_type=F32)


def tn(left, right):
    return lax.dot_general(left, right, (((0,), (0,)), ((), ())), preferred_element_type=F32)


SMALL_COST = pl.CostEstimate(flops=1, bytes_accessed=1, transcendentals=0)


def key_mask(start_row, key_first, keys, size, diagonal):
    key = lax.broadcasted_iota(jnp.int32, (keys, size), 0)
    mask = key >= start_row - key_first
    if diagonal:
        mask = mask & (key <= lax.broadcasted_iota(jnp.int32, (keys, size), 1))
    return mask


KEYS = 128


def key_rows(table, row, first, size):
    return table[3 + row, first // size] * size + first % size


def head_rows(size):
    lane = lax.broadcasted_iota(jnp.int32, (size, 2 * HEAD_DIM), 1)

    def select(value):
        zero = jnp.zeros((size, 2 * HEAD_DIM), value.dtype)
        pair = value[:, : 2 * HEAD_DIM]
        return (
            jnp.where(lane < HEAD_DIM, pair, zero),
            jnp.where(lane < HEAD_DIM, zero, pair),
            value[:, 2 * HEAD_DIM :],
        )

    return select


def pair_lanes(value, head):
    first = 2 * HEAD_DIM * (head // 2)
    return value[:, first : first + 2 * HEAD_DIM]


def attend_forward_kernel(size, table, start_ref, q_ref, k_ref, v_ref, out_ref, lse_ref):
    slot = pl.program_id(1)
    row, block, low = table[0, slot], table[1, slot], table[2, slot]
    start_row = start_ref[0:1, :]
    select = head_rows(size)
    heads = select(q_ref[...] * jnp.asarray(HEAD_DIM**-0.5, BF))

    def load(first, keys):
        at = pl.multiple_of(key_rows(table, row, first, size), keys)
        return k_ref[pl.ds(at, keys), :], jnp.transpose(v_ref[pl.ds(at, keys), :])

    key, value_t = load(block * size, size)
    mask = key_mask(start_row, block * size, size, size, True)
    all_scores = [nt(pair_lanes(key, head), heads[head]) for head in range(3)]
    carry = []
    for head in range(3):
        scores = jnp.where(mask, all_scores[head], MASKED)
        top = jnp.max(scores, axis=0, keepdims=True)
        weight = jnp.exp(scores - top)
        total = jnp.sum(weight, axis=0, keepdims=True)
        acc = nn(value_t[head * HEAD_DIM : (head + 1) * HEAD_DIM], weight.astype(BF))
        carry += [top, total, acc]

    def earlier(step, carry):
        first = block * size - (step + 1) * KEYS
        key, value_t = load(first, KEYS)
        mask = key_mask(start_row, first, KEYS, size, False)
        all_scores = [nt(pair_lanes(key, head), heads[head]) for head in range(3)]
        new = []
        for head in range(3):
            top, total, acc = carry[3 * head : 3 * head + 3]
            scores = jnp.where(mask, all_scores[head], MASKED)
            higher = jnp.maximum(top, jnp.max(scores, axis=0, keepdims=True))
            shrink = jnp.exp(top - higher)
            weight = jnp.exp(scores - higher)
            total = total * shrink + jnp.sum(weight, axis=0, keepdims=True)
            acc = acc * shrink + nn(
                value_t[head * HEAD_DIM : (head + 1) * HEAD_DIM], weight.astype(BF)
            )
            new += [higher, total, acc]
        return tuple(new)

    carry = lax.fori_loop(0, block * (size // KEYS) - low, earlier, tuple(carry))
    parts = [carry[3 * head + 2] / carry[3 * head + 1] for head in range(3)]
    parts.append(jnp.zeros_like(parts[0]))
    out_ref[...] = jnp.transpose(jnp.concatenate(parts, axis=0)).astype(BF)
    for head in range(3):
        lse_ref[head : head + 1, :] = carry[3 * head] + jnp.log(carry[3 * head + 1])


def attend_forward(qkv, table, starts, size):
    width = 4 * HEAD_DIM
    tokens = qkv.shape[0]
    return pl.pallas_call(
        functools.partial(attend_forward_kernel, size),
        grid_spec=pltpu.PrefetchScalarGridSpec(
            num_scalar_prefetch=1,
            grid=(2, 6),
            in_specs=[
                pl.BlockSpec((8, size), lambda p, s, *_: (0, s)),
                pl.BlockSpec((size, width), lambda p, s, *_: (s, 3 * p)),
                pl.BlockSpec((tokens, width), lambda p, s, *_: (0, 3 * p + 1)),
                pl.BlockSpec((tokens, width), lambda p, s, *_: (0, 3 * p + 2)),
            ],
            out_specs=[
                pl.BlockSpec((size, width), lambda p, s, *_: (s, p)),
                pl.BlockSpec((8, size), lambda p, s, *_: (p, s)),
            ],
        ),
        out_shape=[
            jax.ShapeDtypeStruct((6 * size, 2 * width), BF),
            jax.ShapeDtypeStruct((16, 6 * size), F32),
        ],
        compiler_params=params(),
        cost_estimate=SMALL_COST,
        name="attend_forward",
    )(table, starts, qkv, qkv, qkv)


def attend_backward_kernel(
    size, table, start_ref, q_ref, k_ref, v_ref, out_ref, grad_ref, lse_ref,
    d_ref, sum_ref, dk_acc, dv_acc,
):
    slot = pl.program_id(0)
    width = 4 * HEAD_DIM
    row, block, low = table[0, slot], table[1, slot], table[2, slot]
    start_row = start_ref[0:1, :]
    select = head_rows(size)
    q_heads = select(q_ref[...] * jnp.asarray(HEAD_DIM**-0.5, BF))
    grad = grad_ref[...]
    g_heads = select(grad)
    products = jnp.transpose(grad.astype(F32) * out_ref[...].astype(F32))
    deltas = [
        jnp.sum(products[head * HEAD_DIM : (head + 1) * HEAD_DIM], axis=0, keepdims=True)
        for head in range(3)
    ]

    @pl.when(slot == 0)
    def _():
        dk_acc[...] = jnp.zeros_like(dk_acc)
        dv_acc[...] = jnp.zeros_like(dv_acc)
        sum_ref[...] = jnp.zeros_like(sum_ref)

    def one_block(first, keys, diagonal):
        at = pl.multiple_of(key_rows(table, row, first, size), keys)
        key, value = k_ref[pl.ds(at, keys), :], v_ref[pl.ds(at, keys), :]
        key_t = jnp.transpose(key)
        mask = key_mask(start_row, first, keys, size, diagonal)
        all_scores = [nt(pair_lanes(key, head), q_heads[head]) for head in range(3)]
        all_grads = [nt(pair_lanes(value, head), g_heads[head]) for head in range(3)]
        dq_parts, dk_parts, dv_parts = [], [], []
        for head in range(3):
            scores = jnp.where(mask, all_scores[head], MASKED)
            prob = jnp.exp(scores - lse_ref[head : head + 1, :])
            score_grad = (prob * (all_grads[head] - deltas[head])).astype(BF)
            dk_parts.append(nn(score_grad, q_heads[head]))
            dv_parts.append(nn(prob.astype(BF), g_heads[head]))
            dq_parts.append(nn(key_t[head * HEAD_DIM : (head + 1) * HEAD_DIM], score_grad))
        dk_acc[pl.ds(at, keys), : width // 2] += dk_parts[0] + dk_parts[1]
        dk_acc[pl.ds(at, keys), width // 2 :] += dk_parts[2]
        dv_acc[pl.ds(at, keys), : width // 2] += dv_parts[0] + dv_parts[1]
        dv_acc[pl.ds(at, keys), width // 2 :] += dv_parts[2]
        return jnp.concatenate(dq_parts, axis=0)

    dq_t = one_block(block * size, size, True)
    dq_t = lax.fori_loop(
        0,
        block * (size // KEYS) - low,
        lambda step, acc: acc + one_block(block * size - (step + 1) * KEYS, KEYS, False),
        dq_t,
    )
    dq_t = jnp.concatenate([dq_t, jnp.zeros((HEAD_DIM, size), F32)], axis=0)
    dq = (jnp.transpose(dq_t) * HEAD_DIM**-0.5).astype(BF)
    d_ref[pl.ds(pl.multiple_of(slot * size, size), size), :width] = dq
    sum_ref[0:1, :] += jnp.sum(dq.astype(F32), axis=0, keepdims=True)

    @pl.when(slot == pl.num_programs(0) - 1)
    def _():
        d_ref[6 * size :, :width] = jnp.zeros((2 * size, width), BF)
        d_ref[:, width : 2 * width] = dk_acc[...].astype(BF)
        dv = dv_acc[...].astype(BF)
        d_ref[:, 2 * width :] = dv
        sum_ref[1:2, :] = jnp.sum(dv.astype(F32), axis=0, keepdims=True)


def attend_backward(qkv, attended, grad, lse, table, starts, size, shard):
    tokens = qkv.shape[0]
    width = 4 * HEAD_DIM
    block = pl.BlockSpec((size, width), lambda s, *_: (s, shard))
    return pl.pallas_call(
        functools.partial(attend_backward_kernel, size),
        grid_spec=pltpu.PrefetchScalarGridSpec(
            num_scalar_prefetch=1,
            grid=(6,),
            in_specs=[
                pl.BlockSpec((8, size), lambda s, *_: (0, s)),
                pl.BlockSpec((size, width), lambda s, *_: (s, 3 * shard)),
                pl.BlockSpec((tokens, width), lambda s, *_: (0, 3 * shard + 1)),
                pl.BlockSpec((tokens, width), lambda s, *_: (0, 3 * shard + 2)),
                block,
                block,
                pl.BlockSpec((8, size), lambda s, *_: (shard, s)),
            ],
            out_specs=[
                pl.BlockSpec((tokens, 3 * width), lambda s, *_: (0, 0)),
                pl.BlockSpec((8, width), lambda s, *_: (0, 0)),
            ],
            scratch_shapes=[pltpu.VMEM((tokens, width), F32), pltpu.VMEM((tokens, width), F32)],
        ),
        out_shape=[
            jax.ShapeDtypeStruct((tokens, 3 * width), BF),
            jax.ShapeDtypeStruct((8, width), F32),
        ],
        compiler_params=params(),
        cost_estimate=SMALL_COST,
        name="attend_backward",
    )(table, starts, qkv, qkv, qkv, attended, grad, lse)


def prepare_kernel(size, place_ref, ids_ref, *refs):
    vectors, (start_ref, table_ref, vec_ref, rows_ref) = refs[:-4], refs[-4:]
    for i, ref in enumerate(vectors):
        vec_ref[i : i + 1, :] = ref[...].astype(F32).reshape(1, -1)
    vec_ref[len(vectors) :, :] = jnp.zeros((8 - len(vectors), vec_ref.shape[1]), F32)
    place = place_ref[0]
    ids = ids_ref[...]
    length = ids.shape[1]
    position = lax.broadcasted_iota(jnp.int32, ids.shape, 1)
    starts = position
    for doc in range(8):
        here = ids == doc
        first_one = jnp.min(jnp.where(here, position, length), axis=1, keepdims=True)
        starts = jnp.where(here, first_one, starts)
    rows_ref[...] = starts
    for i in range(8):
        for j in range(8):
            table_ref[i, j] = 0
    for slot in range(6):
        row, block = SLOT_ROW[slot], SLOT_K[slot] ^ place
        source = jnp.where(place >= 2, 2, 0) if row == 0 else 1
        at = pl.ds(pl.multiple_of(block * size, size), size)
        first_row, second_row, third_row = rows_ref[0:1, at], rows_ref[1:2, at], rows_ref[2:3, at]
        mine = second_row if row else jnp.where(source == 2, third_row, first_row)
        start_ref[:, slot * size : (slot + 1) * size] = jnp.broadcast_to(mine, (8, size))
        table_ref[0, slot] = row
        table_ref[1, slot] = block
        table_ref[2, slot] = jnp.min(mine) // KEYS
    for row in range(2):
        for block in range(4):
            slots = SLOT[row]
            near = block ^ place
            table_ref[3 + row, block] = jnp.where(
                near < 2,
                jnp.where(near == 0, slots[0], slots[1]),
                jnp.where(near == 2, slots[2], slots[3]),
            )


def prepare(doc_ids, place, vectors, size):
    ids = jnp.pad(jnp.transpose(doc_ids), ((0, 5), (0, 0)), constant_values=-1)
    vmem, smem = pl.BlockSpec(memory_space=pltpu.VMEM), pl.BlockSpec(memory_space=pltpu.SMEM)
    return pl.pallas_call(
        functools.partial(prepare_kernel, size),
        in_specs=[smem, vmem] + [vmem] * len(vectors),
        out_specs=[vmem, smem, vmem],
        out_shape=[
            jax.ShapeDtypeStruct((8, 6 * size), jnp.int32),
            jax.ShapeDtypeStruct((8, 8), jnp.int32),
            jax.ShapeDtypeStruct((8, vectors[0].shape[0]), F32),
        ],
        scratch_shapes=[pltpu.VMEM(ids.shape, jnp.int32)],
        cost_estimate=SMALL_COST,
        name="prepare",
    )(place.reshape(1).astype(jnp.int32), ids, *vectors)


GELU_C = 0.7978845608028654
GELU_A = 0.044715


def two_blocks(step, refs, held_ref):
    home_ref, near_ref, far_ref, far_near_ref = refs
    half = home_ref.shape[0] // 2

    @pl.when(step == 0)
    def _():
        held_ref[...] = home_ref[...]

    @pl.when(step == 1)
    def _():
        held_ref[...] = near_ref[...]

    @pl.when(step == 2)
    def _():
        held_ref[:half] = far_ref[:half]
        held_ref[half:] = far_near_ref[:half]

    if far_ref.shape[0] > half:

        @pl.when(step == 3)
        def _():
            held_ref[:half] = far_ref[half:]
            held_ref[half:] = far_near_ref[half:]

    return held_ref[...]


def other_core(ref, step):
    value = ref[...].astype(F32)
    half = value.shape[0] // 2
    turned = jnp.concatenate([value[half:], value[:half]], axis=0)
    return jnp.where(step == 2, turned, value)


def other_pair(step):
    return jnp.where(step == 2, 2, 1 - step)


def mlp_kernel(
    x0, x1, x2, x3, own_ref, other_ref, b0, b1, b2, b3, vec_ref, upb_own, upb_far, up_own, up_far, dn_own, dn_far,
    rstd_ref, mid_ref, act_ref, hg_ref, out_ref, give_ref, midin_ref, upbg_ref, bg_ref, held_ref,
):
    step = pl.program_id(0)
    proj_bias, gain, shift = vec_ref[0:1, :], vec_ref[1:2, :], vec_ref[2:3, :]
    residual = two_blocks(step, (x0, x1, x2, x3), held_ref).astype(F32) + own_ref[...].astype(F32)
    residual = residual + other_core(other_ref, step) + proj_bias
    centered = residual - jnp.mean(residual, axis=-1, keepdims=True)
    variance = jnp.mean(centered * centered, axis=-1, keepdims=True)
    rstd = lax.rsqrt(variance + NORM_EPS)
    rstd_ref[...] = jnp.broadcast_to(rstd, rstd_ref.shape)
    mid = (centered * rstd * gain + shift).astype(BF)
    mid_ref[...] = mid
    bg = two_blocks(step, (b0, b1, b2, b3), bg_ref)

    @pl.when(step == 0)
    def _():
        upbg_ref[...] = jnp.zeros_like(upbg_ref)

    out = None
    midin = None
    weights = ((up_own[...], dn_own[...], upb_own[...]), (up_far[0], dn_far[0], upb_far[...]))
    for part, (up_w, dn_w, up_bias) in enumerate(weights):
        hidden = nn(mid, up_w) + up_bias[1:2].astype(F32)
        act_grad = nt(bg, dn_w)
        square = hidden * hidden
        bent = jnp.tanh(GELU_C * (hidden + GELU_A * hidden * square))
        half = 0.5 * (1.0 + bent)
        act = (hidden * half).astype(BF)
        slope = half + 0.5 * hidden * (1.0 - bent * bent) * (GELU_C + 3.0 * GELU_C * GELU_A * square)
        grad = (act_grad * slope).astype(BF)
        act_ref[part] = act
        hg_ref[part] = grad
        upbg_ref[part : part + 1, :] += jnp.sum(grad.astype(F32), axis=0, keepdims=True)
        out_part = nn(act, dn_w)
        midin_part = nt(grad, up_w)
        out = out_part if out is None else out + out_part
        midin = midin_part if midin is None else midin + midin_part
    midin_ref[...] = midin.astype(BF)
    size = out.shape[0] // 2

    @pl.when(step == 0)
    def _():
        out_ref[: 2 * size] = out + residual + vec_ref[3:4, :]

    @pl.when(step == 1)
    def _():
        give_ref[: 2 * size] = out.astype(BF)

    @pl.when(step == 2)
    def _():
        out_ref[2 * size :] = (out + residual)[:size] + vec_ref[3:4, :]
        give_ref[2 * size :] = out[size:].astype(BF)


def mlp(tokens, own, other, bg, vectors, qkv_own, qkv_far, up_own, down_own, far, size):
    rows, width = own.shape
    inner = up_own.shape[1]
    block = pl.BlockSpec((2 * size, width), lambda i: (i, 0))
    wide = pl.BlockSpec((2, 2 * size, inner), lambda i: (0, i, 0))
    half = pl.BlockSpec((rows // 2, width), lambda i: (0, 0))
    return pl.pallas_call(
        mlp_kernel,
        grid=(3,),
        in_specs=[fixed((2 * size, width))] * 4
        + [
            block,
            pl.BlockSpec((2 * size, width), lambda i: (other_pair(i), 0)),
        ]
        + [fixed(value.shape) for value in bg]
        + [
            fixed((8, width)),
            pl.BlockSpec((16, width), lambda i: (9 * HEAD_DIM // 16, 0)),
            pl.BlockSpec((16, width), lambda i: (9 * HEAD_DIM // 16, 0)),
            fixed((width, inner)),
            pl.BlockSpec((1, width, inner), lambda i: (0, 0, 0), pipeline_mode=pl.Buffered(1)),
            fixed((inner, width)),
            pl.BlockSpec((1, inner, width), lambda i: (1, 0, 0), pipeline_mode=pl.Buffered(1)),
        ],
        out_specs=[
            pl.BlockSpec((2 * size, 128), lambda i: (i, 0)),
            block, wide, wide, half, half, block,
            pl.BlockSpec((8, inner), lambda i: (0, 0)),
            block,
        ],
        out_shape=[
            jax.ShapeDtypeStruct((rows, 128), F32),
            jax.ShapeDtypeStruct((rows, width), BF),
            jax.ShapeDtypeStruct((2, rows, inner), BF),
            jax.ShapeDtypeStruct((2, rows, inner), BF),
            jax.ShapeDtypeStruct((rows // 2, width), F32),
            jax.ShapeDtypeStruct((rows // 2, width), BF),
            jax.ShapeDtypeStruct((rows, width), BF),
            jax.ShapeDtypeStruct((8, inner), F32),
            jax.ShapeDtypeStruct((rows, width), BF),
        ],
        scratch_shapes=[pltpu.VMEM((2 * size, width), BF)],
        compiler_params=params(),
        cost_estimate=SMALL_COST,
        name="mlp",
    )(*tokens, own, other, *bg, vectors, qkv_own, qkv_far, up_own, far, down_own, far)


def sum_tokens_kernel(rows, has_extra, left_ref, right_ref, *refs):
    left = left_ref[0] if len(left_ref.shape) == 3 else left_ref[...]
    right = right_ref[0] if len(right_ref.shape) == 3 else right_ref[...]
    total = tn(left, right)[:rows]
    if has_extra:
        total = total + refs[0][...].astype(F32)
    refs[-1][...] = total.astype(refs[-1].dtype)


def sum_tokens(
    left, right, extra=None, dtype=BF, part=0, parts=1, rows=256, first=0, count=None, room=0, into=None
):
    block = 256
    blocks = left.shape[-1] // block
    count = count or parts * blocks
    tokens, width = right.shape[-2:]

    def spec(value, lanes, at):
        if value.ndim == 3 and parts > 1:
            return pl.BlockSpec((1, tokens, lanes), lambda i: (i // blocks, 0, i % blocks))
        if value.ndim == 3:
            return pl.BlockSpec((1, tokens, lanes), lambda i: (part, 0, at(i)))
        return pl.BlockSpec((tokens, lanes), lambda i: (0, at(i)))

    base = 0 if into is None else into.shape[0] // rows - count
    out = pl.BlockSpec((rows, width), lambda i: (base + i, 0))
    specs = [spec(left, block, lambda i: first + i), spec(right, width, lambda i: 0)]
    operands = [left, right]
    if extra is not None:
        specs.append(pl.BlockSpec((rows, width), lambda i: (i, 0)))
        operands.append(extra)
    aliases = {}
    shape = jax.ShapeDtypeStruct((count * rows + room, width), dtype)
    if into is not None:
        specs.append(pl.BlockSpec(memory_space=pl.ANY))
        aliases = {len(operands): 0}
        operands.append(into)
        shape = jax.ShapeDtypeStruct(into.shape, into.dtype)
    return pl.pallas_call(
        functools.partial(sum_tokens_kernel, rows, extra is not None),
        grid=(count,),
        in_specs=specs,
        out_specs=out,
        out_shape=shape,
        input_output_aliases=aliases,
        compiler_params=params(),
        cost_estimate=SMALL_COST,
        name="sum_tokens",
    )(*operands)


def project_kernel(heads_ref, far_w, own_w, out_ref):
    lanes = 4 * HEAD_DIM
    feats = far_w.shape[0]
    total = nn(heads_ref[:, :feats], far_w[...])
    out_ref[...] = (total + nn(heads_ref[:, lanes : lanes + feats], own_w[...])).astype(BF)


def project(heads, far_w, own_w, size):
    rows, lanes = heads.shape
    width = far_w.shape[1]
    return pl.pallas_call(
        project_kernel,
        grid=(3,),
        in_specs=[
            pl.BlockSpec((2 * size, lanes), lambda i: (i, 0)), fixed(far_w.shape), fixed(own_w.shape)
        ],
        out_specs=pl.BlockSpec((2 * size, width), lambda i: (i, 0)),
        out_shape=jax.ShapeDtypeStruct((rows, width), BF),
        compiler_params=params(),
        cost_estimate=SMALL_COST,
        name="project",
    )(heads, far_w, own_w)


def mid_backward_kernel(
    mid_ref, rstd_ref, own_ref, other_ref, bg_ref, vec_ref, far_w, own_w,
    rg_ref, ag_ref, atg_ref, sum_ref,
):
    step = pl.program_id(0)
    gain, shift = vec_ref[1:2, :], vec_ref[2:3, :]
    rstd = rstd_ref[:, 0:1]
    xhat = (mid_ref[...].astype(F32) - shift) * (1.0 / gain)
    mid_in = own_ref[...].astype(F32) + other_core(other_ref, step)
    gy = mid_in * gain
    through = rstd * (
        gy
        - jnp.mean(gy, axis=-1, keepdims=True)
        - xhat * jnp.mean(gy * xhat, axis=-1, keepdims=True)
    )
    total = bg_ref[...].astype(F32) + through
    low = total.astype(BF)
    ag_ref[...] = low
    lanes = 4 * HEAD_DIM
    feats = far_w.shape[0]
    for shard, w_ref in enumerate((far_w, own_w)):
        atg_ref[:, shard * lanes : shard * lanes + feats] = nt(low, w_ref[...]).astype(BF)
        atg_ref[:, shard * lanes + feats : (shard + 1) * lanes] = jnp.zeros(
            (low.shape[0], lanes - feats), BF
        )
    size = total.shape[0] // 2

    @pl.when(step == 0)
    def _():
        rg_ref[: 2 * size] = total
        sum_ref[...] = jnp.zeros_like(sum_ref)

    @pl.when(step == 2)
    def _():
        rg_ref[2 * size :] = total[:size]

    sum_ref[0:1, :] += jnp.sum(mid_in * xhat, axis=0, keepdims=True)
    sum_ref[1:2, :] += jnp.sum(mid_in, axis=0, keepdims=True)
    sum_ref[2:3, :] += jnp.sum(low.astype(F32), axis=0, keepdims=True)
    sum_ref[3:4, :] += jnp.sum(bg_ref[...].astype(F32), axis=0, keepdims=True)


def mid_backward(mid, rstd, own, other, bg, vectors, far_w, own_w, size):
    rows, width = own.shape
    lanes = 8 * HEAD_DIM
    block = pl.BlockSpec((2 * size, width), lambda i: (i, 0))
    return pl.pallas_call(
        mid_backward_kernel,
        grid=(3,),
        in_specs=[
            block,
            pl.BlockSpec((2 * size, 128), lambda i: (i, 0)),
            block,
            pl.BlockSpec((2 * size, width), lambda i: (other_pair(i), 0)),
            block,
            fixed((8, width)),
            fixed(far_w.shape),
            fixed(own_w.shape),
        ],
        out_specs=[
            pl.BlockSpec((rows // 2, width), lambda i: (0, 0)),
            block,
            pl.BlockSpec((2 * size, lanes), lambda i: (i, 0)),
            pl.BlockSpec((8, width), lambda i: (0, 0)),
        ],
        out_shape=[
            jax.ShapeDtypeStruct((rows // 2, width), F32),
            jax.ShapeDtypeStruct((rows, width), BF),
            jax.ShapeDtypeStruct((rows, lanes), BF),
            jax.ShapeDtypeStruct((8, width), F32),
        ],
        compiler_params=params(),
        cost_estimate=SMALL_COST,
        name="mid_backward",
    )(mid, rstd, own, other, bg, vectors, far_w, own_w)


def bias_row(ref):
    return ref[9 * HEAD_DIM : 9 * HEAD_DIM + 1].astype(F32)


def pad_heads(w_ref, padded_ref):
    lanes, feats = 4 * HEAD_DIM, 3 * HEAD_DIM
    for i in range(3):
        padded_ref[i * lanes : i * lanes + feats] = w_ref[i * feats : (i + 1) * feats]
        padded_ref[i * lanes + feats : (i + 1) * lanes] = jnp.zeros(
            (lanes - feats, w_ref.shape[1]), BF
        )


def first_kernel(x0, x1, x2, x3, vec_ref, far_ref, own_ref, normed_ref, qkv_ref, far_w, own_w, held_ref):
    @pl.when(pl.program_id(0) == 0)
    def _():
        pad_heads(far_ref, far_w)
        pad_heads(own_ref, own_w)

    stream = two_blocks(pl.program_id(0), (x0, x1, x2, x3), held_ref).astype(F32)
    centered = stream - jnp.mean(stream, axis=-1, keepdims=True)
    variance = jnp.mean(centered * centered, axis=-1, keepdims=True)
    normed = (
        centered * lax.rsqrt(variance + NORM_EPS) * vec_ref[4:5, :] + vec_ref[5:6, :]
    ).astype(BF)
    normed_ref[...] = normed
    third = far_w.shape[0]
    qkv_ref[:, :third] = (nt(normed, far_w[...]) + bias_row(far_ref)).astype(BF)
    qkv_ref[:, third:] = (nt(normed, own_w[...]) + bias_row(own_ref)).astype(BF)


def first(tokens, vectors, far, own, size):
    width = tokens[0].shape[1]
    rows = 8 * size
    outs = 6 * 4 * HEAD_DIM
    block = pl.BlockSpec((2 * size, width), lambda i: (i, 0))
    return pl.pallas_call(
        first_kernel,
        grid=(4,),
        in_specs=[fixed((2 * size, width))] * 4
        + [fixed((8, width)), fixed(far.shape), fixed(own.shape)],
        out_specs=[block, pl.BlockSpec((2 * size, outs), lambda i: (i, 0))],
        out_shape=[
            jax.ShapeDtypeStruct((rows, width), BF),
            jax.ShapeDtypeStruct((rows, outs), BF),
        ],
        scratch_shapes=[pltpu.VMEM((outs // 2, width), BF)] * 2
        + [pltpu.VMEM((2 * size, width), BF)],
        compiler_params=params(),
        cost_estimate=SMALL_COST,
        name="first_norm_qkv",
    )(*tokens, vectors, far, own)


def first_in_kernel(far_d, own_d, far_ref, own_w_ref, own_ref, give_ref, far_w, own_w):
    step = pl.program_id(0)
    half = far_d.shape[0] // 2

    @pl.when(step == 0)
    def _():
        pad_heads(far_ref, far_w)
        pad_heads(own_w_ref, own_w)

    total = (nn(far_d[...], far_w[...]) + nn(own_d[...], own_w[...])).astype(BF)

    @pl.when(step == 0)
    def _():
        own_ref[: 2 * half] = total

    @pl.when(step == 1)
    def _():
        give_ref[: 2 * half] = total

    @pl.when(step == 2)
    def _():
        own_ref[2 * half : 3 * half] = total[:half]
        give_ref[2 * half : 3 * half] = total[half:]

    @pl.when(step == 3)
    def _():
        own_ref[3 * half :] = total[:half]
        give_ref[3 * half :] = total[half:]


def first_in(far_grad, own_grad, far, own, size):
    rows, lanes = far_grad.shape
    width = far.shape[1]
    block = pl.BlockSpec((2 * size, lanes), lambda i: (i, 0))
    whole = pl.BlockSpec((rows // 2, width), lambda i: (0, 0))
    return pl.pallas_call(
        first_in_kernel,
        grid=(4,),
        in_specs=[block, block, fixed(far.shape), fixed(own.shape)],
        out_specs=[whole, whole],
        out_shape=[jax.ShapeDtypeStruct((rows // 2, width), BF)] * 2,
        scratch_shapes=[pltpu.VMEM((lanes, width), BF)] * 2,
        compiler_params=params(),
        cost_estimate=SMALL_COST,
        name="first_in",
    )(far_grad, own_grad, far, own)


def first_backward_kernel(home_ref, away_ref, own_ref, got_ref, rg_ref, vec_ref, *refs):
    extra_ref, (in_ref, sum_ref) = (refs[0] if len(refs) == 3 else None), refs[-2:]
    stream = jnp.where(pl.program_id(0) == 0, home_ref[...], away_ref[...]).astype(F32)
    centered = stream - jnp.mean(stream, axis=-1, keepdims=True)
    rstd = lax.rsqrt(jnp.mean(centered * centered, axis=-1, keepdims=True) + NORM_EPS)
    xhat = centered * rstd
    grad = own_ref[...].astype(F32) + got_ref[...].astype(F32)
    if extra_ref is not None:
        grad = grad + extra_ref[...].astype(F32)
    gy = grad * vec_ref[4:5, :]
    through = rstd * (
        gy
        - jnp.mean(gy, axis=-1, keepdims=True)
        - xhat * jnp.mean(gy * xhat, axis=-1, keepdims=True)
    )
    in_ref[...] = (rg_ref[...] + through).astype(BF)

    @pl.when(pl.program_id(0) == 0)
    def _():
        sum_ref[...] = jnp.zeros_like(sum_ref)

    sum_ref[0:1, :] += jnp.sum(grad * xhat, axis=0, keepdims=True)
    sum_ref[1:2, :] += jnp.sum(grad, axis=0, keepdims=True)


def first_backward(tokens, own, got, residual_grad, vectors, extra, size, owned):
    width = tokens[0].shape[1]
    stride = owned[1] - owned[0] if len(owned) > 1 else 1
    block = pl.BlockSpec((size, width), lambda i: (owned[0] + stride * i, 0))
    home = pl.BlockSpec((size, width), lambda i: (owned[0], 0))
    away = pl.BlockSpec((size, width), lambda i: (0, 0))
    more = () if extra is None else (extra,)
    return pl.pallas_call(
        first_backward_kernel,
        grid=(len(owned),),
        in_specs=[home, away, block, block, block, fixed((8, width))]
        + [pl.BlockSpec((size, width), lambda i: (0, 0))] * len(more),
        out_specs=[
            pl.BlockSpec((size, width), lambda i: (i, 0)),
            pl.BlockSpec((8, width), lambda i: (0, 0)),
        ],
        out_shape=[
            jax.ShapeDtypeStruct((len(owned) * size, width), BF),
            jax.ShapeDtypeStruct((8, width), F32),
        ],
        compiler_params=params(),
        cost_estimate=SMALL_COST,
        name="first_backward",
    )(tokens[0], tokens[2], own, got, residual_grad, vectors, *more)


def dp_partners(count, bit):
    return [(d, d ^ bit) for d in range(count)]


def dp_bits():
    return [1 << i for i in range(lax.axis_size("dp").bit_length() - 1)]


def dp_swap(value, bit):
    return lax.ppermute(value, "dp", dp_partners(lax.axis_size("dp"), bit))


def upper(bit):
    return (lax.axis_index("dp") & bit) != 0


def in_order(value, got, bit, axis=0):
    return jnp.where(
        upper(bit),
        jnp.concatenate([got, value], axis=axis),
        jnp.concatenate([value, got], axis=axis),
    )


def double(value, bit, axis=0):
    return in_order(value, dp_swap(value, bit), bit, axis)


def dp_part(value, axis):
    bits = dp_bits()
    place = sum(jnp.where(upper(bit), value.shape[axis] // (2 * bit), 0) for bit in bits)
    return lax.dynamic_slice_in_dim(value, place, value.shape[axis] // (2 * bits[-1]), axis)


def dp_stages():
    bits = dp_bits()
    return [bits[:1]] + [bits[i : i + 2] for i in range(1, len(bits), 2)]


def masks(bits):
    if len(bits) == 1:
        return [bits[0]]
    return [bits[1], bits[0], bits[0] | bits[1]]


def member(bits):
    place = jnp.where(upper(bits[-1]), 1, 0)
    return place if len(bits) == 1 else place + jnp.where(upper(bits[0]), 2, 0)


class Step:
    def whole(self, value):
        with jax.named_scope(self.name):
            kept, give = self.split(value)
            return self.join(kept, [dp_swap(x, mask) for x, mask in zip(give, self.masks)])


class Scatter(Step):
    def __init__(self, name, bits):
        self.name, self.masks = name, masks(bits)
        self.bits = bits

    def split(self, value):
        axis = value.ndim - 2
        rows = value.shape[axis] // (2 ** len(self.bits))
        mine = member(self.bits)
        pieces = [
            lax.dynamic_slice_in_dim(value, (mine ^ distance) * rows, rows, axis)
            for distance in range(2 ** len(self.bits))
        ]
        return pieces[0], [piece.astype(BF) for piece in pieces[1:]]

    def join(self, kept, got):
        total = kept.astype(F32)
        for piece in got:
            total = total + piece.astype(F32)
        return total


class Gather(Step):
    def __init__(self, name, bits):
        self.name, self.masks = name, masks(bits)
        self.bits = bits

    def split(self, value):
        value = value.astype(BF)
        return value, [value] * len(self.masks)

    def join(self, kept, got):
        if len(self.bits) == 1:
            return in_order(kept, got[0], self.bits[0])
        low = in_order(kept, got[0], self.bits[1])
        return in_order(low, in_order(got[1], got[2], self.bits[1]), self.bits[0])


class GatherAndAdd(Gather):
    def split(self, value):
        pieces, total = value
        rows = -(-total.shape[0] // 16) * 16
        total_low = jnp.pad(total.astype(BF), ((0, rows - total.shape[0]), (0, 0)))
        message = jnp.concatenate([total_low, pieces], axis=0)
        return (pieces, total), [message] * len(self.masks)

    def join(self, kept, got):
        pieces, total = kept
        rows = -(-total.shape[0] // 16) * 16
        for message in got:
            total = total + message[: total.shape[0]].astype(F32)
        return super().join(pieces, [message[rows:] for message in got]), total


def exchange(values, steps, *held):
    values, held = lax.optimization_barrier((tuple(values), held))
    halves = []
    for value, step in zip(values, steps):
        with jax.named_scope(step.name):
            halves.append(step.split(value))
    halves, held = lax.optimization_barrier((halves, held))
    joined = []
    for (kept, give), step in zip(halves, steps):
        with jax.named_scope(step.name):
            got = [dp_swap(piece, mask) for piece, mask in zip(give, step.masks)]
            joined.append((kept, got))

    def finish(*late):
        gots = [got for _, got in joined]
        gots, _ = lax.optimization_barrier((gots, late))
        out = []
        for (kept, _), got, step in zip(joined, gots, steps):
            with jax.named_scope(step.name):
                out.append(step.join(kept, got))
        return out

    return finish, held


def sum_over_tensor(value):
    diagonal = ((0, 3), (1, 2), (2, 1), (3, 0))
    return value + core_swap(value) + x_swap(value) + lax.ppermute(value, "tensor", diagonal)


def after(value, *earlier):
    return lax.optimization_barrier((value,) + earlier)[0]


def body(
    hidden_in,
    doc_ids,
    first_gain,
    first_shift,
    qkv_weight,
    qv_bias,
    proj_weight,
    proj_bias,
    second_gain,
    second_shift,
    up_weight,
    up_bias,
    down_weight,
    down_bias,
    out_grad,
):
    size, rows_dev, width = hidden_in.shape
    length = doc_ids.shape[0]
    place = lax.axis_index("tensor")
    right = place >= 2
    feats = qkv_weight.shape[2]
    inner = up_weight.shape[1]

    def split_rows(value):
        first, mid, last = value[:, 0], value[:, 1], value[:, 2]
        return jnp.where(right, last, first), mid, jnp.where(right, first, last)

    def join_rows(main, mid, other):
        return jnp.stack(
            [jnp.where(right, other, main), mid, jnp.where(right, main, other)], axis=1
        )

    def head_sums(sums_own, sums_far, up_sums):
        slots = []
        for own, away in (
            (up_sums[0:1], up_sums[1:2]),
            (sums_own[:2, :feats].reshape(1, -1), sums_far[:2, :feats].reshape(1, -1)),
        ):
            index = lax.broadcasted_iota(jnp.int32, (4, own.shape[1]), 0)
            value = jnp.where(index == place, own, jnp.where(index == place ^ 2, away, 0.0))
            slots.append(value.reshape(-1, width))
        return slots

    pieces = jnp.stack([dp_part(up_weight, 0), dp_part(down_weight, 0)])
    with jax.named_scope("mlp_weights_x"):
        far_mlp = x_swap(pieces)

    space = jnp.zeros((4 * HEAD_DIM - feats,), BF)
    biases = jnp.concatenate(
        [qv_bias[0], space, jnp.zeros((4 * HEAD_DIM,), BF), qv_bias[1], space, up_bias]
    ).reshape(2, width)
    qkv_own = jnp.concatenate(
        [
            jnp.transpose(qkv_weight, (1, 2, 0)).reshape(3 * feats, width),
            jnp.pad(biases, ((0, 14), (0, 0))),
        ],
        axis=0,
    )

    main, mid, away = split_rows(hidden_in)
    home = jnp.concatenate([main, mid], axis=0)
    with jax.named_scope("tokens"):
        far = x_swap(jnp.concatenate([away, mid], axis=0))
        near = core_swap(home)
        far_near = core_swap(far)
    tokens = (home, near, far, far_near)

    with jax.named_scope("qkv_weights_x"):
        qkv_far = x_swap(qkv_own)
    local_ids = lax.dynamic_slice_in_dim(doc_ids, place * size, size, 0)
    cot = jnp.where((local_ids >= 0)[:, :, None], out_grad, jnp.zeros_like(out_grad))
    g_main, g_mid, g_away = split_rows(cot)
    g_home = jnp.concatenate([g_main, g_mid], axis=0)
    start_rows, table, vectors = prepare(
        doc_ids,
        place,
        (proj_bias, second_gain, second_shift, down_bias, first_gain, first_shift),
        size,
    )

    with jax.named_scope("mlp_weights_dp"):
        far_mlp, qkv_own, g_home, g_away = lax.optimization_barrier(
            (far_mlp, qkv_own, g_home, g_away)
        )
        for bit in reversed(dp_bits()[1:]):
            far_mlp, table, start_rows, vectors = lax.optimization_barrier(
                (double(far_mlp, bit, 1), table, start_rows, vectors)
            )
        far_mlp, held, tokens = lax.optimization_barrier((far_mlp, qkv_far, tokens))
        got_mlp = dp_swap(far_mlp, dp_bits()[0])

    with jax.named_scope("cotangent"):
        g_near = core_swap(g_home)
        g_far = x_swap(after(g_away, held))
        g_far_near = core_swap(g_far)

    with jax.named_scope("proj_weight_x"):
        proj_far = x_swap(after(proj_weight, held))
    normed, qkv = first(tokens, vectors, held, qkv_own, size)
    attended, lse = attend_forward(qkv, table, start_rows, size)
    attn_part = project(after(attended, g_far, g_near, got_mlp), proj_far, proj_weight, size)
    with jax.named_scope("attn_core"):
        attn_other = core_swap(attn_part)
    far_mlp = in_order(far_mlp, got_mlp, dp_bits()[0], 1)

    mid_rstd, normed_mid, act, hidden_grad, out_own, out_give, mid_part, up_sums, branch_grad = mlp(
        tokens, attn_part, attn_other, (g_home, g_near, g_far, g_far_near), vectors, qkv_own, held,
        up_weight, down_weight, far_mlp, size,
    )

    stages = dp_stages()
    first_stage, high_stages = stages[0], stages[1:]

    d, u, t = "down_grad_dp", "up_proj_grad_dp", "qkv_grad_dp"
    singles = [[bit] for bit in dp_bits()[1:]]

    with jax.named_scope("mid_core"):
        mid_other = core_swap(mid_part)
    up_away = sum_tokens(normed_mid, hidden_grad, part=1)
    with jax.named_scope("up_grad_x"):
        up_got = x_swap(up_away)

    down = sum_tokens(act, after(branch_grad, up_away), parts=2).reshape(2, inner, width)
    finish, (mid_rstd, mid_part, attended, hidden_grad, out_give) = exchange(
        [down], [Scatter(d, first_stage)], mid_rstd, mid_part, attended, hidden_grad, out_give
    )
    residual_grad, attn_grad, attended_grad, mid_sums = mid_backward(
        normed_mid, mid_rstd, mid_part, mid_other, branch_grad, vectors,
        proj_far, proj_weight, size,
    )
    proj_away = sum_tokens(attended, attn_grad, rows=feats, count=1)
    with jax.named_scope("proj_grad_x"):
        proj_got = x_swap(proj_away)
    d_far, sums_far = attend_backward(
        qkv, attended, after(attended_grad, proj_away), lse, table, start_rows, size, 0
    )
    qkv_away = sum_tokens(d_far, normed, rows=feats)
    with jax.named_scope("qkv_grad_x"):
        qkv_got = x_swap(qkv_away)
    (down,) = finish(qkv_away)

    finish, (attended_grad, out_give) = exchange(
        [down], [Scatter(d, singles[0])], after(attended_grad, qkv_away), out_give
    )
    with jax.named_scope("block_out"):
        out_got = core_swap(out_give)
    d_own, sums_own = attend_backward(
        qkv, attended, attended_grad, lse, table, start_rows, size, 1
    )
    (down,) = finish(d_own)

    finish, (d_own, up_got, out_got, hidden_grad) = exchange(
        [down], [Scatter(d, singles[1])], d_own, up_got, out_got, hidden_grad
    )
    up = sum_tokens(normed_mid, hidden_grad, up_got, F32, room=feats)
    up, qkv_got, proj_got = lax.optimization_barrier((up, qkv_got, proj_got))
    up = sum_tokens(
        attended, attn_grad, proj_got, F32, rows=feats, first=1, count=1, into=up
    )
    (down,) = finish(up)
    for bits in singles[2:]:
        finish, _ = exchange([down], [Scatter(d, bits)])
        (down,) = finish()
    down_own, down_away = down[0], down[1].astype(BF)

    finish_up, (d_own, qkv_got, down_own, down_away) = exchange(
        [up], [Scatter(u, first_stage)], d_own, qkv_got, down_own, down_away
    )
    with jax.named_scope("down_grad_x"):
        down_got = x_swap(down_away)
    tail = sum_tokens(d_own, normed, qkv_got, F32, rows=feats)
    down_got, tail = lax.optimization_barrier((down_got, tail))
    down = down_own + down_got.astype(F32)

    down_gathers = [Gather(d, bits) for bits in reversed(singles)] + [Gather(d, first_stage)]
    for step in down_gathers[:-3]:
        finish, _ = exchange([down], [step])
        (down,) = finish()
    steps = [Scatter(t, first_stage), down_gathers[-3]]
    finish, (d_own, out_got) = exchange([tail, down], steps, d_own, out_got)
    own_in, give_in = first_in(d_far, d_own, held, qkv_own, size)
    with jax.named_scope("block_out"):
        out_full = (out_own + out_got.astype(F32)).astype(BF)
        out_away = x_swap(out_full[2 * size :])
    (up,) = finish_up(own_in, out_away)

    finish_high, (own_in, give_in) = exchange(
        [up], [Scatter(u, high_stages[0])], own_in, give_in
    )
    tail, down = finish()
    finish, (own_in, give_in) = exchange([down], [down_gathers[-2]], own_in, give_in)
    with jax.named_scope("first_core"):
        got_in = core_swap(give_in)
    mid_sum = (own_in[3 * size :].astype(F32) + got_in[3 * size :].astype(F32)).astype(BF)
    with jax.named_scope("first_mid_x"):
        extra = x_swap(mid_sum)
    in_main, sums_main = first_backward(
        tokens, own_in, got_in, residual_grad, vectors, None, size, (0, 2)
    )
    (up,) = finish_high(in_main)
    (down,) = finish(in_main)
    for bits in high_stages[1:]:
        finish, _ = exchange([up], [Scatter(u, bits)])
        (up,) = finish()

    up_gathers = [Gather(u, bits) for bits in reversed(singles)] + [Gather(u, first_stage)]
    for step in up_gathers[:-3]:
        finish, _ = exchange([up], [step])
        (up,) = finish()
    steps = [Scatter(t, high_stages[0]), up_gathers[-3], down_gathers[-1]]
    finish, (in_main, extra) = exchange([tail, up, down], steps, in_main, extra)
    with jax.named_scope("in_grad_x"):
        in_away = x_swap(in_main[size:])
    in_mid, sums_mid = first_backward(
        tokens, own_in, got_in, residual_grad, vectors, extra, size, (1,)
    )
    tail, up, down = finish(in_mid, in_away)
    for bits in high_stages[1:]:
        finish, _ = exchange([tail], [Scatter(t, bits)])
        (tail,) = finish()
    small = jnp.concatenate(
        [(sums_main + sums_mid)[:2], 0.5 * mid_sums[:4], *head_sums(sums_own, sums_far, up_sums)],
        axis=0,
    )

    steps = [Gather(t, first_stage), up_gathers[-2]]
    finish, (small, in_away, down) = exchange([tail, up], steps, small, in_away, down)
    with jax.named_scope("small_sums"):
        small = sum_over_tensor(small)
        small = small + dp_swap(small, first_stage[0])
    tail, up = finish(small)

    last = high_stages[-1] if len(high_stages[-1]) == 2 else high_stages[-2]
    for bits in reversed([bits for bits in high_stages if bits is not last]):
        finish, _ = exchange([(tail, small)], [GatherAndAdd(t, bits)])
        ((tail, small),) = finish()
    steps = [GatherAndAdd(t, last), up_gathers[-1]]
    finish, _ = exchange([(tail, small), up], steps)
    (tail, small), up = finish()
    tail = tail.reshape(-1, 2, tail.shape[0] // (2 ** len(dp_bits())), width)
    tail = jnp.transpose(tail, (1, 0, 2, 3)).reshape(3 * feats, width)

    block_out = join_rows(out_full[:size], out_full[size : 2 * size], out_away)
    in_grad = join_rows(in_main[:size], in_mid, in_away)

    up_bias_grad = lax.dynamic_slice_in_dim(small, 6 + place, 1, 0)[0]
    qv_all = small[10:].reshape(4, 2, feats)
    qv_bias_grad = lax.dynamic_slice_in_dim(qv_all, place, 1, 0)[0]

    qkv_weight_grad = jnp.transpose(
        tail.reshape(3, feats, width), (2, 0, 1)
    ).astype(F32)
    return (
        block_out,
        in_grad,
        small[0],
        small[1],
        qkv_weight_grad,
        qv_bias_grad,
        up[inner:].astype(F32),
        small[4],
        small[2],
        small[3],
        up[:inner].astype(F32),
        up_bias_grad,
        down.astype(F32),
        small[5],
    )


def solution(mesh):
    in_specs = (
        P("tensor", "dp", None),
        P(None, "dp"),
        P(),
        P(),
        P(None, None, "tensor"),
        P(None, "tensor"),
        P("tensor", None),
        P(),
        P(),
        P(),
        P(None, "tensor"),
        P("tensor"),
        P("tensor", None),
        P(),
        P("tensor", "dp", None),
    )
    out_specs = (
        P("tensor", "dp", None),
        P("tensor", "dp", None),
        P(),
        P(),
        P(None, None, "tensor"),
        P(None, "tensor"),
        P("tensor", None),
        P(),
        P(),
        P(),
        P(None, "tensor"),
        P("tensor"),
        P("tensor", None),
        P(),
    )
    return jax.shard_map(body, mesh=mesh, in_specs=in_specs, out_specs=out_specs, check_vma=False)
```

```python
import functools

import jax
import jax.numpy as jnp
from jax import lax
from jax.experimental import pallas as pl
from jax.experimental.pallas import tpu as pltpu
from jax.sharding import PartitionSpec as P

HEAD_DIM = 64
NORM_EPS = 1e-05
MASKED = -1e30
BF = jnp.bfloat16
F32 = jnp.float32
VMEM_LIMIT = 56 * 1024 * 1024

SLOT = ((0, 2, 4, 5), (1, 3, 6, 7))
SLOT_ROW = (0, 1, 0, 1, 0, 0)
SLOT_K = (0, 0, 1, 1, 2, 3)
X_SWAP = ((0, 2), (1, 3), (2, 0), (3, 1))
CORE_SWAP = ((0, 1), (1, 0), (2, 3), (3, 2))


def x_swap(value):
    return lax.ppermute(value, "tensor", X_SWAP)


def core_swap(value):
    return lax.ppermute(value, "tensor", CORE_SWAP)


def params(semantics=None):
    return pltpu.CompilerParams(vmem_limit_bytes=VMEM_LIMIT)


def fixed(shape):
    return pl.BlockSpec(shape, lambda *ids: (0,) * len(shape), pipeline_mode=pl.Buffered(1))


def nt(left, right):
    return lax.dot_general(left, right, (((1,), (1,)), ((), ())), preferred_element_type=F32)


def nn(left, right):
    return lax.dot_general(left, right, (((1,), (0,)), ((), ())), preferred_element_type=F32)


def tn(left, right):
    return lax.dot_general(left, right, (((0,), (0,)), ((), ())), preferred_element_type=F32)


SMALL_COST = pl.CostEstimate(flops=1, bytes_accessed=1, transcendentals=0)


def key_mask(start_row, key_first, keys, size, diagonal):
    key = lax.broadcasted_iota(jnp.int32, (keys, size), 0)
    mask = key >= start_row - key_first
    if diagonal:
        mask = mask & (key <= lax.broadcasted_iota(jnp.int32, (keys, size), 1))
    return mask


KEYS = 128


def key_rows(table, row, first, size):
    return table[3 + row, first // size] * size + first % size


def head_rows(size):
    lane = lax.broadcasted_iota(jnp.int32, (size, 2 * HEAD_DIM), 1)

    def select(value):
        zero = jnp.zeros((size, 2 * HEAD_DIM), value.dtype)
        pair = value[:, : 2 * HEAD_DIM]
        return (
            jnp.where(lane < HEAD_DIM, pair, zero),
            jnp.where(lane < HEAD_DIM, zero, pair),
            value[:, 2 * HEAD_DIM :],
        )

    return select


def pair_lanes(value, head):
    first = 2 * HEAD_DIM * (head // 2)
    return value[:, first : first + 2 * HEAD_DIM]


def attend_forward_kernel(size, table, start_ref, q_ref, k_ref, v_ref, out_ref, lse_ref):
    slot = pl.program_id(1)
    row, block, low = table[0, slot], table[1, slot], table[2, slot]
    start_row = start_ref[0:1, :]
    select = head_rows(size)
    heads = select(q_ref[...] * jnp.asarray(HEAD_DIM**-0.5, BF))

    def load(first, keys):
        at = pl.multiple_of(key_rows(table, row, first, size), keys)
        return k_ref[pl.ds(at, keys), :], jnp.transpose(v_ref[pl.ds(at, keys), :])

    key, value_t = load(block * size, size)
    mask = key_mask(start_row, block * size, size, size, True)
    all_scores = [nt(pair_lanes(key, head), heads[head]) for head in range(3)]
    carry = []
    for head in range(3):
        scores = jnp.where(mask, all_scores[head], MASKED)
        top = jnp.max(scores, axis=0, keepdims=True)
        weight = jnp.exp(scores - top)
        total = jnp.sum(weight, axis=0, keepdims=True)
        acc = nn(value_t[head * HEAD_DIM : (head + 1) * HEAD_DIM], weight.astype(BF))
        carry += [top, total, acc]

    def earlier(step, carry):
        first = block * size - (step + 1) * KEYS
        key, value_t = load(first, KEYS)
        mask = key_mask(start_row, first, KEYS, size, False)
        all_scores = [nt(pair_lanes(key, head), heads[head]) for head in range(3)]
        new = []
        for head in range(3):
            top, total, acc = carry[3 * head : 3 * head + 3]
            scores = jnp.where(mask, all_scores[head], MASKED)
            higher = jnp.maximum(top, jnp.max(scores, axis=0, keepdims=True))
            shrink = jnp.exp(top - higher)
            weight = jnp.exp(scores - higher)
            total = total * shrink + jnp.sum(weight, axis=0, keepdims=True)
            acc = acc * shrink + nn(
                value_t[head * HEAD_DIM : (head + 1) * HEAD_DIM], weight.astype(BF)
            )
            new += [higher, total, acc]
        return tuple(new)

    carry = lax.fori_loop(0, block * (size // KEYS) - low, earlier, tuple(carry))
    parts = [carry[3 * head + 2] / carry[3 * head + 1] for head in range(3)]
    parts.append(jnp.zeros_like(parts[0]))
    out_ref[...] = jnp.transpose(jnp.concatenate(parts, axis=0)).astype(BF)
    for head in range(3):
        lse_ref[head : head + 1, :] = carry[3 * head] + jnp.log(carry[3 * head + 1])


def attend_forward(qkv, table, starts, size):
    width = 4 * HEAD_DIM
    tokens = qkv.shape[0]
    return pl.pallas_call(
        functools.partial(attend_forward_kernel, size),
        grid_spec=pltpu.PrefetchScalarGridSpec(
            num_scalar_prefetch=1,
            grid=(2, 6),
            in_specs=[
                pl.BlockSpec((8, size), lambda p, s, *_: (0, s)),
                pl.BlockSpec((size, width), lambda p, s, *_: (s, 3 * p)),
                pl.BlockSpec((tokens, width), lambda p, s, *_: (0, 3 * p + 1)),
                pl.BlockSpec((tokens, width), lambda p, s, *_: (0, 3 * p + 2)),
            ],
            out_specs=[
                pl.BlockSpec((size, width), lambda p, s, *_: (s, p)),
                pl.BlockSpec((8, size), lambda p, s, *_: (p, s)),
            ],
        ),
        out_shape=[
            jax.ShapeDtypeStruct((6 * size, 2 * width), BF),
            jax.ShapeDtypeStruct((16, 6 * size), F32),
        ],
        compiler_params=params(),
        cost_estimate=SMALL_COST,
        name="attend_forward",
    )(table, starts, qkv, qkv, qkv)


def attend_backward_kernel(
    size, table, start_ref, q_ref, k_ref, v_ref, out_ref, grad_ref, lse_ref,
    d_ref, sum_ref, dk_acc, dv_acc,
):
    slot = pl.program_id(0)
    width = 4 * HEAD_DIM
    row, block, low = table[0, slot], table[1, slot], table[2, slot]
    start_row = start_ref[0:1, :]
    select = head_rows(size)
    q_heads = select(q_ref[...] * jnp.asarray(HEAD_DIM**-0.5, BF))
    grad = grad_ref[...]
    g_heads = select(grad)
    products = jnp.transpose(grad.astype(F32) * out_ref[...].astype(F32))
    deltas = [
        jnp.sum(products[head * HEAD_DIM : (head + 1) * HEAD_DIM], axis=0, keepdims=True)
        for head in range(3)
    ]

    @pl.when(slot == 0)
    def _():
        dk_acc[...] = jnp.zeros_like(dk_acc)
        dv_acc[...] = jnp.zeros_like(dv_acc)
        sum_ref[...] = jnp.zeros_like(sum_ref)

    def one_block(first, keys, diagonal):
        at = pl.multiple_of(key_rows(table, row, first, size), keys)
        key, value = k_ref[pl.ds(at, keys), :], v_ref[pl.ds(at, keys), :]
        key_t = jnp.transpose(key)
        mask = key_mask(start_row, first, keys, size, diagonal)
        all_scores = [nt(pair_lanes(key, head), q_heads[head]) for head in range(3)]
        all_grads = [nt(pair_lanes(value, head), g_heads[head]) for head in range(3)]
        dq_parts, dk_parts, dv_parts = [], [], []
        for head in range(3):
            scores = jnp.where(mask, all_scores[head], MASKED)
            prob = jnp.exp(scores - lse_ref[head : head + 1, :])
            score_grad = (prob * (all_grads[head] - deltas[head])).astype(BF)
            dk_parts.append(nn(score_grad, q_heads[head]))
            dv_parts.append(nn(prob.astype(BF), g_heads[head]))
            dq_parts.append(nn(key_t[head * HEAD_DIM : (head + 1) * HEAD_DIM], score_grad))
        dk_acc[pl.ds(at, keys), : width // 2] += dk_parts[0] + dk_parts[1]
        dk_acc[pl.ds(at, keys), width // 2 :] += dk_parts[2]
        dv_acc[pl.ds(at, keys), : width // 2] += dv_parts[0] + dv_parts[1]
        dv_acc[pl.ds(at, keys), width // 2 :] += dv_parts[2]
        return jnp.concatenate(dq_parts, axis=0)

    dq_t = one_block(block * size, size, True)
    dq_t = lax.fori_loop(
        0,
        block * (size // KEYS) - low,
        lambda step, acc: acc + one_block(block * size - (step + 1) * KEYS, KEYS, False),
        dq_t,
    )
    dq_t = jnp.concatenate([dq_t, jnp.zeros((HEAD_DIM, size), F32)], axis=0)
    dq = (jnp.transpose(dq_t) * HEAD_DIM**-0.5).astype(BF)
    d_ref[pl.ds(pl.multiple_of(slot * size, size), size), :width] = dq
    sum_ref[0:1, :] += jnp.sum(dq.astype(F32), axis=0, keepdims=True)

    @pl.when(slot == pl.num_programs(0) - 1)
    def _():
        d_ref[6 * size :, :width] = jnp.zeros((2 * size, width), BF)
        d_ref[:, width : 2 * width] = dk_acc[...].astype(BF)
        dv = dv_acc[...].astype(BF)
        d_ref[:, 2 * width :] = dv
        sum_ref[1:2, :] = jnp.sum(dv.astype(F32), axis=0, keepdims=True)


def attend_backward(qkv, attended, grad, lse, table, starts, size, shard):
    tokens = qkv.shape[0]
    width = 4 * HEAD_DIM
    block = pl.BlockSpec((size, width), lambda s, *_: (s, shard))
    return pl.pallas_call(
        functools.partial(attend_backward_kernel, size),
        grid_spec=pltpu.PrefetchScalarGridSpec(
            num_scalar_prefetch=1,
            grid=(6,),
            in_specs=[
                pl.BlockSpec((8, size), lambda s, *_: (0, s)),
                pl.BlockSpec((size, width), lambda s, *_: (s, 3 * shard)),
                pl.BlockSpec((tokens, width), lambda s, *_: (0, 3 * shard + 1)),
                pl.BlockSpec((tokens, width), lambda s, *_: (0, 3 * shard + 2)),
                block,
                block,
                pl.BlockSpec((8, size), lambda s, *_: (shard, s)),
            ],
            out_specs=[
                pl.BlockSpec((tokens, 3 * width), lambda s, *_: (0, 0)),
                pl.BlockSpec((8, width), lambda s, *_: (0, 0)),
            ],
            scratch_shapes=[pltpu.VMEM((tokens, width), F32), pltpu.VMEM((tokens, width), F32)],
        ),
        out_shape=[
            jax.ShapeDtypeStruct((tokens, 3 * width), BF),
            jax.ShapeDtypeStruct((8, width), F32),
        ],
        compiler_params=params(),
        cost_estimate=SMALL_COST,
        name="attend_backward",
    )(table, starts, qkv, qkv, qkv, attended, grad, lse)


def prepare_kernel(size, place_ref, ids_ref, *refs):
    vectors, (start_ref, table_ref, vec_ref, rows_ref) = refs[:-4], refs[-4:]
    for i, ref in enumerate(vectors):
        vec_ref[i : i + 1, :] = ref[...].astype(F32).reshape(1, -1)
    vec_ref[len(vectors) :, :] = jnp.zeros((8 - len(vectors), vec_ref.shape[1]), F32)
    place = place_ref[0]
    ids = ids_ref[...]
    length = ids.shape[1]
    position = lax.broadcasted_iota(jnp.int32, ids.shape, 1)
    starts = position
    for doc in range(8):
        here = ids == doc
        first_one = jnp.min(jnp.where(here, position, length), axis=1, keepdims=True)
        starts = jnp.where(here, first_one, starts)
    rows_ref[...] = starts
    for i in range(8):
        for j in range(8):
            table_ref[i, j] = 0
    for slot in range(6):
        row, block = SLOT_ROW[slot], SLOT_K[slot] ^ place
        source = jnp.where(place >= 2, 2, 0) if row == 0 else 1
        at = pl.ds(pl.multiple_of(block * size, size), size)
        first_row, second_row, third_row = rows_ref[0:1, at], rows_ref[1:2, at], rows_ref[2:3, at]
        mine = second_row if row else jnp.where(source == 2, third_row, first_row)
        start_ref[:, slot * size : (slot + 1) * size] = jnp.broadcast_to(mine, (8, size))
        table_ref[0, slot] = row
        table_ref[1, slot] = block
        table_ref[2, slot] = jnp.min(mine) // KEYS
    for row in range(2):
        for block in range(4):
            slots = SLOT[row]
            near = block ^ place
            table_ref[3 + row, block] = jnp.where(
                near < 2,
                jnp.where(near == 0, slots[0], slots[1]),
                jnp.where(near == 2, slots[2], slots[3]),
            )


def prepare(doc_ids, place, vectors, size):
    ids = jnp.pad(jnp.transpose(doc_ids), ((0, 5), (0, 0)), constant_values=-1)
    vmem, smem = pl.BlockSpec(memory_space=pltpu.VMEM), pl.BlockSpec(memory_space=pltpu.SMEM)
    return pl.pallas_call(
        functools.partial(prepare_kernel, size),
        in_specs=[smem, vmem] + [vmem] * len(vectors),
        out_specs=[vmem, smem, vmem],
        out_shape=[
            jax.ShapeDtypeStruct((8, 6 * size), jnp.int32),
            jax.ShapeDtypeStruct((8, 8), jnp.int32),
            jax.ShapeDtypeStruct((8, vectors[0].shape[0]), F32),
        ],
        scratch_shapes=[pltpu.VMEM(ids.shape, jnp.int32)],
        cost_estimate=SMALL_COST,
        name="prepare",
    )(place.reshape(1).astype(jnp.int32), ids, *vectors)


GELU_C = 0.7978845608028654
GELU_A = 0.044715


def two_blocks(step, refs, held_ref):
    home_ref, near_ref, far_ref, far_near_ref = refs
    half = home_ref.shape[0] // 2

    @pl.when(step == 0)
    def _():
        held_ref[...] = home_ref[...]

    @pl.when(step == 1)
    def _():
        held_ref[...] = near_ref[...]

    @pl.when(step == 2)
    def _():
        held_ref[:half] = far_ref[:half]
        held_ref[half:] = far_near_ref[:half]

    if far_ref.shape[0] > half:

        @pl.when(step == 3)
        def _():
            held_ref[:half] = far_ref[half:]
            held_ref[half:] = far_near_ref[half:]

    return held_ref[...]


def other_core(ref, step):
    value = ref[...].astype(F32)
    half = value.shape[0] // 2
    turned = jnp.concatenate([value[half:], value[:half]], axis=0)
    return jnp.where(step == 2, turned, value)


def other_pair(step):
    return jnp.where(step == 2, 2, 1 - step)


def mlp_kernel(
    x0, x1, x2, x3, own_ref, other_ref, b0, b1, b2, b3, vec_ref, upb_own, upb_far, up_own, up_far, dn_own, dn_far,
    rstd_ref, mid_ref, act_ref, hg_ref, out_ref, give_ref, midin_ref, upbg_ref, bg_ref, held_ref,
):
    step = pl.program_id(0)
    proj_bias, gain, shift = vec_ref[0:1, :], vec_ref[1:2, :], vec_ref[2:3, :]
    residual = two_blocks(step, (x0, x1, x2, x3), held_ref).astype(F32) + own_ref[...].astype(F32)
    residual = residual + other_core(other_ref, step) + proj_bias
    centered = residual - jnp.mean(residual, axis=-1, keepdims=True)
    variance = jnp.mean(centered * centered, axis=-1, keepdims=True)
    rstd = lax.rsqrt(variance + NORM_EPS)
    rstd_ref[...] = jnp.broadcast_to(rstd, rstd_ref.shape)
    mid = (centered * rstd * gain + shift).astype(BF)
    mid_ref[...] = mid
    bg = two_blocks(step, (b0, b1, b2, b3), bg_ref)

    @pl.when(step == 0)
    def _():
        upbg_ref[...] = jnp.zeros_like(upbg_ref)

    out = None
    midin = None
    weights = ((up_own[...], dn_own[...], upb_own[...]), (up_far[0], dn_far[0], upb_far[...]))
    for part, (up_w, dn_w, up_bias) in enumerate(weights):
        hidden = nn(mid, up_w) + up_bias[1:2].astype(F32)
        act_grad = nt(bg, dn_w)
        square = hidden * hidden
        bent = jnp.tanh(GELU_C * (hidden + GELU_A * hidden * square))
        half = 0.5 * (1.0 + bent)
        act = (hidden * half).astype(BF)
        slope = half + 0.5 * hidden * (1.0 - bent * bent) * (GELU_C + 3.0 * GELU_C * GELU_A * square)
        grad = (act_grad * slope).astype(BF)
        act_ref[part] = act
        hg_ref[part] = grad
        upbg_ref[part : part + 1, :] += jnp.sum(grad.astype(F32), axis=0, keepdims=True)
        out_part = nn(act, dn_w)
        midin_part = nt(grad, up_w)
        out = out_part if out is None else out + out_part
        midin = midin_part if midin is None else midin + midin_part
    midin_ref[...] = midin.astype(BF)
    size = out.shape[0] // 2

    @pl.when(step == 0)
    def _():
        out_ref[: 2 * size] = out + residual + vec_ref[3:4, :]

    @pl.when(step == 1)
    def _():
        give_ref[: 2 * size] = out.astype(BF)

    @pl.when(step == 2)
    def _():
        out_ref[2 * size :] = (out + residual)[:size] + vec_ref[3:4, :]
        give_ref[2 * size :] = out[size:].astype(BF)


def mlp(tokens, own, other, bg, vectors, qkv_own, qkv_far, up_own, down_own, far, size):
    rows, width = own.shape
    inner = up_own.shape[1]
    block = pl.BlockSpec((2 * size, width), lambda i: (i, 0))
    wide = pl.BlockSpec((2, 2 * size, inner), lambda i: (0, i, 0))
    half = pl.BlockSpec((rows // 2, width), lambda i: (0, 0))
    return pl.pallas_call(
        mlp_kernel,
        grid=(3,),
        in_specs=[fixed((2 * size, width))] * 4
        + [
            block,
            pl.BlockSpec((2 * size, width), lambda i: (other_pair(i), 0)),
        ]
        + [fixed(value.shape) for value in bg]
        + [
            fixed((8, width)),
            pl.BlockSpec((16, width), lambda i: (9 * HEAD_DIM // 16, 0)),
            pl.BlockSpec((16, width), lambda i: (9 * HEAD_DIM // 16, 0)),
            fixed((width, inner)),
            pl.BlockSpec((1, width, inner), lambda i: (0, 0, 0), pipeline_mode=pl.Buffered(1)),
            fixed((inner, width)),
            pl.BlockSpec((1, inner, width), lambda i: (1, 0, 0), pipeline_mode=pl.Buffered(1)),
        ],
        out_specs=[
            pl.BlockSpec((2 * size, 128), lambda i: (i, 0)),
            block, wide, wide, half, half, block,
            pl.BlockSpec((8, inner), lambda i: (0, 0)),
            block,
        ],
        out_shape=[
            jax.ShapeDtypeStruct((rows, 128), F32),
            jax.ShapeDtypeStruct((rows, width), BF),
            jax.ShapeDtypeStruct((2, rows, inner), BF),
            jax.ShapeDtypeStruct((2, rows, inner), BF),
            jax.ShapeDtypeStruct((rows // 2, width), F32),
            jax.ShapeDtypeStruct((rows // 2, width), BF),
            jax.ShapeDtypeStruct((rows, width), BF),
            jax.ShapeDtypeStruct((8, inner), F32),
            jax.ShapeDtypeStruct((rows, width), BF),
        ],
        scratch_shapes=[pltpu.VMEM((2 * size, width), BF)],
        compiler_params=params(),
        cost_estimate=SMALL_COST,
        name="mlp",
    )(*tokens, own, other, *bg, vectors, qkv_own, qkv_far, up_own, far, down_own, far)


def sum_tokens_kernel(rows, has_extra, left_ref, right_ref, *refs):
    left = left_ref[0] if len(left_ref.shape) == 3 else left_ref[...]
    right = right_ref[0] if len(right_ref.shape) == 3 else right_ref[...]
    total = tn(left, right)[:rows]
    if has_extra:
        total = total + refs[0][...].astype(F32)
    refs[-1][...] = total.astype(refs[-1].dtype)


def sum_tokens(
    left, right, extra=None, dtype=BF, part=0, parts=1, rows=256, first=0, count=None, room=0, into=None
):
    block = 256
    blocks = left.shape[-1] // block
    count = count or parts * blocks
    tokens, width = right.shape[-2:]

    def spec(value, lanes, at):
        if value.ndim == 3 and parts > 1:
            return pl.BlockSpec((1, tokens, lanes), lambda i: (i // blocks, 0, i % blocks))
        if value.ndim == 3:
            return pl.BlockSpec((1, tokens, lanes), lambda i: (part, 0, at(i)))
        return pl.BlockSpec((tokens, lanes), lambda i: (0, at(i)))

    base = 0 if into is None else into.shape[0] // rows - count
    out = pl.BlockSpec((rows, width), lambda i: (base + i, 0))
    specs = [spec(left, block, lambda i: first + i), spec(right, width, lambda i: 0)]
    operands = [left, right]
    if extra is not None:
        specs.append(pl.BlockSpec((rows, width), lambda i: (i, 0)))
        operands.append(extra)
    aliases = {}
    shape = jax.ShapeDtypeStruct((count * rows + room, width), dtype)
    if into is not None:
        specs.append(pl.BlockSpec(memory_space=pl.ANY))
        aliases = {len(operands): 0}
        operands.append(into)
        shape = jax.ShapeDtypeStruct(into.shape, into.dtype)
    return pl.pallas_call(
        functools.partial(sum_tokens_kernel, rows, extra is not None),
        grid=(count,),
        in_specs=specs,
        out_specs=out,
        out_shape=shape,
        input_output_aliases=aliases,
        compiler_params=params(),
        cost_estimate=SMALL_COST,
        name="sum_tokens",
    )(*operands)


def project_kernel(heads_ref, far_w, own_w, out_ref):
    lanes = 4 * HEAD_DIM
    feats = far_w.shape[0]
    total = nn(heads_ref[:, :feats], far_w[...])
    out_ref[...] = (total + nn(heads_ref[:, lanes : lanes + feats], own_w[...])).astype(BF)


def project(heads, far_w, own_w, size):
    rows, lanes = heads.shape
    width = far_w.shape[1]
    return pl.pallas_call(
        project_kernel,
        grid=(3,),
        in_specs=[
            pl.BlockSpec((2 * size, lanes), lambda i: (i, 0)), fixed(far_w.shape), fixed(own_w.shape)
        ],
        out_specs=pl.BlockSpec((2 * size, width), lambda i: (i, 0)),
        out_shape=jax.ShapeDtypeStruct((rows, width), BF),
        compiler_params=params(),
        cost_estimate=SMALL_COST,
        name="project",
    )(heads, far_w, own_w)


def mid_backward_kernel(
    mid_ref, rstd_ref, own_ref, other_ref, bg_ref, vec_ref, far_w, own_w,
    rg_ref, ag_ref, atg_ref, sum_ref,
):
    step = pl.program_id(0)
    gain, shift = vec_ref[1:2, :], vec_ref[2:3, :]
    rstd = rstd_ref[:, 0:1]
    xhat = (mid_ref[...].astype(F32) - shift) * (1.0 / gain)
    mid_in = own_ref[...].astype(F32) + other_core(other_ref, step)
    gy = mid_in * gain
    through = rstd * (
        gy
        - jnp.mean(gy, axis=-1, keepdims=True)
        - xhat * jnp.mean(gy * xhat, axis=-1, keepdims=True)
    )
    total = bg_ref[...].astype(F32) + through
    low = total.astype(BF)
    ag_ref[...] = low
    lanes = 4 * HEAD_DIM
    feats = far_w.shape[0]
    for shard, w_ref in enumerate((far_w, own_w)):
        atg_ref[:, shard * lanes : shard * lanes + feats] = nt(low, w_ref[...]).astype(BF)
        atg_ref[:, shard * lanes + feats : (shard + 1) * lanes] = jnp.zeros(
            (low.shape[0], lanes - feats), BF
        )
    size = total.shape[0] // 2

    @pl.when(step == 0)
    def _():
        rg_ref[: 2 * size] = total
        sum_ref[...] = jnp.zeros_like(sum_ref)

    @pl.when(step == 2)
    def _():
        rg_ref[2 * size :] = total[:size]

    sum_ref[0:1, :] += jnp.sum(mid_in * xhat, axis=0, keepdims=True)
    sum_ref[1:2, :] += jnp.sum(mid_in, axis=0, keepdims=True)
    sum_ref[2:3, :] += jnp.sum(low.astype(F32), axis=0, keepdims=True)
    sum_ref[3:4, :] += jnp.sum(bg_ref[...].astype(F32), axis=0, keepdims=True)


def mid_backward(mid, rstd, own, other, bg, vectors, far_w, own_w, size):
    rows, width = own.shape
    lanes = 8 * HEAD_DIM
    block = pl.BlockSpec((2 * size, width), lambda i: (i, 0))
    return pl.pallas_call(
        mid_backward_kernel,
        grid=(3,),
        in_specs=[
            block,
            pl.BlockSpec((2 * size, 128), lambda i: (i, 0)),
            block,
            pl.BlockSpec((2 * size, width), lambda i: (other_pair(i), 0)),
            block,
            fixed((8, width)),
            fixed(far_w.shape),
            fixed(own_w.shape),
        ],
        out_specs=[
            pl.BlockSpec((rows // 2, width), lambda i: (0, 0)),
            block,
            pl.BlockSpec((2 * size, lanes), lambda i: (i, 0)),
            pl.BlockSpec((8, width), lambda i: (0, 0)),
        ],
        out_shape=[
            jax.ShapeDtypeStruct((rows // 2, width), F32),
            jax.ShapeDtypeStruct((rows, width), BF),
            jax.ShapeDtypeStruct((rows, lanes), BF),
            jax.ShapeDtypeStruct((8, width), F32),
        ],
        compiler_params=params(),
        cost_estimate=SMALL_COST,
        name="mid_backward",
    )(mid, rstd, own, other, bg, vectors, far_w, own_w)


def bias_row(ref):
    return ref[9 * HEAD_DIM : 9 * HEAD_DIM + 1].astype(F32)


def pad_heads(w_ref, padded_ref):
    lanes, feats = 4 * HEAD_DIM, 3 * HEAD_DIM
    for i in range(3):
        padded_ref[i * lanes : i * lanes + feats] = w_ref[i * feats : (i + 1) * feats]
        padded_ref[i * lanes + feats : (i + 1) * lanes] = jnp.zeros(
            (lanes - feats, w_ref.shape[1]), BF
        )


def first_kernel(x0, x1, x2, x3, vec_ref, far_ref, own_ref, normed_ref, qkv_ref, far_w, own_w, held_ref):
    @pl.when(pl.program_id(0) == 0)
    def _():
        pad_heads(far_ref, far_w)
        pad_heads(own_ref, own_w)

    stream = two_blocks(pl.program_id(0), (x0, x1, x2, x3), held_ref).astype(F32)
    centered = stream - jnp.mean(stream, axis=-1, keepdims=True)
    variance = jnp.mean(centered * centered, axis=-1, keepdims=True)
    normed = (
        centered * lax.rsqrt(variance + NORM_EPS) * vec_ref[4:5, :] + vec_ref[5:6, :]
    ).astype(BF)
    normed_ref[...] = normed
    third = far_w.shape[0]
    qkv_ref[:, :third] = (nt(normed, far_w[...]) + bias_row(far_ref)).astype(BF)
    qkv_ref[:, third:] = (nt(normed, own_w[...]) + bias_row(own_ref)).astype(BF)


def first(tokens, vectors, far, own, size):
    width = tokens[0].shape[1]
    rows = 8 * size
    outs = 6 * 4 * HEAD_DIM
    block = pl.BlockSpec((2 * size, width), lambda i: (i, 0))
    return pl.pallas_call(
        first_kernel,
        grid=(4,),
        in_specs=[fixed((2 * size, width))] * 4
        + [fixed((8, width)), fixed(far.shape), fixed(own.shape)],
        out_specs=[block, pl.BlockSpec((2 * size, outs), lambda i: (i, 0))],
        out_shape=[
            jax.ShapeDtypeStruct((rows, width), BF),
            jax.ShapeDtypeStruct((rows, outs), BF),
        ],
        scratch_shapes=[pltpu.VMEM((outs // 2, width), BF)] * 2
        + [pltpu.VMEM((2 * size, width), BF)],
        compiler_params=params(),
        cost_estimate=SMALL_COST,
        name="first_norm_qkv",
    )(*tokens, vectors, far, own)


def first_in_kernel(far_d, own_d, far_ref, own_w_ref, own_ref, give_ref, far_w, own_w):
    step = pl.program_id(0)
    half = far_d.shape[0] // 2

    @pl.when(step == 0)
    def _():
        pad_heads(far_ref, far_w)
        pad_heads(own_w_ref, own_w)

    total = (nn(far_d[...], far_w[...]) + nn(own_d[...], own_w[...])).astype(BF)

    @pl.when(step == 0)
    def _():
        own_ref[: 2 * half] = total

    @pl.when(step == 1)
    def _():
        give_ref[: 2 * half] = total

    @pl.when(step == 2)
    def _():
        own_ref[2 * half : 3 * half] = total[:half]
        give_ref[2 * half : 3 * half] = total[half:]

    @pl.when(step == 3)
    def _():
        own_ref[3 * half :] = total[:half]
        give_ref[3 * half :] = total[half:]


def first_in(far_grad, own_grad, far, own, size):
    rows, lanes = far_grad.shape
    width = far.shape[1]
    block = pl.BlockSpec((2 * size, lanes), lambda i: (i, 0))
    whole = pl.BlockSpec((rows // 2, width), lambda i: (0, 0))
    return pl.pallas_call(
        first_in_kernel,
        grid=(4,),
        in_specs=[block, block, fixed(far.shape), fixed(own.shape)],
        out_specs=[whole, whole],
        out_shape=[jax.ShapeDtypeStruct((rows // 2, width), BF)] * 2,
        scratch_shapes=[pltpu.VMEM((lanes, width), BF)] * 2,
        compiler_params=params(),
        cost_estimate=SMALL_COST,
        name="first_in",
    )(far_grad, own_grad, far, own)


def first_backward_kernel(home_ref, away_ref, own_ref, got_ref, rg_ref, vec_ref, *refs):
    extra_ref, (in_ref, sum_ref) = (refs[0] if len(refs) == 3 else None), refs[-2:]
    stream = jnp.where(pl.program_id(0) == 0, home_ref[...], away_ref[...]).astype(F32)
    centered = stream - jnp.mean(stream, axis=-1, keepdims=True)
    rstd = lax.rsqrt(jnp.mean(centered * centered, axis=-1, keepdims=True) + NORM_EPS)
    xhat = centered * rstd
    grad = own_ref[...].astype(F32) + got_ref[...].astype(F32)
    if extra_ref is not None:
        grad = grad + extra_ref[...].astype(F32)
    gy = grad * vec_ref[4:5, :]
    through = rstd * (
        gy
        - jnp.mean(gy, axis=-1, keepdims=True)
        - xhat * jnp.mean(gy * xhat, axis=-1, keepdims=True)
    )
    in_ref[...] = (rg_ref[...] + through).astype(BF)

    @pl.when(pl.program_id(0) == 0)
    def _():
        sum_ref[...] = jnp.zeros_like(sum_ref)

    sum_ref[0:1, :] += jnp.sum(grad * xhat, axis=0, keepdims=True)
    sum_ref[1:2, :] += jnp.sum(grad, axis=0, keepdims=True)


def first_backward(tokens, own, got, residual_grad, vectors, extra, size, owned):
    width = tokens[0].shape[1]
    stride = owned[1] - owned[0] if len(owned) > 1 else 1
    block = pl.BlockSpec((size, width), lambda i: (owned[0] + stride * i, 0))
    home = pl.BlockSpec((size, width), lambda i: (owned[0], 0))
    away = pl.BlockSpec((size, width), lambda i: (0, 0))
    more = () if extra is None else (extra,)
    return pl.pallas_call(
        first_backward_kernel,
        grid=(len(owned),),
        in_specs=[home, away, block, block, block, fixed((8, width))]
        + [pl.BlockSpec((size, width), lambda i: (0, 0))] * len(more),
        out_specs=[
            pl.BlockSpec((size, width), lambda i: (i, 0)),
            pl.BlockSpec((8, width), lambda i: (0, 0)),
        ],
        out_shape=[
            jax.ShapeDtypeStruct((len(owned) * size, width), BF),
            jax.ShapeDtypeStruct((8, width), F32),
        ],
        compiler_params=params(),
        cost_estimate=SMALL_COST,
        name="first_backward",
    )(tokens[0], tokens[2], own, got, residual_grad, vectors, *more)


def dp_partners(count, bit):
    return [(d, d ^ bit) for d in range(count)]


def dp_bits():
    return [1 << i for i in range(lax.axis_size("dp").bit_length() - 1)]


def dp_swap(value, bit):
    return lax.ppermute(value, "dp", dp_partners(lax.axis_size("dp"), bit))


def upper(bit):
    return (lax.axis_index("dp") & bit) != 0


def in_order(value, got, bit, axis=0):
    return jnp.where(
        upper(bit),
        jnp.concatenate([got, value], axis=axis),
        jnp.concatenate([value, got], axis=axis),
    )


def double(value, bit, axis=0):
    return in_order(value, dp_swap(value, bit), bit, axis)


def dp_part(value, axis):
    bits = dp_bits()
    place = sum(jnp.where(upper(bit), value.shape[axis] // (2 * bit), 0) for bit in bits)
    return lax.dynamic_slice_in_dim(value, place, value.shape[axis] // (2 * bits[-1]), axis)


def dp_stages():
    bits = dp_bits()
    return [bits[:1]] + [bits[i : i + 2] for i in range(1, len(bits), 2)]


def masks(bits):
    if len(bits) == 1:
        return [bits[0]]
    return [bits[1], bits[0], bits[0] | bits[1]]


def member(bits):
    place = jnp.where(upper(bits[-1]), 1, 0)
    return place if len(bits) == 1 else place + jnp.where(upper(bits[0]), 2, 0)


class Step:
    def whole(self, value):
        with jax.named_scope(self.name):
            kept, give = self.split(value)
            return self.join(kept, [dp_swap(x, mask) for x, mask in zip(give, self.masks)])


class Scatter(Step):
    def __init__(self, name, bits):
        self.name, self.masks = name, masks(bits)
        self.bits = bits

    def split(self, value):
        axis = value.ndim - 2
        rows = value.shape[axis] // (2 ** len(self.bits))
        mine = member(self.bits)
        pieces = [
            lax.dynamic_slice_in_dim(value, (mine ^ distance) * rows, rows, axis)
            for distance in range(2 ** len(self.bits))
        ]
        return pieces[0], [piece.astype(BF) for piece in pieces[1:]]

    def join(self, kept, got):
        total = kept.astype(F32)
        for piece in got:
            total = total + piece.astype(F32)
        return total


class Gather(Step):
    def __init__(self, name, bits):
        self.name, self.masks = name, masks(bits)
        self.bits = bits

    def split(self, value):
        value = value.astype(BF)
        return value, [value] * len(self.masks)

    def join(self, kept, got):
        if len(self.bits) == 1:
            return in_order(kept, got[0], self.bits[0])
        low = in_order(kept, got[0], self.bits[1])
        return in_order(low, in_order(got[1], got[2], self.bits[1]), self.bits[0])


class GatherAndAdd(Gather):
    def split(self, value):
        pieces, total = value
        rows = -(-total.shape[0] // 16) * 16
        total_low = jnp.pad(total.astype(BF), ((0, rows - total.shape[0]), (0, 0)))
        message = jnp.concatenate([total_low, pieces], axis=0)
        return (pieces, total), [message] * len(self.masks)

    def join(self, kept, got):
        pieces, total = kept
        rows = -(-total.shape[0] // 16) * 16
        for message in got:
            total = total + message[: total.shape[0]].astype(F32)
        return super().join(pieces, [message[rows:] for message in got]), total


def exchange(values, steps, *held):
    values, held = lax.optimization_barrier((tuple(values), held))
    halves = []
    for value, step in zip(values, steps):
        with jax.named_scope(step.name):
            halves.append(step.split(value))
    halves, held = lax.optimization_barrier((halves, held))
    joined = []
    for (kept, give), step in zip(halves, steps):
        with jax.named_scope(step.name):
            got = [dp_swap(piece, mask) for piece, mask in zip(give, step.masks)]
            joined.append((kept, got))

    def finish(*late):
        gots = [got for _, got in joined]
        gots, _ = lax.optimization_barrier((gots, late))
        out = []
        for (kept, _), got, step in zip(joined, gots, steps):
            with jax.named_scope(step.name):
                out.append(step.join(kept, got))
        return out

    return finish, held


def sum_over_tensor(value):
    diagonal = ((0, 3), (1, 2), (2, 1), (3, 0))
    return value + core_swap(value) + x_swap(value) + lax.ppermute(value, "tensor", diagonal)


def after(value, *earlier):
    return lax.optimization_barrier((value,) + earlier)[0]


def body(
    hidden_in,
    doc_ids,
    first_gain,
    first_shift,
    qkv_weight,
    qv_bias,
    proj_weight,
    proj_bias,
    second_gain,
    second_shift,
    up_weight,
    up_bias,
    down_weight,
    down_bias,
    out_grad,
):
    size, rows_dev, width = hidden_in.shape
    length = doc_ids.shape[0]
    place = lax.axis_index("tensor")
    right = place >= 2
    feats = qkv_weight.shape[2]
    inner = up_weight.shape[1]

    def split_rows(value):
        first, mid, last = value[:, 0], value[:, 1], value[:, 2]
        return jnp.where(right, last, first), mid, jnp.where(right, first, last)

    def join_rows(main, mid, other):
        return jnp.stack(
            [jnp.where(right, other, main), mid, jnp.where(right, main, other)], axis=1
        )

    def head_sums(sums_own, sums_far, up_sums):
        slots = []
        for own, away in (
            (up_sums[0:1], up_sums[1:2]),
            (sums_own[:2, :feats].reshape(1, -1), sums_far[:2, :feats].reshape(1, -1)),
        ):
            index = lax.broadcasted_iota(jnp.int32, (4, own.shape[1]), 0)
            value = jnp.where(index == place, own, jnp.where(index == place ^ 2, away, 0.0))
            slots.append(value.reshape(-1, width))
        return slots

    pieces = jnp.stack([dp_part(up_weight, 0), dp_part(down_weight, 0)])
    with jax.named_scope("mlp_weights_x"):
        far_mlp = x_swap(pieces)

    space = jnp.zeros((4 * HEAD_DIM - feats,), BF)
    biases = jnp.concatenate(
        [qv_bias[0], space, jnp.zeros((4 * HEAD_DIM,), BF), qv_bias[1], space, up_bias]
    ).reshape(2, width)
    qkv_own = jnp.concatenate(
        [
            jnp.transpose(qkv_weight, (1, 2, 0)).reshape(3 * feats, width),
            jnp.pad(biases, ((0, 14), (0, 0))),
        ],
        axis=0,
    )

    main, mid, away = split_rows(hidden_in)
    home = jnp.concatenate([main, mid], axis=0)
    with jax.named_scope("tokens"):
        far = x_swap(jnp.concatenate([away, mid], axis=0))
        near = core_swap(home)
        far_near = core_swap(far)
    tokens = (home, near, far, far_near)

    with jax.named_scope("qkv_weights_x"):
        qkv_far = x_swap(qkv_own)
    local_ids = lax.dynamic_slice_in_dim(doc_ids, place * size, size, 0)
    cot = jnp.where((local_ids >= 0)[:, :, None], out_grad, jnp.zeros_like(out_grad))
    g_main, g_mid, g_away = split_rows(cot)
    g_home = jnp.concatenate([g_main, g_mid], axis=0)
    start_rows, table, vectors = prepare(
        doc_ids,
        place,
        (proj_bias, second_gain, second_shift, down_bias, first_gain, first_shift),
        size,
    )

    with jax.named_scope("mlp_weights_dp"):
        far_mlp, qkv_own, g_home, g_away = lax.optimization_barrier(
            (far_mlp, qkv_own, g_home, g_away)
        )
        for bit in reversed(dp_bits()[1:]):
            far_mlp, table, start_rows, vectors = lax.optimization_barrier(
                (double(far_mlp, bit, 1), table, start_rows, vectors)
            )
        far_mlp, held, tokens = lax.optimization_barrier((far_mlp, qkv_far, tokens))
        got_mlp = dp_swap(far_mlp, dp_bits()[0])

    with jax.named_scope("cotangent"):
        g_near = core_swap(g_home)
        g_far = x_swap(after(g_away, held))
        g_far_near = core_swap(g_far)

    with jax.named_scope("proj_weight_x"):
        proj_far = x_swap(after(proj_weight, held))
    normed, qkv = first(tokens, vectors, held, qkv_own, size)
    attended, lse = attend_forward(qkv, table, start_rows, size)
    attn_part = project(after(attended, g_far, g_near, got_mlp), proj_far, proj_weight, size)
    with jax.named_scope("attn_core"):
        attn_other = core_swap(attn_part)
    far_mlp = in_order(far_mlp, got_mlp, dp_bits()[0], 1)

    mid_rstd, normed_mid, act, hidden_grad, out_own, out_give, mid_part, up_sums, branch_grad = mlp(
        tokens, attn_part, attn_other, (g_home, g_near, g_far, g_far_near), vectors, qkv_own, held,
        up_weight, down_weight, far_mlp, size,
    )

    stages = dp_stages()
    first_stage, high_stages = stages[0], stages[1:]

    d, u, t = "down_grad_dp", "up_proj_grad_dp", "qkv_grad_dp"
    singles = [[bit] for bit in dp_bits()[1:]]

    with jax.named_scope("mid_core"):
        mid_other = core_swap(mid_part)
    up_away = sum_tokens(normed_mid, hidden_grad, part=1)
    with jax.named_scope("up_grad_x"):
        up_got = x_swap(up_away)

    down = sum_tokens(act, after(branch_grad, up_away), parts=2).reshape(2, inner, width)
    finish, (mid_rstd, mid_part, attended, hidden_grad, out_give) = exchange(
        [down], [Scatter(d, first_stage)], mid_rstd, mid_part, attended, hidden_grad, out_give
    )
    residual_grad, attn_grad, attended_grad, mid_sums = mid_backward(
        normed_mid, mid_rstd, mid_part, mid_other, branch_grad, vectors,
        proj_far, proj_weight, size,
    )
    proj_away = sum_tokens(attended, attn_grad, rows=feats, count=1)
    with jax.named_scope("proj_grad_x"):
        proj_got = x_swap(proj_away)
    d_far, sums_far = attend_backward(
        qkv, attended, after(attended_grad, proj_away), lse, table, start_rows, size, 0
    )
    qkv_away = sum_tokens(d_far, normed, rows=feats)
    with jax.named_scope("qkv_grad_x"):
        qkv_got = x_swap(qkv_away)
    (down,) = finish(qkv_away)

    finish, (attended_grad, out_give) = exchange(
        [down], [Scatter(d, singles[0])], after(attended_grad, qkv_away), out_give
    )
    with jax.named_scope("block_out"):
        out_got = core_swap(out_give)
    d_own, sums_own = attend_backward(
        qkv, attended, attended_grad, lse, table, start_rows, size, 1
    )
    (down,) = finish(d_own)

    finish, (d_own, up_got, out_got, hidden_grad) = exchange(
        [down], [Scatter(d, singles[1])], d_own, up_got, out_got, hidden_grad
    )
    up = sum_tokens(normed_mid, hidden_grad, up_got, room=feats)
    up, qkv_got, proj_got = lax.optimization_barrier((up, qkv_got, proj_got))
    up = sum_tokens(
        attended, attn_grad, proj_got, rows=feats, first=1, count=1, into=up
    )
    (down,) = finish(up)
    for bits in singles[2:]:
        finish, _ = exchange([down], [Scatter(d, bits)])
        (down,) = finish()
    down_own, down_away = down[0], down[1].astype(BF)

    finish_up, (d_own, qkv_got, down_own, down_away) = exchange(
        [up], [Scatter(u, first_stage)], d_own, qkv_got, down_own, down_away
    )
    with jax.named_scope("down_grad_x"):
        down_got = x_swap(down_away)
    tail = sum_tokens(d_own, normed, qkv_got, rows=feats)
    down_got, tail = lax.optimization_barrier((down_got, tail))
    down = down_own + down_got.astype(F32)

    down_gathers = [Gather(d, bits) for bits in reversed(singles)] + [Gather(d, first_stage)]
    for step in down_gathers[:-3]:
        finish, _ = exchange([down], [step])
        (down,) = finish()
    steps = [Scatter(t, first_stage), down_gathers[-3]]
    finish, (d_own, out_got) = exchange([tail, down], steps, d_own, out_got)
    own_in, give_in = first_in(d_far, d_own, held, qkv_own, size)
    with jax.named_scope("block_out"):
        out_full = (out_own + out_got.astype(F32)).astype(BF)
        out_away = x_swap(out_full[2 * size :])
    (up,) = finish_up(own_in, out_away)

    finish_high, (own_in, give_in) = exchange(
        [up], [Scatter(u, high_stages[0])], own_in, give_in
    )
    tail, down = finish()
    finish, (own_in, give_in) = exchange([down], [down_gathers[-2]], own_in, give_in)
    with jax.named_scope("first_core"):
        got_in = core_swap(give_in)
    mid_sum = (own_in[3 * size :].astype(F32) + got_in[3 * size :].astype(F32)).astype(BF)
    with jax.named_scope("first_mid_x"):
        extra = x_swap(mid_sum)
    in_main, sums_main = first_backward(
        tokens, own_in, got_in, residual_grad, vectors, None, size, (0, 2)
    )
    (up,) = finish_high(in_main)
    (down,) = finish(in_main)
    for bits in high_stages[1:]:
        finish, _ = exchange([up], [Scatter(u, bits)])
        (up,) = finish()

    up_gathers = [Gather(u, bits) for bits in reversed(singles)] + [Gather(u, first_stage)]
    for step in up_gathers[:-3]:
        finish, _ = exchange([up], [step])
        (up,) = finish()
    steps = [Scatter(t, high_stages[0]), up_gathers[-3], down_gathers[-1]]
    finish, (in_main, extra, out_full, out_away) = exchange(
        [tail, up, down], steps, in_main, extra, out_full, out_away
    )
    block_out = join_rows(out_full[:size], out_full[size : 2 * size], out_away)
    in_mid, sums_mid = first_backward(
        tokens, own_in, got_in, residual_grad, vectors, extra, size, (1,)
    )
    tail, up, down = finish(in_mid, block_out)
    for bits in high_stages[1:]:
        finish, _ = exchange([tail], [Scatter(t, bits)])
        (tail,) = finish()
    small = jnp.concatenate(
        [(sums_main + sums_mid)[:2], 0.5 * mid_sums[:4], *head_sums(sums_own, sums_far, up_sums)],
        axis=0,
    )

    steps = [Gather(t, first_stage), up_gathers[-2]]
    finish, (small, in_main, down) = exchange([tail, up], steps, small, in_main, down)
    with jax.named_scope("small_sums"):
        small = sum_over_tensor(small)
        small = small + dp_swap(small, first_stage[0])
    with jax.named_scope("in_grad_x"):
        in_away = x_swap(after(in_main[size:], small))
    down = down.astype(F32)
    tail, up = finish(small, down)

    last = high_stages[-1] if len(high_stages[-1]) == 2 else high_stages[-2]
    for bits in reversed([bits for bits in high_stages if bits is not last]):
        finish, _ = exchange([(tail, small)], [GatherAndAdd(t, bits)])
        ((tail, small),) = finish()
    finish_up, (tail, small) = exchange([up], [up_gathers[-1]], tail, small)
    finish, _ = exchange([(tail, small)], [GatherAndAdd(t, last)])
    (up,) = finish_up()
    up_weight_grad, proj_weight_grad = up[:inner].astype(F32), up[inner:].astype(F32)
    ((tail, small),) = finish(up_weight_grad, proj_weight_grad)
    tail = tail.reshape(-1, 2, tail.shape[0] // (2 ** len(dp_bits())), width)
    tail = jnp.transpose(tail, (1, 0, 2, 3)).reshape(3 * feats, width)

    in_grad = join_rows(in_main[:size], in_mid, in_away)

    up_bias_grad = lax.dynamic_slice_in_dim(small, 6 + place, 1, 0)[0]
    qv_all = small[10:].reshape(4, 2, feats)
    qv_bias_grad = lax.dynamic_slice_in_dim(qv_all, place, 1, 0)[0]

    qkv_weight_grad = jnp.transpose(
        tail.reshape(3, feats, width), (2, 0, 1)
    ).astype(F32)
    return (
        block_out,
        in_grad,
        small[0],
        small[1],
        qkv_weight_grad,
        qv_bias_grad,
        proj_weight_grad,
        small[4],
        small[2],
        small[3],
        up_weight_grad,
        up_bias_grad,
        down,
        small[5],
    )


def solution(mesh):
    in_specs = (
        P("tensor", "dp", None),
        P(None, "dp"),
        P(),
        P(),
        P(None, None, "tensor"),
        P(None, "tensor"),
        P("tensor", None),
        P(),
        P(),
        P(),
        P(None, "tensor"),
        P("tensor"),
        P("tensor", None),
        P(),
        P("tensor", "dp", None),
    )
    out_specs = (
        P("tensor", "dp", None),
        P("tensor", "dp", None),
        P(),
        P(),
        P(None, None, "tensor"),
        P(None, "tensor"),
        P("tensor", None),
        P(),
        P(),
        P(),
        P(None, "tensor"),
        P("tensor"),
        P("tensor", None),
        P(),
    )
    return jax.shard_map(body, mesh=mesh, in_specs=in_specs, out_specs=out_specs, check_vma=False)
```

```python
import functools

import jax
import jax.numpy as jnp
from jax import lax
from jax.experimental import pallas as pl
from jax.experimental.pallas import tpu as pltpu
from jax.sharding import PartitionSpec as P

HEAD_DIM = 64
NORM_EPS = 1e-05
MASKED = -1e30
BF = jnp.bfloat16
F32 = jnp.float32
VMEM_LIMIT = 56 * 1024 * 1024

SLOT = ((0, 2, 4, 5), (1, 3, 6, 7))
SLOT_ROW = (0, 1, 0, 1, 0, 0)
SLOT_K = (0, 0, 1, 1, 2, 3)
X_SWAP = ((0, 2), (1, 3), (2, 0), (3, 1))
CORE_SWAP = ((0, 1), (1, 0), (2, 3), (3, 2))
DIAGONAL = ((0, 3), (1, 2), (2, 1), (3, 0))


def x_swap(value):
    return lax.ppermute(value, "tensor", X_SWAP)


def core_swap(value):
    return lax.ppermute(value, "tensor", CORE_SWAP)


def params(semantics=None):
    return pltpu.CompilerParams(vmem_limit_bytes=VMEM_LIMIT)


def fixed(shape):
    return pl.BlockSpec(shape, lambda *ids: (0,) * len(shape), pipeline_mode=pl.Buffered(1))


def nt(left, right):
    return lax.dot_general(left, right, (((1,), (1,)), ((), ())), preferred_element_type=F32)


def nn(left, right):
    return lax.dot_general(left, right, (((1,), (0,)), ((), ())), preferred_element_type=F32)


def tn(left, right):
    return lax.dot_general(left, right, (((0,), (0,)), ((), ())), preferred_element_type=F32)


SMALL_COST = pl.CostEstimate(flops=1, bytes_accessed=1, transcendentals=0)


def key_mask(start_row, key_first, keys, size, diagonal):
    key = lax.broadcasted_iota(jnp.int32, (keys, size), 0)
    mask = key >= start_row - key_first
    if diagonal:
        mask = mask & (key <= lax.broadcasted_iota(jnp.int32, (keys, size), 1))
    return mask


KEYS = 128


def key_rows(table, row, first, size):
    return table[3 + row, first // size] * size + first % size


def head_rows(size):
    lane = lax.broadcasted_iota(jnp.int32, (size, 2 * HEAD_DIM), 1)

    def select(value):
        zero = jnp.zeros((size, 2 * HEAD_DIM), value.dtype)
        pair = value[:, : 2 * HEAD_DIM]
        return (
            jnp.where(lane < HEAD_DIM, pair, zero),
            jnp.where(lane < HEAD_DIM, zero, pair),
            value[:, 2 * HEAD_DIM :],
        )

    return select


def pair_lanes(value, head):
    first = 2 * HEAD_DIM * (head // 2)
    return value[:, first : first + 2 * HEAD_DIM]


def attend_forward_kernel(size, table, start_ref, *refs):
    parts = (refs[:3], refs[3:6])
    out_ref, lse_ref = refs[6:]
    slot = pl.program_id(0)
    row, block, low = table[0, slot], table[1, slot], table[2, slot]
    start_row = start_ref[0:1, :]
    select = head_rows(size)
    heads = [
        head for q_ref, _, _ in parts for head in select(q_ref[...] * jnp.asarray(HEAD_DIM**-0.5, BF))
    ]
    count = len(heads)

    def load(first, keys):
        at = pl.multiple_of(key_rows(table, row, first, size), keys)
        loaded = [
            (k_ref[pl.ds(at, keys), :], jnp.transpose(v_ref[pl.ds(at, keys), :]))
            for _, k_ref, v_ref in parts
        ]
        scores = [
            nt(pair_lanes(loaded[head // 3][0], head % 3), heads[head]) for head in range(count)
        ]
        values = [
            loaded[head // 3][1][head % 3 * HEAD_DIM : (head % 3 + 1) * HEAD_DIM]
            for head in range(count)
        ]
        return scores, values

    all_scores, values = load(block * size, size)
    mask = key_mask(start_row, block * size, size, size, True)
    carry = []
    for head in range(count):
        scores = jnp.where(mask, all_scores[head], MASKED)
        top = jnp.max(scores, axis=0, keepdims=True)
        weight = jnp.exp(scores - top)
        total = jnp.sum(weight, axis=0, keepdims=True)
        carry += [top, total, nn(values[head], weight.astype(BF))]

    def earlier(step, carry):
        first = block * size - (step + 1) * KEYS
        all_scores, values = load(first, KEYS)
        mask = key_mask(start_row, first, KEYS, size, False)
        new = []
        for head in range(count):
            top, total, acc = carry[3 * head : 3 * head + 3]
            scores = jnp.where(mask, all_scores[head], MASKED)
            higher = jnp.maximum(top, jnp.max(scores, axis=0, keepdims=True))
            shrink = jnp.exp(top - higher)
            weight = jnp.exp(scores - higher)
            total = total * shrink + jnp.sum(weight, axis=0, keepdims=True)
            new += [higher, total, acc * shrink + nn(values[head], weight.astype(BF))]
        return tuple(new)

    carry = lax.fori_loop(0, block * (size // KEYS) - low, earlier, tuple(carry))
    for shard in range(2):
        rows = []
        for head in range(3 * shard, 3 * shard + 3):
            rows.append(carry[3 * head + 2] / carry[3 * head + 1])
            at = 8 * shard + head % 3
            lse_ref[at : at + 1, :] = carry[3 * head] + jnp.log(carry[3 * head + 1])
        rows.append(jnp.zeros_like(rows[0]))
        lanes = slice(4 * HEAD_DIM * shard, 4 * HEAD_DIM * (shard + 1))
        out_ref[:, lanes] = jnp.transpose(jnp.concatenate(rows, axis=0)).astype(BF)


def attend_forward(qkv, table, starts, size):
    width = 4 * HEAD_DIM
    tokens = qkv.shape[0]
    specs = [pl.BlockSpec((8, size), lambda s, *_: (0, s))]
    for shard in range(2):
        specs += [
            pl.BlockSpec((size, width), functools.partial(lambda c, s, *_: (s, c), 3 * shard)),
            pl.BlockSpec((tokens, width), functools.partial(lambda c, s, *_: (0, c), 3 * shard + 1)),
            pl.BlockSpec((tokens, width), functools.partial(lambda c, s, *_: (0, c), 3 * shard + 2)),
        ]
    return pl.pallas_call(
        functools.partial(attend_forward_kernel, size),
        grid_spec=pltpu.PrefetchScalarGridSpec(
            num_scalar_prefetch=1,
            grid=(6,),
            in_specs=specs,
            out_specs=[
                pl.BlockSpec((size, 2 * width), lambda s, *_: (s, 0)),
                pl.BlockSpec((16, size), lambda s, *_: (0, s)),
            ],
        ),
        out_shape=[
            jax.ShapeDtypeStruct((6 * size, 2 * width), BF),
            jax.ShapeDtypeStruct((16, 6 * size), F32),
        ],
        compiler_params=params(),
        cost_estimate=SMALL_COST,
        name="attend_forward",
    )(table, starts, *[qkv] * 6)


def attend_backward_kernel(
    size, table, start_ref, q_ref, k_ref, v_ref, out_ref, grad_ref, lse_ref,
    d_ref, sum_ref, dk_acc, dv_acc,
):
    slot = pl.program_id(0)
    width = 4 * HEAD_DIM
    row, block, low = table[0, slot], table[1, slot], table[2, slot]
    start_row = start_ref[0:1, :]
    select = head_rows(size)
    q_heads = select(q_ref[...] * jnp.asarray(HEAD_DIM**-0.5, BF))
    grad = grad_ref[...]
    g_heads = select(grad)
    products = jnp.transpose(grad.astype(F32) * out_ref[...].astype(F32))
    deltas = [
        jnp.sum(products[head * HEAD_DIM : (head + 1) * HEAD_DIM], axis=0, keepdims=True)
        for head in range(3)
    ]

    @pl.when(slot == 0)
    def _():
        dk_acc[...] = jnp.zeros_like(dk_acc)
        dv_acc[...] = jnp.zeros_like(dv_acc)
        sum_ref[...] = jnp.zeros_like(sum_ref)

    def one_block(first, keys, diagonal):
        at = pl.multiple_of(key_rows(table, row, first, size), keys)
        key, value = k_ref[pl.ds(at, keys), :], v_ref[pl.ds(at, keys), :]
        key_t = jnp.transpose(key)
        mask = key_mask(start_row, first, keys, size, diagonal)
        all_scores = [nt(pair_lanes(key, head), q_heads[head]) for head in range(3)]
        all_grads = [nt(pair_lanes(value, head), g_heads[head]) for head in range(3)]
        dq_parts, dk_parts, dv_parts = [], [], []
        for head in range(3):
            scores = jnp.where(mask, all_scores[head], MASKED)
            prob = jnp.exp(scores - lse_ref[head : head + 1, :])
            score_grad = (prob * (all_grads[head] - deltas[head])).astype(BF)
            dk_parts.append(nn(score_grad, q_heads[head]))
            dv_parts.append(nn(prob.astype(BF), g_heads[head]))
            dq_parts.append(nn(key_t[head * HEAD_DIM : (head + 1) * HEAD_DIM], score_grad))
        dk_acc[pl.ds(at, keys), : width // 2] += dk_parts[0] + dk_parts[1]
        dk_acc[pl.ds(at, keys), width // 2 :] += dk_parts[2]
        dv_acc[pl.ds(at, keys), : width // 2] += dv_parts[0] + dv_parts[1]
        dv_acc[pl.ds(at, keys), width // 2 :] += dv_parts[2]
        return jnp.concatenate(dq_parts, axis=0)

    dq_t = one_block(block * size, size, True)
    dq_t = lax.fori_loop(
        0,
        block * (size // KEYS) - low,
        lambda step, acc: acc + one_block(block * size - (step + 1) * KEYS, KEYS, False),
        dq_t,
    )
    dq_t = jnp.concatenate([dq_t, jnp.zeros((HEAD_DIM, size), F32)], axis=0)
    dq = (jnp.transpose(dq_t) * HEAD_DIM**-0.5).astype(BF)
    d_ref[pl.ds(pl.multiple_of(slot * size, size), size), :width] = dq
    sum_ref[0:1, :] += jnp.sum(dq.astype(F32), axis=0, keepdims=True)

    @pl.when(slot == pl.num_programs(0) - 1)
    def _():
        d_ref[6 * size :, :width] = jnp.zeros((2 * size, width), BF)
        d_ref[:, width : 2 * width] = dk_acc[...].astype(BF)
        dv = dv_acc[...].astype(BF)
        d_ref[:, 2 * width :] = dv
        sum_ref[1:2, :] = jnp.sum(dv.astype(F32), axis=0, keepdims=True)


def attend_backward(qkv, attended, grad, lse, table, starts, size, shard):
    tokens = qkv.shape[0]
    width = 4 * HEAD_DIM
    block = pl.BlockSpec((size, width), lambda s, *_: (s, shard))
    return pl.pallas_call(
        functools.partial(attend_backward_kernel, size),
        grid_spec=pltpu.PrefetchScalarGridSpec(
            num_scalar_prefetch=1,
            grid=(6,),
            in_specs=[
                pl.BlockSpec((8, size), lambda s, *_: (0, s)),
                pl.BlockSpec((size, width), lambda s, *_: (s, 3 * shard)),
                pl.BlockSpec((tokens, width), lambda s, *_: (0, 3 * shard + 1)),
                pl.BlockSpec((tokens, width), lambda s, *_: (0, 3 * shard + 2)),
                block,
                block,
                pl.BlockSpec((8, size), lambda s, *_: (shard, s)),
            ],
            out_specs=[
                pl.BlockSpec((tokens, 3 * width), lambda s, *_: (0, 0)),
                pl.BlockSpec((8, width), lambda s, *_: (0, 0)),
            ],
            scratch_shapes=[pltpu.VMEM((tokens, width), F32), pltpu.VMEM((tokens, width), F32)],
        ),
        out_shape=[
            jax.ShapeDtypeStruct((tokens, 3 * width), BF),
            jax.ShapeDtypeStruct((8, width), F32),
        ],
        compiler_params=params(),
        cost_estimate=SMALL_COST,
        name="attend_backward",
    )(table, starts, qkv, qkv, qkv, attended, grad, lse)


def prepare_kernel(size, place_ref, ids_ref, *refs):
    vectors, (start_ref, table_ref, vec_ref, rows_ref) = refs[:-4], refs[-4:]
    for i, ref in enumerate(vectors):
        vec_ref[i : i + 1, :] = ref[...].astype(F32).reshape(1, -1)
    vec_ref[len(vectors) :, :] = jnp.zeros((8 - len(vectors), vec_ref.shape[1]), F32)
    place = place_ref[0]
    ids = ids_ref[...]
    length = ids.shape[1]
    position = lax.broadcasted_iota(jnp.int32, ids.shape, 1)
    starts = position
    for doc in range(8):
        here = ids == doc
        first_one = jnp.min(jnp.where(here, position, length), axis=1, keepdims=True)
        starts = jnp.where(here, first_one, starts)
    rows_ref[...] = starts
    for i in range(8):
        for j in range(8):
            table_ref[i, j] = 0
    for slot in range(6):
        row, block = SLOT_ROW[slot], SLOT_K[slot] ^ place
        source = jnp.where(place >= 2, 2, 0) if row == 0 else 1
        at = pl.ds(pl.multiple_of(block * size, size), size)
        first_row, second_row, third_row = rows_ref[0:1, at], rows_ref[1:2, at], rows_ref[2:3, at]
        mine = second_row if row else jnp.where(source == 2, third_row, first_row)
        start_ref[:, slot * size : (slot + 1) * size] = jnp.broadcast_to(mine, (8, size))
        table_ref[0, slot] = row
        table_ref[1, slot] = block
        table_ref[2, slot] = jnp.min(mine) // KEYS
    for row in range(2):
        for block in range(4):
            slots = SLOT[row]
            near = block ^ place
            table_ref[3 + row, block] = jnp.where(
                near < 2,
                jnp.where(near == 0, slots[0], slots[1]),
                jnp.where(near == 2, slots[2], slots[3]),
            )


def prepare(doc_ids, place, vectors, size):
    ids = jnp.pad(jnp.transpose(doc_ids), ((0, 5), (0, 0)), constant_values=-1)
    vmem, smem = pl.BlockSpec(memory_space=pltpu.VMEM), pl.BlockSpec(memory_space=pltpu.SMEM)
    return pl.pallas_call(
        functools.partial(prepare_kernel, size),
        in_specs=[smem, vmem] + [vmem] * len(vectors),
        out_specs=[vmem, smem, vmem],
        out_shape=[
            jax.ShapeDtypeStruct((8, 6 * size), jnp.int32),
            jax.ShapeDtypeStruct((8, 8), jnp.int32),
            jax.ShapeDtypeStruct((8, vectors[0].shape[0]), F32),
        ],
        scratch_shapes=[pltpu.VMEM(ids.shape, jnp.int32)],
        cost_estimate=SMALL_COST,
        name="prepare",
    )(place.reshape(1).astype(jnp.int32), ids, *vectors)


GELU_C = 0.7978845608028654
GELU_A = 0.044715


def two_blocks(step, refs, held_ref):
    home_ref, near_ref, far_ref, far_near_ref = refs
    half = home_ref.shape[0] // 2

    @pl.when(step == 0)
    def _():
        held_ref[...] = home_ref[...]

    @pl.when(step == 1)
    def _():
        held_ref[...] = near_ref[...]

    @pl.when(step == 2)
    def _():
        held_ref[:half] = far_ref[:half]
        held_ref[half:] = far_near_ref[:half]

    if far_ref.shape[0] > half:

        @pl.when(step == 3)
        def _():
            held_ref[:half] = far_ref[half:]
            held_ref[half:] = far_near_ref[half:]

    return held_ref[...]


def other_core(ref, step):
    value = ref[...].astype(F32)
    half = value.shape[0] // 2
    turned = jnp.concatenate([value[half:], value[:half]], axis=0)
    return jnp.where(step == 2, turned, value)


def other_pair(step):
    return jnp.where(step == 2, 2, 1 - step)


def mlp_kernel(
    x0, x1, x2, x3, own_ref, other_ref, b0, b1, b2, b3, vec_ref, upb_own, upb_far, up_own, up_far, dn_own, dn_far,
    rstd_ref, mid_ref, act_ref, hg_ref, out_ref, give_ref, midin_ref, upbg_ref, bg_ref, held_ref,
):
    step = pl.program_id(0)
    proj_bias, gain, shift = vec_ref[0:1, :], vec_ref[1:2, :], vec_ref[2:3, :]
    residual = two_blocks(step, (x0, x1, x2, x3), held_ref).astype(F32) + own_ref[...].astype(F32)
    residual = residual + other_core(other_ref, step) + proj_bias
    centered = residual - jnp.mean(residual, axis=-1, keepdims=True)
    variance = jnp.mean(centered * centered, axis=-1, keepdims=True)
    rstd = lax.rsqrt(variance + NORM_EPS)
    rstd_ref[...] = jnp.broadcast_to(rstd, rstd_ref.shape)
    mid = (centered * rstd * gain + shift).astype(BF)
    mid_ref[...] = mid
    bg = two_blocks(step, (b0, b1, b2, b3), bg_ref)

    @pl.when(step == 0)
    def _():
        upbg_ref[...] = jnp.zeros_like(upbg_ref)

    out = None
    midin = None
    weights = ((up_own[...], dn_own[...], upb_own[...]), (up_far[0], dn_far[0], upb_far[...]))
    for part, (up_w, dn_w, up_bias) in enumerate(weights):
        hidden = nn(mid, up_w) + up_bias[1:2].astype(F32)
        act_grad = nt(bg, dn_w)
        square = hidden * hidden
        bent = jnp.tanh(GELU_C * (hidden + GELU_A * hidden * square))
        half = 0.5 * (1.0 + bent)
        act = (hidden * half).astype(BF)
        slope = half + 0.5 * hidden * (1.0 - bent * bent) * (GELU_C + 3.0 * GELU_C * GELU_A * square)
        grad = (act_grad * slope).astype(BF)
        act_ref[part] = act
        hg_ref[part] = grad
        upbg_ref[part : part + 1, :] += jnp.sum(grad.astype(F32), axis=0, keepdims=True)
        out_part = nn(act, dn_w)
        midin_part = nt(grad, up_w)
        out = out_part if out is None else out + out_part
        midin = midin_part if midin is None else midin + midin_part
    midin_ref[...] = midin.astype(BF)
    size = out.shape[0] // 2

    @pl.when(step == 0)
    def _():
        out_ref[: 2 * size] = out + residual + vec_ref[3:4, :]

    @pl.when(step == 1)
    def _():
        give_ref[: 2 * size] = out.astype(BF)

    @pl.when(step == 2)
    def _():
        out_ref[2 * size :] = (out + residual)[:size] + vec_ref[3:4, :]
        give_ref[2 * size :] = out[size:].astype(BF)


def mlp(tokens, own, other, bg, vectors, qkv_own, qkv_far, up_own, down_own, far, size):
    rows, width = own.shape
    inner = up_own.shape[1]
    block = pl.BlockSpec((2 * size, width), lambda i: (i, 0))
    wide = pl.BlockSpec((2, 2 * size, inner), lambda i: (0, i, 0))
    half = pl.BlockSpec((rows // 2, width), lambda i: (0, 0))
    return pl.pallas_call(
        mlp_kernel,
        grid=(3,),
        in_specs=[fixed((2 * size, width))] * 4
        + [
            block,
            pl.BlockSpec((2 * size, width), lambda i: (other_pair(i), 0)),
        ]
        + [fixed(value.shape) for value in bg]
        + [
            fixed((8, width)),
            pl.BlockSpec((16, width), lambda i: (9 * HEAD_DIM // 16, 0)),
            pl.BlockSpec((16, width), lambda i: (9 * HEAD_DIM // 16, 0)),
            fixed((width, inner)),
            pl.BlockSpec((1, width, inner), lambda i: (0, 0, 0), pipeline_mode=pl.Buffered(1)),
            fixed((inner, width)),
            pl.BlockSpec((1, inner, width), lambda i: (1, 0, 0), pipeline_mode=pl.Buffered(1)),
        ],
        out_specs=[
            pl.BlockSpec((2 * size, 128), lambda i: (i, 0)),
            block, wide, wide, half, half, block,
            pl.BlockSpec((8, inner), lambda i: (0, 0)),
            block,
        ],
        out_shape=[
            jax.ShapeDtypeStruct((rows, 128), F32),
            jax.ShapeDtypeStruct((rows, width), BF),
            jax.ShapeDtypeStruct((2, rows, inner), BF),
            jax.ShapeDtypeStruct((2, rows, inner), BF),
            jax.ShapeDtypeStruct((rows // 2, width), F32),
            jax.ShapeDtypeStruct((rows // 2, width), BF),
            jax.ShapeDtypeStruct((rows, width), BF),
            jax.ShapeDtypeStruct((8, inner), F32),
            jax.ShapeDtypeStruct((rows, width), BF),
        ],
        scratch_shapes=[pltpu.VMEM((2 * size, width), BF)],
        compiler_params=params(),
        cost_estimate=SMALL_COST,
        name="mlp",
    )(*tokens, own, other, *bg, vectors, qkv_own, qkv_far, up_own, far, down_own, far)


def sum_tokens_kernel(rows, has_extra, left_ref, right_ref, *refs):
    left = left_ref[0] if len(left_ref.shape) == 3 else left_ref[...]
    right = right_ref[0] if len(right_ref.shape) == 3 else right_ref[...]
    total = tn(left, right)[:rows]
    if has_extra:
        total = total + refs[0][...].astype(F32)
    refs[-1][...] = total.astype(refs[-1].dtype)


def sum_tokens(
    left, right, extra=None, dtype=BF, part=0, parts=1, rows=256, first=0, count=None, room=0, into=None
):
    block = 256
    blocks = left.shape[-1] // block
    count = count or parts * blocks
    tokens, width = right.shape[-2:]

    def spec(value, lanes, at):
        if value.ndim == 3 and parts > 1:
            return pl.BlockSpec((1, tokens, lanes), lambda i: (i // blocks, 0, i % blocks))
        if value.ndim == 3:
            return pl.BlockSpec((1, tokens, lanes), lambda i: (part, 0, at(i)))
        return pl.BlockSpec((tokens, lanes), lambda i: (0, at(i)))

    base = 0 if into is None else into.shape[0] // rows - count
    out = pl.BlockSpec((rows, width), lambda i: (base + i, 0))
    specs = [spec(left, block, lambda i: first + i), spec(right, width, lambda i: 0)]
    operands = [left, right]
    if extra is not None:
        specs.append(pl.BlockSpec((rows, width), lambda i: (i, 0)))
        operands.append(extra)
    aliases = {}
    shape = jax.ShapeDtypeStruct((count * rows + room, width), dtype)
    if into is not None:
        specs.append(pl.BlockSpec(memory_space=pl.ANY))
        aliases = {len(operands): 0}
        operands.append(into)
        shape = jax.ShapeDtypeStruct(into.shape, into.dtype)
    return pl.pallas_call(
        functools.partial(sum_tokens_kernel, rows, extra is not None),
        grid=(count,),
        in_specs=specs,
        out_specs=out,
        out_shape=shape,
        input_output_aliases=aliases,
        compiler_params=params(),
        cost_estimate=SMALL_COST,
        name="sum_tokens",
    )(*operands)


def project_kernel(heads_ref, far_w, own_w, out_ref):
    lanes = 4 * HEAD_DIM
    feats = far_w.shape[0]
    total = nn(heads_ref[:, :feats], far_w[...])
    out_ref[...] = (total + nn(heads_ref[:, lanes : lanes + feats], own_w[...])).astype(BF)


def project(heads, far_w, own_w, size):
    rows, lanes = heads.shape
    width = far_w.shape[1]
    return pl.pallas_call(
        project_kernel,
        grid=(3,),
        in_specs=[
            pl.BlockSpec((2 * size, lanes), lambda i: (i, 0)), fixed(far_w.shape), fixed(own_w.shape)
        ],
        out_specs=pl.BlockSpec((2 * size, width), lambda i: (i, 0)),
        out_shape=jax.ShapeDtypeStruct((rows, width), BF),
        compiler_params=params(),
        cost_estimate=SMALL_COST,
        name="project",
    )(heads, far_w, own_w)


def mid_backward_kernel(
    mid_ref, rstd_ref, own_ref, other_ref, bg_ref, vec_ref, far_w, own_w,
    rg_ref, ag_ref, atg_ref, sum_ref,
):
    step = pl.program_id(0)
    gain, shift = vec_ref[1:2, :], vec_ref[2:3, :]
    rstd = rstd_ref[:, 0:1]
    xhat = (mid_ref[...].astype(F32) - shift) * (1.0 / gain)
    mid_in = own_ref[...].astype(F32) + other_core(other_ref, step)
    gy = mid_in * gain
    through = rstd * (
        gy
        - jnp.mean(gy, axis=-1, keepdims=True)
        - xhat * jnp.mean(gy * xhat, axis=-1, keepdims=True)
    )
    total = bg_ref[...].astype(F32) + through
    low = total.astype(BF)
    ag_ref[...] = low
    lanes = 4 * HEAD_DIM
    feats = far_w.shape[0]
    for shard, w_ref in enumerate((far_w, own_w)):
        atg_ref[:, shard * lanes : shard * lanes + feats] = nt(low, w_ref[...]).astype(BF)
        atg_ref[:, shard * lanes + feats : (shard + 1) * lanes] = jnp.zeros(
            (low.shape[0], lanes - feats), BF
        )
    size = total.shape[0] // 2

    @pl.when(step == 0)
    def _():
        rg_ref[: 2 * size] = total
        sum_ref[...] = jnp.zeros_like(sum_ref)

    @pl.when(step == 2)
    def _():
        rg_ref[2 * size :] = total[:size]

    sum_ref[0:1, :] += jnp.sum(mid_in * xhat, axis=0, keepdims=True)
    sum_ref[1:2, :] += jnp.sum(mid_in, axis=0, keepdims=True)
    sum_ref[2:3, :] += jnp.sum(low.astype(F32), axis=0, keepdims=True)
    sum_ref[3:4, :] += jnp.sum(bg_ref[...].astype(F32), axis=0, keepdims=True)


def mid_backward(mid, rstd, own, other, bg, vectors, far_w, own_w, size):
    rows, width = own.shape
    lanes = 8 * HEAD_DIM
    block = pl.BlockSpec((2 * size, width), lambda i: (i, 0))
    return pl.pallas_call(
        mid_backward_kernel,
        grid=(3,),
        in_specs=[
            block,
            pl.BlockSpec((2 * size, 128), lambda i: (i, 0)),
            block,
            pl.BlockSpec((2 * size, width), lambda i: (other_pair(i), 0)),
            block,
            fixed((8, width)),
            fixed(far_w.shape),
            fixed(own_w.shape),
        ],
        out_specs=[
            pl.BlockSpec((rows // 2, width), lambda i: (0, 0)),
            block,
            pl.BlockSpec((2 * size, lanes), lambda i: (i, 0)),
            pl.BlockSpec((8, width), lambda i: (0, 0)),
        ],
        out_shape=[
            jax.ShapeDtypeStruct((rows // 2, width), F32),
            jax.ShapeDtypeStruct((rows, width), BF),
            jax.ShapeDtypeStruct((rows, lanes), BF),
            jax.ShapeDtypeStruct((8, width), F32),
        ],
        compiler_params=params(),
        cost_estimate=SMALL_COST,
        name="mid_backward",
    )(mid, rstd, own, other, bg, vectors, far_w, own_w)


def bias_row(ref):
    return ref[9 * HEAD_DIM : 9 * HEAD_DIM + 1].astype(F32)


def pad_heads(w_ref, padded_ref):
    lanes, feats = 4 * HEAD_DIM, 3 * HEAD_DIM
    for i in range(3):
        padded_ref[i * lanes : i * lanes + feats] = w_ref[i * feats : (i + 1) * feats]
        padded_ref[i * lanes + feats : (i + 1) * lanes] = jnp.zeros(
            (lanes - feats, w_ref.shape[1]), BF
        )


def first_kernel(x0, x1, x2, x3, vec_ref, far_ref, own_ref, normed_ref, qkv_ref, far_w, own_w, held_ref):
    @pl.when(pl.program_id(0) == 0)
    def _():
        pad_heads(far_ref, far_w)
        pad_heads(own_ref, own_w)

    stream = two_blocks(pl.program_id(0), (x0, x1, x2, x3), held_ref).astype(F32)
    centered = stream - jnp.mean(stream, axis=-1, keepdims=True)
    variance = jnp.mean(centered * centered, axis=-1, keepdims=True)
    normed = (
        centered * lax.rsqrt(variance + NORM_EPS) * vec_ref[4:5, :] + vec_ref[5:6, :]
    ).astype(BF)
    normed_ref[...] = normed
    third = far_w.shape[0]
    qkv_ref[:, :third] = (nt(normed, far_w[...]) + bias_row(far_ref)).astype(BF)
    qkv_ref[:, third:] = (nt(normed, own_w[...]) + bias_row(own_ref)).astype(BF)


def first(tokens, vectors, far, own, size):
    width = tokens[0].shape[1]
    rows = 8 * size
    outs = 6 * 4 * HEAD_DIM
    block = pl.BlockSpec((2 * size, width), lambda i: (i, 0))
    return pl.pallas_call(
        first_kernel,
        grid=(4,),
        in_specs=[fixed((2 * size, width))] * 4
        + [fixed((8, width)), fixed(far.shape), fixed(own.shape)],
        out_specs=[block, pl.BlockSpec((2 * size, outs), lambda i: (i, 0))],
        out_shape=[
            jax.ShapeDtypeStruct((rows, width), BF),
            jax.ShapeDtypeStruct((rows, outs), BF),
        ],
        scratch_shapes=[pltpu.VMEM((outs // 2, width), BF)] * 2
        + [pltpu.VMEM((2 * size, width), BF)],
        compiler_params=params(),
        cost_estimate=SMALL_COST,
        name="first_norm_qkv",
    )(*tokens, vectors, far, own)


def first_in_kernel(far_d, own_d, far_ref, own_w_ref, own_ref, give_ref, far_w, own_w):
    step = pl.program_id(0)
    half = far_d.shape[0] // 2

    @pl.when(step == 0)
    def _():
        pad_heads(far_ref, far_w)
        pad_heads(own_w_ref, own_w)

    total = (nn(far_d[...], far_w[...]) + nn(own_d[...], own_w[...])).astype(BF)

    @pl.when(step == 0)
    def _():
        own_ref[: 2 * half] = total

    @pl.when(step == 1)
    def _():
        give_ref[: 2 * half] = total

    @pl.when(step == 2)
    def _():
        own_ref[2 * half : 3 * half] = total[:half]
        give_ref[2 * half : 3 * half] = total[half:]

    @pl.when(step == 3)
    def _():
        own_ref[3 * half :] = total[:half]
        give_ref[3 * half :] = total[half:]


def first_in(far_grad, own_grad, far, own, size):
    rows, lanes = far_grad.shape
    width = far.shape[1]
    block = pl.BlockSpec((2 * size, lanes), lambda i: (i, 0))
    whole = pl.BlockSpec((rows // 2, width), lambda i: (0, 0))
    return pl.pallas_call(
        first_in_kernel,
        grid=(4,),
        in_specs=[block, block, fixed(far.shape), fixed(own.shape)],
        out_specs=[whole, whole],
        out_shape=[jax.ShapeDtypeStruct((rows // 2, width), BF)] * 2,
        scratch_shapes=[pltpu.VMEM((lanes, width), BF)] * 2,
        compiler_params=params(),
        cost_estimate=SMALL_COST,
        name="first_in",
    )(far_grad, own_grad, far, own)


def first_backward_kernel(home_ref, away_ref, own_ref, got_ref, rg_ref, vec_ref, *refs):
    extra_ref, (in_ref, sum_ref) = (refs[0] if len(refs) == 3 else None), refs[-2:]
    stream = jnp.where(pl.program_id(0) == 0, home_ref[...], away_ref[...]).astype(F32)
    centered = stream - jnp.mean(stream, axis=-1, keepdims=True)
    rstd = lax.rsqrt(jnp.mean(centered * centered, axis=-1, keepdims=True) + NORM_EPS)
    xhat = centered * rstd
    grad = own_ref[...].astype(F32) + got_ref[...].astype(F32)
    if extra_ref is not None:
        grad = grad + extra_ref[...].astype(F32)
    gy = grad * vec_ref[4:5, :]
    through = rstd * (
        gy
        - jnp.mean(gy, axis=-1, keepdims=True)
        - xhat * jnp.mean(gy * xhat, axis=-1, keepdims=True)
    )
    in_ref[...] = (rg_ref[...] + through).astype(BF)

    @pl.when(pl.program_id(0) == 0)
    def _():
        sum_ref[...] = jnp.zeros_like(sum_ref)

    sum_ref[0:1, :] += jnp.sum(grad * xhat, axis=0, keepdims=True)
    sum_ref[1:2, :] += jnp.sum(grad, axis=0, keepdims=True)


def first_backward(tokens, own, got, residual_grad, vectors, extra, size, owned):
    width = tokens[0].shape[1]
    stride = owned[1] - owned[0] if len(owned) > 1 else 1
    block = pl.BlockSpec((size, width), lambda i: (owned[0] + stride * i, 0))
    home = pl.BlockSpec((size, width), lambda i: (owned[0], 0))
    away = pl.BlockSpec((size, width), lambda i: (0, 0))
    more = () if extra is None else (extra,)
    return pl.pallas_call(
        first_backward_kernel,
        grid=(len(owned),),
        in_specs=[home, away, block, block, block, fixed((8, width))]
        + [pl.BlockSpec((size, width), lambda i: (0, 0))] * len(more),
        out_specs=[
            pl.BlockSpec((size, width), lambda i: (i, 0)),
            pl.BlockSpec((8, width), lambda i: (0, 0)),
        ],
        out_shape=[
            jax.ShapeDtypeStruct((len(owned) * size, width), BF),
            jax.ShapeDtypeStruct((8, width), F32),
        ],
        compiler_params=params(),
        cost_estimate=SMALL_COST,
        name="first_backward",
    )(tokens[0], tokens[2], own, got, residual_grad, vectors, *more)


def dp_partners(count, bit):
    return [(d, d ^ bit) for d in range(count)]


def dp_bits():
    return [1 << i for i in range(lax.axis_size("dp").bit_length() - 1)]


def dp_swap(value, bit):
    return lax.ppermute(value, "dp", dp_partners(lax.axis_size("dp"), bit))


def upper(bit):
    return (lax.axis_index("dp") & bit) != 0


def in_order(value, got, bit, axis=0):
    return jnp.where(
        upper(bit),
        jnp.concatenate([got, value], axis=axis),
        jnp.concatenate([value, got], axis=axis),
    )


def double(value, bit, axis=0):
    return in_order(value, dp_swap(value, bit), bit, axis)


def dp_part(value, axis):
    bits = dp_bits()
    place = sum(jnp.where(upper(bit), value.shape[axis] // (2 * bit), 0) for bit in bits)
    return lax.dynamic_slice_in_dim(value, place, value.shape[axis] // (2 * bits[-1]), axis)


def dp_stages():
    bits = dp_bits()
    return [bits[:1]] + [bits[i : i + 2] for i in range(1, len(bits), 2)]


def masks(bits):
    if len(bits) == 1:
        return [bits[0]]
    return [bits[1], bits[0], bits[0] | bits[1]]


def member(bits):
    place = jnp.where(upper(bits[-1]), 1, 0)
    return place if len(bits) == 1 else place + jnp.where(upper(bits[0]), 2, 0)


class Step:
    def whole(self, value):
        with jax.named_scope(self.name):
            kept, give = self.split(value)
            return self.join(kept, [dp_swap(x, mask) for x, mask in zip(give, self.masks)])


class Scatter(Step):
    def __init__(self, name, bits):
        self.name, self.masks = name, masks(bits)
        self.bits = bits

    def split(self, value):
        axis = value.ndim - 2
        rows = value.shape[axis] // (2 ** len(self.bits))
        mine = member(self.bits)
        pieces = [
            lax.dynamic_slice_in_dim(value, (mine ^ distance) * rows, rows, axis)
            for distance in range(2 ** len(self.bits))
        ]
        return pieces[0], [piece.astype(BF) for piece in pieces[1:]]

    def join(self, kept, got):
        total = kept.astype(F32)
        for piece in got:
            total = total + piece.astype(F32)
        return total


class Gather(Step):
    def __init__(self, name, bits):
        self.name, self.masks = name, masks(bits)
        self.bits = bits

    def split(self, value):
        value = value.astype(BF)
        return value, [value] * len(self.masks)

    def join(self, kept, got):
        if len(self.bits) == 1:
            return in_order(kept, got[0], self.bits[0])
        low = in_order(kept, got[0], self.bits[1])
        return in_order(low, in_order(got[1], got[2], self.bits[1]), self.bits[0])


class GatherAndAdd(Gather):
    def split(self, value):
        pieces, total = value
        rows = -(-total.shape[0] // 16) * 16
        total_low = jnp.pad(total.astype(BF), ((0, rows - total.shape[0]), (0, 0)))
        message = jnp.concatenate([total_low, pieces], axis=0)
        return (pieces, total), [message] * len(self.masks)

    def join(self, kept, got):
        pieces, total = kept
        rows = -(-total.shape[0] // 16) * 16
        for message in got:
            total = total + message[: total.shape[0]].astype(F32)
        return super().join(pieces, [message[rows:] for message in got]), total


def exchange(values, steps, *held):
    values, held = lax.optimization_barrier((tuple(values), held))
    halves = []
    for value, step in zip(values, steps):
        with jax.named_scope(step.name):
            halves.append(step.split(value))
    halves, held = lax.optimization_barrier((halves, held))
    joined = []
    for (kept, give), step in zip(halves, steps):
        with jax.named_scope(step.name):
            got = [dp_swap(piece, mask) for piece, mask in zip(give, step.masks)]
            joined.append((kept, got))

    def finish(*late):
        gots = [got for _, got in joined]
        gots, _ = lax.optimization_barrier((gots, late))
        out = []
        for (kept, _), got, step in zip(joined, gots, steps):
            with jax.named_scope(step.name):
                out.append(step.join(kept, got))
        return out

    return finish, held


def sum_over_tensor(value):
    return value + core_swap(value) + x_swap(value) + lax.ppermute(value, "tensor", DIAGONAL)


def after(value, *earlier):
    return lax.optimization_barrier((value,) + earlier)[0]


def body(
    hidden_in,
    doc_ids,
    first_gain,
    first_shift,
    qkv_weight,
    qv_bias,
    proj_weight,
    proj_bias,
    second_gain,
    second_shift,
    up_weight,
    up_bias,
    down_weight,
    down_bias,
    out_grad,
):
    size, rows_dev, width = hidden_in.shape
    length = doc_ids.shape[0]
    place = lax.axis_index("tensor")
    right = place >= 2
    feats = qkv_weight.shape[2]
    inner = up_weight.shape[1]

    def split_rows(value):
        first, mid, last = value[:, 0], value[:, 1], value[:, 2]
        return jnp.where(right, last, first), mid, jnp.where(right, first, last)

    def join_rows(main, mid, other):
        return jnp.stack(
            [jnp.where(right, other, main), mid, jnp.where(right, main, other)], axis=1
        )

    def head_sums(sums_own, sums_far, up_sums):
        slots = []
        for own, away in (
            (up_sums[0:1], up_sums[1:2]),
            (sums_own[:2, :feats].reshape(1, -1), sums_far[:2, :feats].reshape(1, -1)),
        ):
            index = lax.broadcasted_iota(jnp.int32, (4, own.shape[1]), 0)
            value = jnp.where(index == place, own, jnp.where(index == place ^ 2, away, 0.0))
            slots.append(value.reshape(-1, width))
        return slots

    pieces = jnp.stack([dp_part(up_weight, 0), dp_part(down_weight, 0)])
    with jax.named_scope("mlp_weights_x"):
        far_mlp = x_swap(pieces)

    space = jnp.zeros((4 * HEAD_DIM - feats,), BF)
    biases = jnp.concatenate(
        [qv_bias[0], space, jnp.zeros((4 * HEAD_DIM,), BF), qv_bias[1], space, up_bias]
    ).reshape(2, width)
    qkv_own = jnp.concatenate(
        [
            jnp.transpose(qkv_weight, (1, 2, 0)).reshape(3 * feats, width),
            jnp.pad(biases, ((0, 14), (0, 0))),
        ],
        axis=0,
    )

    main, mid, away = split_rows(hidden_in)
    home = jnp.concatenate([main, mid], axis=0)
    with jax.named_scope("tokens"):
        far = x_swap(jnp.concatenate([away, mid], axis=0))
        near = core_swap(home)
        far_near = core_swap(far)
    tokens = (home, near, far, far_near)

    with jax.named_scope("qkv_weights_x"):
        qkv_far = x_swap(qkv_own)
    local_ids = lax.dynamic_slice_in_dim(doc_ids, place * size, size, 0)
    cot = jnp.where((local_ids >= 0)[:, :, None], out_grad, jnp.zeros_like(out_grad))
    g_main, g_mid, g_away = split_rows(cot)
    g_home = jnp.concatenate([g_main, g_mid], axis=0)
    start_rows, table, vectors = prepare(
        doc_ids,
        place,
        (proj_bias, second_gain, second_shift, down_bias, first_gain, first_shift),
        size,
    )

    with jax.named_scope("mlp_weights_dp"):
        far_mlp, qkv_own, g_home, g_away = lax.optimization_barrier(
            (far_mlp, qkv_own, g_home, g_away)
        )
        for bit in reversed(dp_bits()[1:]):
            far_mlp, table, start_rows, vectors = lax.optimization_barrier(
                (double(far_mlp, bit, 1), table, start_rows, vectors)
            )
        far_mlp, held, tokens = lax.optimization_barrier((far_mlp, qkv_far, tokens))
        got_mlp = dp_swap(far_mlp, dp_bits()[0])

    with jax.named_scope("cotangent"):
        g_near = core_swap(g_home)
        g_far = x_swap(after(g_away, held))
        g_far_near = lax.ppermute(after(g_away, held), "tensor", DIAGONAL)

    with jax.named_scope("proj_weight_x"):
        proj_far = x_swap(after(proj_weight, held))
    normed, qkv = first(tokens, vectors, held, qkv_own, size)
    attended, lse = attend_forward(qkv, table, start_rows, size)
    attn_part = project(after(attended, g_far, g_near, g_far_near, got_mlp), proj_far, proj_weight, size)
    with jax.named_scope("attn_core"):
        attn_other = core_swap(attn_part)
    far_mlp = in_order(far_mlp, got_mlp, dp_bits()[0], 1)

    mid_rstd, normed_mid, act, hidden_grad, out_own, out_give, mid_part, up_sums, branch_grad = mlp(
        tokens, attn_part, attn_other, (g_home, g_near, g_far, g_far_near), vectors, qkv_own, held,
        up_weight, down_weight, far_mlp, size,
    )

    stages = dp_stages()
    first_stage, high_stages = stages[0], stages[1:]

    d, u, t = "down_grad_dp", "up_proj_grad_dp", "qkv_grad_dp"
    singles = [[bit] for bit in dp_bits()[1:]]

    with jax.named_scope("mid_core"):
        mid_other = core_swap(mid_part)
    up_away = sum_tokens(normed_mid, hidden_grad, part=1)
    with jax.named_scope("up_grad_x"):
        up_got = x_swap(up_away)

    down = sum_tokens(act, after(branch_grad, up_away), parts=2).reshape(2, inner, width)
    finish, (mid_rstd, mid_part, attended, hidden_grad, out_give) = exchange(
        [down], [Scatter(d, first_stage)], mid_rstd, mid_part, attended, hidden_grad, out_give
    )
    residual_grad, attn_grad, attended_grad, mid_sums = mid_backward(
        normed_mid, mid_rstd, mid_part, mid_other, branch_grad, vectors,
        proj_far, proj_weight, size,
    )
    proj_away = sum_tokens(attended, attn_grad, rows=feats, count=1)
    with jax.named_scope("proj_grad_x"):
        proj_got = x_swap(proj_away)
    d_far, sums_far = attend_backward(
        qkv, attended, after(attended_grad, proj_away), lse, table, start_rows, size, 0
    )
    qkv_away = sum_tokens(d_far, normed, rows=feats)
    with jax.named_scope("qkv_grad_x"):
        qkv_got = x_swap(qkv_away)
    (down,) = finish(qkv_away)

    finish, (attended_grad, out_give) = exchange(
        [down], [Scatter(d, singles[0])], after(attended_grad, qkv_away), out_give
    )
    with jax.named_scope("block_out"):
        out_got = core_swap(out_give)
    d_own, sums_own = attend_backward(
        qkv, attended, attended_grad, lse, table, start_rows, size, 1
    )
    (down,) = finish(d_own)

    finish, (d_own, up_got, out_got, hidden_grad) = exchange(
        [down], [Scatter(d, singles[1])], d_own, up_got, out_got, hidden_grad
    )
    up = sum_tokens(normed_mid, hidden_grad, up_got, room=feats)
    up, qkv_got, proj_got = lax.optimization_barrier((up, qkv_got, proj_got))
    up = sum_tokens(
        attended, attn_grad, proj_got, rows=feats, first=1, count=1, into=up
    )
    (down,) = finish(up)
    for bits in singles[2:]:
        finish, _ = exchange([down], [Scatter(d, bits)])
        (down,) = finish()
    down_own, down_away = down[0], down[1].astype(BF)

    finish_up, (d_own, qkv_got, down_own, down_away) = exchange(
        [up], [Scatter(u, first_stage)], d_own, qkv_got, down_own, down_away
    )
    with jax.named_scope("down_grad_x"):
        down_got = x_swap(down_away)
    tail = sum_tokens(d_own, normed, qkv_got, rows=feats)
    down_got, tail = lax.optimization_barrier((down_got, tail))
    down = down_own + down_got.astype(F32)

    down_gathers = [Gather(d, bits) for bits in reversed(singles)] + [Gather(d, first_stage)]
    for step in down_gathers[:-3]:
        finish, _ = exchange([down], [step])
        (down,) = finish()
    steps = [Scatter(t, first_stage), down_gathers[-3]]
    finish, (d_own, out_got) = exchange([tail, down], steps, d_own, out_got)
    own_in, give_in = first_in(d_far, d_own, held, qkv_own, size)
    with jax.named_scope("block_out"):
        out_full = (out_own + out_got.astype(F32)).astype(BF)
        out_away = x_swap(out_full[2 * size :])
    (up,) = finish_up(own_in, out_away)

    finish_high, (own_in, give_in) = exchange(
        [up], [Scatter(u, high_stages[0])], own_in, give_in
    )
    tail, down = finish()
    finish, (own_in, give_in) = exchange([down], [down_gathers[-2]], own_in, give_in)
    with jax.named_scope("first_core"):
        got_in = core_swap(give_in)
    mid_sum = (own_in[3 * size :].astype(F32) + got_in[3 * size :].astype(F32)).astype(BF)
    with jax.named_scope("first_mid_x"):
        extra = x_swap(mid_sum)
    in_main, sums_main = first_backward(
        tokens, own_in, got_in, residual_grad, vectors, None, size, (0, 2)
    )
    (up,) = finish_high(in_main)
    (down,) = finish(in_main)
    for bits in high_stages[1:]:
        finish, _ = exchange([up], [Scatter(u, bits)])
        (up,) = finish()

    up_gathers = [Gather(u, bits) for bits in reversed(singles)] + [Gather(u, first_stage)]
    for step in up_gathers[:-3]:
        finish, _ = exchange([up], [step])
        (up,) = finish()
    steps = [Scatter(t, high_stages[0]), up_gathers[-3], down_gathers[-1]]
    finish, (in_main, extra, out_full, out_away) = exchange(
        [tail, up, down], steps, in_main, extra, out_full, out_away
    )
    block_out = join_rows(out_full[:size], out_full[size : 2 * size], out_away)
    in_mid, sums_mid = first_backward(
        tokens, own_in, got_in, residual_grad, vectors, extra, size, (1,)
    )
    tail, up, down = finish(in_mid, block_out)
    for bits in high_stages[1:]:
        finish, _ = exchange([tail], [Scatter(t, bits)])
        (tail,) = finish()
    small = jnp.concatenate(
        [(sums_main + sums_mid)[:2], 0.5 * mid_sums[:4], *head_sums(sums_own, sums_far, up_sums)],
        axis=0,
    )

    steps = [Gather(t, first_stage), up_gathers[-2]]
    finish, (small, in_main, down) = exchange([tail, up], steps, small, in_main, down)
    with jax.named_scope("small_sums"):
        small = sum_over_tensor(small)
        small = small + dp_swap(small, first_stage[0])
    with jax.named_scope("in_grad_x"):
        in_away = x_swap(after(in_main[size:], small))
    down = down.astype(F32)
    tail, up = finish(small, down)

    last = high_stages[-1] if len(high_stages[-1]) == 2 else high_stages[-2]
    for bits in reversed([bits for bits in high_stages if bits is not last]):
        finish, _ = exchange([(tail, small)], [GatherAndAdd(t, bits)])
        ((tail, small),) = finish()
    finish_up, (tail, small) = exchange([up], [up_gathers[-1]], tail, small)
    finish, _ = exchange([(tail, small)], [GatherAndAdd(t, last)])
    (up,) = finish_up()
    up_weight_grad, proj_weight_grad = up[:inner].astype(F32), up[inner:].astype(F32)
    ((tail, small),) = finish(up_weight_grad, proj_weight_grad)
    tail = tail.reshape(-1, 2, tail.shape[0] // (2 ** len(dp_bits())), width)
    tail = jnp.transpose(tail, (1, 0, 2, 3)).reshape(3 * feats, width)

    in_grad = join_rows(in_main[:size], in_mid, in_away)

    up_bias_grad = lax.dynamic_slice_in_dim(small, 6 + place, 1, 0)[0]
    qv_all = small[10:].reshape(4, 2, feats)
    qv_bias_grad = lax.dynamic_slice_in_dim(qv_all, place, 1, 0)[0]

    qkv_weight_grad = jnp.transpose(
        tail.reshape(3, feats, width), (2, 0, 1)
    ).astype(F32)
    return (
        block_out,
        in_grad,
        small[0],
        small[1],
        qkv_weight_grad,
        qv_bias_grad,
        proj_weight_grad,
        small[4],
        small[2],
        small[3],
        up_weight_grad,
        up_bias_grad,
        down,
        small[5],
    )


def solution(mesh):
    in_specs = (
        P("tensor", "dp", None),
        P(None, "dp"),
        P(),
        P(),
        P(None, None, "tensor"),
        P(None, "tensor"),
        P("tensor", None),
        P(),
        P(),
        P(),
        P(None, "tensor"),
        P("tensor"),
        P("tensor", None),
        P(),
        P("tensor", "dp", None),
    )
    out_specs = (
        P("tensor", "dp", None),
        P("tensor", "dp", None),
        P(),
        P(),
        P(None, None, "tensor"),
        P(None, "tensor"),
        P("tensor", None),
        P(),
        P(),
        P(),
        P(None, "tensor"),
        P("tensor"),
        P("tensor", None),
        P(),
    )
    return jax.shard_map(body, mesh=mesh, in_specs=in_specs, out_specs=out_specs, check_vma=False)
```

```python
import functools

import jax
import jax.numpy as jnp
from jax import lax
from jax.experimental import pallas as pl
from jax.experimental.pallas import tpu as pltpu
from jax.sharding import PartitionSpec as P

HEAD_DIM = 64
NORM_EPS = 1e-05
MASKED = -1e30
BF = jnp.bfloat16
F32 = jnp.float32
VMEM_LIMIT = 56 * 1024 * 1024

SLOT = ((0, 2, 4, 5), (1, 3, 6, 7))
SLOT_ROW = (0, 1, 0, 1, 0, 0)
SLOT_K = (0, 0, 1, 1, 2, 3)
X_SWAP = ((0, 2), (1, 3), (2, 0), (3, 1))
CORE_SWAP = ((0, 1), (1, 0), (2, 3), (3, 2))
DIAGONAL = ((0, 3), (1, 2), (2, 1), (3, 0))


def x_swap(value):
    return lax.ppermute(value, "tensor", X_SWAP)


def core_swap(value):
    return lax.ppermute(value, "tensor", CORE_SWAP)


def params(semantics=None):
    return pltpu.CompilerParams(vmem_limit_bytes=VMEM_LIMIT)


def fixed(shape):
    return pl.BlockSpec(shape, lambda *ids: (0,) * len(shape), pipeline_mode=pl.Buffered(1))


def nt(left, right):
    return lax.dot_general(left, right, (((1,), (1,)), ((), ())), preferred_element_type=F32)


def nn(left, right):
    return lax.dot_general(left, right, (((1,), (0,)), ((), ())), preferred_element_type=F32)


def tn(left, right):
    return lax.dot_general(left, right, (((0,), (0,)), ((), ())), preferred_element_type=F32)


SMALL_COST = pl.CostEstimate(flops=1, bytes_accessed=1, transcendentals=0)


def key_mask(start_row, key_first, keys, size, diagonal):
    key = lax.broadcasted_iota(jnp.int32, (keys, size), 0)
    mask = key >= start_row - key_first
    if diagonal:
        mask = mask & (key <= lax.broadcasted_iota(jnp.int32, (keys, size), 1))
    return mask


KEYS = 128


def key_rows(table, row, first, size):
    return table[3 + row, first // size] * size + first % size


def head_rows(size):
    lane = lax.broadcasted_iota(jnp.int32, (size, 2 * HEAD_DIM), 1)

    def select(value):
        zero = jnp.zeros((size, 2 * HEAD_DIM), value.dtype)
        pair = value[:, : 2 * HEAD_DIM]
        return (
            jnp.where(lane < HEAD_DIM, pair, zero),
            jnp.where(lane < HEAD_DIM, zero, pair),
            value[:, 2 * HEAD_DIM :],
        )

    return select


def pair_lanes(value, head):
    first = 2 * HEAD_DIM * (head // 2)
    return value[:, first : first + 2 * HEAD_DIM]


def attend_forward_kernel(size, table, start_ref, *refs):
    parts = (refs[:3], refs[3:6])
    out_ref, lse_ref = refs[6:]
    slot = pl.program_id(0)
    row, block, low = table[0, slot], table[1, slot], table[2, slot]
    start_row = start_ref[0:1, :]
    select = head_rows(size)
    heads = [
        head for q_ref, _, _ in parts for head in select(q_ref[...] * jnp.asarray(HEAD_DIM**-0.5, BF))
    ]
    count = len(heads)

    def load(first, keys):
        at = pl.multiple_of(key_rows(table, row, first, size), keys)
        loaded = [
            (k_ref[pl.ds(at, keys), :], jnp.transpose(v_ref[pl.ds(at, keys), :]))
            for _, k_ref, v_ref in parts
        ]
        scores = [
            nt(pair_lanes(loaded[head // 3][0], head % 3), heads[head]) for head in range(count)
        ]
        values = [
            loaded[head // 3][1][head % 3 * HEAD_DIM : (head % 3 + 1) * HEAD_DIM]
            for head in range(count)
        ]
        return scores, values

    all_scores, values = load(block * size, size)
    mask = key_mask(start_row, block * size, size, size, True)
    carry = []
    for head in range(count):
        scores = jnp.where(mask, all_scores[head], MASKED)
        top = jnp.max(scores, axis=0, keepdims=True)
        weight = jnp.exp(scores - top)
        total = jnp.sum(weight, axis=0, keepdims=True)
        carry += [top, total, nn(values[head], weight.astype(BF))]

    def earlier(step, carry):
        first = block * size - (step + 1) * KEYS
        all_scores, values = load(first, KEYS)
        mask = key_mask(start_row, first, KEYS, size, False)
        new = []
        for head in range(count):
            top, total, acc = carry[3 * head : 3 * head + 3]
            scores = jnp.where(mask, all_scores[head], MASKED)
            higher = jnp.maximum(top, jnp.max(scores, axis=0, keepdims=True))
            shrink = jnp.exp(top - higher)
            weight = jnp.exp(scores - higher)
            total = total * shrink + jnp.sum(weight, axis=0, keepdims=True)
            new += [higher, total, acc * shrink + nn(values[head], weight.astype(BF))]
        return tuple(new)

    carry = lax.fori_loop(0, block * (size // KEYS) - low, earlier, tuple(carry))
    for shard in range(2):
        rows = []
        for head in range(3 * shard, 3 * shard + 3):
            rows.append(carry[3 * head + 2] / carry[3 * head + 1])
            at = 8 * shard + head % 3
            lse_ref[at : at + 1, :] = carry[3 * head] + jnp.log(carry[3 * head + 1])
        rows.append(jnp.zeros_like(rows[0]))
        lanes = slice(4 * HEAD_DIM * shard, 4 * HEAD_DIM * (shard + 1))
        out_ref[:, lanes] = jnp.transpose(jnp.concatenate(rows, axis=0)).astype(BF)


def attend_forward(qkv, table, starts, size):
    width = 4 * HEAD_DIM
    tokens = qkv.shape[0]
    specs = [pl.BlockSpec((8, size), lambda s, *_: (0, s))]
    for shard in range(2):
        specs += [
            pl.BlockSpec((size, width), functools.partial(lambda c, s, *_: (s, c), 3 * shard)),
            pl.BlockSpec((tokens, width), functools.partial(lambda c, s, *_: (0, c), 3 * shard + 1)),
            pl.BlockSpec((tokens, width), functools.partial(lambda c, s, *_: (0, c), 3 * shard + 2)),
        ]
    return pl.pallas_call(
        functools.partial(attend_forward_kernel, size),
        grid_spec=pltpu.PrefetchScalarGridSpec(
            num_scalar_prefetch=1,
            grid=(6,),
            in_specs=specs,
            out_specs=[
                pl.BlockSpec((size, 2 * width), lambda s, *_: (s, 0)),
                pl.BlockSpec((16, size), lambda s, *_: (0, s)),
            ],
        ),
        out_shape=[
            jax.ShapeDtypeStruct((6 * size, 2 * width), BF),
            jax.ShapeDtypeStruct((16, 6 * size), F32),
        ],
        compiler_params=params(),
        cost_estimate=SMALL_COST,
        name="attend_forward",
    )(table, starts, *[qkv] * 6)


def attend_backward_kernel(
    size, table, start_ref, q_ref, k_ref, v_ref, out_ref, grad_ref, lse_ref,
    d_ref, sum_ref, dk_acc, dv_acc,
):
    slot = pl.program_id(0)
    width = 4 * HEAD_DIM
    row, block, low = table[0, slot], table[1, slot], table[2, slot]
    start_row = start_ref[0:1, :]
    select = head_rows(size)
    q_heads = select(q_ref[...] * jnp.asarray(HEAD_DIM**-0.5, BF))
    grad = grad_ref[...]
    g_heads = select(grad)
    products = jnp.transpose(grad.astype(F32) * out_ref[...].astype(F32))
    deltas = [
        jnp.sum(products[head * HEAD_DIM : (head + 1) * HEAD_DIM], axis=0, keepdims=True)
        for head in range(3)
    ]

    @pl.when(slot == 0)
    def _():
        dk_acc[...] = jnp.zeros_like(dk_acc)
        dv_acc[...] = jnp.zeros_like(dv_acc)
        sum_ref[...] = jnp.zeros_like(sum_ref)

    def one_block(first, keys, diagonal):
        at = pl.multiple_of(key_rows(table, row, first, size), keys)
        key, value = k_ref[pl.ds(at, keys), :], v_ref[pl.ds(at, keys), :]
        key_t = jnp.transpose(key)
        mask = key_mask(start_row, first, keys, size, diagonal)
        all_scores = [nt(pair_lanes(key, head), q_heads[head]) for head in range(3)]
        all_grads = [nt(pair_lanes(value, head), g_heads[head]) for head in range(3)]
        dq_parts, dk_parts, dv_parts = [], [], []
        for head in range(3):
            scores = jnp.where(mask, all_scores[head], MASKED)
            prob = jnp.exp(scores - lse_ref[head : head + 1, :])
            score_grad = (prob * (all_grads[head] - deltas[head])).astype(BF)
            dk_parts.append(nn(score_grad, q_heads[head]))
            dv_parts.append(nn(prob.astype(BF), g_heads[head]))
            dq_parts.append(nn(key_t[head * HEAD_DIM : (head + 1) * HEAD_DIM], score_grad))
        dk_acc[pl.ds(at, keys), : width // 2] += dk_parts[0] + dk_parts[1]
        dk_acc[pl.ds(at, keys), width // 2 :] += dk_parts[2]
        dv_acc[pl.ds(at, keys), : width // 2] += dv_parts[0] + dv_parts[1]
        dv_acc[pl.ds(at, keys), width // 2 :] += dv_parts[2]
        return jnp.concatenate(dq_parts, axis=0)

    dq_t = one_block(block * size, size, True)
    dq_t = lax.fori_loop(
        0,
        block * (size // KEYS) - low,
        lambda step, acc: acc + one_block(block * size - (step + 1) * KEYS, KEYS, False),
        dq_t,
    )
    dq_t = jnp.concatenate([dq_t, jnp.zeros((HEAD_DIM, size), F32)], axis=0)
    dq = (jnp.transpose(dq_t) * HEAD_DIM**-0.5).astype(BF)
    d_ref[pl.ds(pl.multiple_of(slot * size, size), size), :width] = dq
    sum_ref[0:1, :] += jnp.sum(dq.astype(F32), axis=0, keepdims=True)

    @pl.when(slot == pl.num_programs(0) - 1)
    def _():
        d_ref[6 * size :, :width] = jnp.zeros((2 * size, width), BF)
        d_ref[:, width : 2 * width] = dk_acc[...].astype(BF)
        dv = dv_acc[...].astype(BF)
        d_ref[:, 2 * width :] = dv
        sum_ref[1:2, :] = jnp.sum(dv.astype(F32), axis=0, keepdims=True)


def attend_backward(qkv, attended, grad, lse, table, starts, size, shard):
    tokens = qkv.shape[0]
    width = 4 * HEAD_DIM
    block = pl.BlockSpec((size, width), lambda s, *_: (s, shard))
    return pl.pallas_call(
        functools.partial(attend_backward_kernel, size),
        grid_spec=pltpu.PrefetchScalarGridSpec(
            num_scalar_prefetch=1,
            grid=(6,),
            in_specs=[
                pl.BlockSpec((8, size), lambda s, *_: (0, s)),
                pl.BlockSpec((size, width), lambda s, *_: (s, 3 * shard)),
                pl.BlockSpec((tokens, width), lambda s, *_: (0, 3 * shard + 1)),
                pl.BlockSpec((tokens, width), lambda s, *_: (0, 3 * shard + 2)),
                block,
                block,
                pl.BlockSpec((8, size), lambda s, *_: (shard, s)),
            ],
            out_specs=[
                pl.BlockSpec((tokens, 3 * width), lambda s, *_: (0, 0)),
                pl.BlockSpec((8, width), lambda s, *_: (0, 0)),
            ],
            scratch_shapes=[pltpu.VMEM((tokens, width), F32), pltpu.VMEM((tokens, width), F32)],
        ),
        out_shape=[
            jax.ShapeDtypeStruct((tokens, 3 * width), BF),
            jax.ShapeDtypeStruct((8, width), F32),
        ],
        compiler_params=params(),
        cost_estimate=SMALL_COST,
        name="attend_backward",
    )(table, starts, qkv, qkv, qkv, attended, grad, lse)


def prepare_kernel(size, place_ref, ids_ref, *refs):
    vectors, (start_ref, table_ref, vec_ref, rows_ref) = refs[:-4], refs[-4:]
    for i, ref in enumerate(vectors):
        vec_ref[i : i + 1, :] = ref[...].astype(F32).reshape(1, -1)
    vec_ref[len(vectors) :, :] = jnp.zeros((8 - len(vectors), vec_ref.shape[1]), F32)
    place = place_ref[0]
    ids = ids_ref[...]
    length = ids.shape[1]
    position = lax.broadcasted_iota(jnp.int32, ids.shape, 1)
    starts = position
    for doc in range(8):
        here = ids == doc
        first_one = jnp.min(jnp.where(here, position, length), axis=1, keepdims=True)
        starts = jnp.where(here, first_one, starts)
    rows_ref[...] = starts
    for i in range(8):
        for j in range(8):
            table_ref[i, j] = 0
    for slot in range(6):
        row, block = SLOT_ROW[slot], SLOT_K[slot] ^ place
        source = jnp.where(place >= 2, 2, 0) if row == 0 else 1
        at = pl.ds(pl.multiple_of(block * size, size), size)
        first_row, second_row, third_row = rows_ref[0:1, at], rows_ref[1:2, at], rows_ref[2:3, at]
        mine = second_row if row else jnp.where(source == 2, third_row, first_row)
        start_ref[:, slot * size : (slot + 1) * size] = jnp.broadcast_to(mine, (8, size))
        table_ref[0, slot] = row
        table_ref[1, slot] = block
        table_ref[2, slot] = jnp.min(mine) // KEYS
    for row in range(2):
        for block in range(4):
            slots = SLOT[row]
            near = block ^ place
            table_ref[3 + row, block] = jnp.where(
                near < 2,
                jnp.where(near == 0, slots[0], slots[1]),
                jnp.where(near == 2, slots[2], slots[3]),
            )


def prepare(doc_ids, place, vectors, size):
    ids = jnp.pad(jnp.transpose(doc_ids), ((0, 5), (0, 0)), constant_values=-1)
    vmem, smem = pl.BlockSpec(memory_space=pltpu.VMEM), pl.BlockSpec(memory_space=pltpu.SMEM)
    return pl.pallas_call(
        functools.partial(prepare_kernel, size),
        in_specs=[smem, vmem] + [vmem] * len(vectors),
        out_specs=[vmem, smem, vmem],
        out_shape=[
            jax.ShapeDtypeStruct((8, 6 * size), jnp.int32),
            jax.ShapeDtypeStruct((8, 8), jnp.int32),
            jax.ShapeDtypeStruct((8, vectors[0].shape[0]), F32),
        ],
        scratch_shapes=[pltpu.VMEM(ids.shape, jnp.int32)],
        cost_estimate=SMALL_COST,
        name="prepare",
    )(place.reshape(1).astype(jnp.int32), ids, *vectors)


GELU_C = 0.7978845608028654
GELU_A = 0.044715


def two_blocks(step, refs, held_ref):
    home_ref, near_ref, far_ref, far_near_ref = refs
    half = home_ref.shape[0] // 2

    @pl.when(step == 0)
    def _():
        held_ref[...] = home_ref[...]

    @pl.when(step == 1)
    def _():
        held_ref[...] = near_ref[...]

    @pl.when(step == 2)
    def _():
        held_ref[:half] = far_ref[:half]
        held_ref[half:] = far_near_ref[:half]

    if far_ref.shape[0] > half:

        @pl.when(step == 3)
        def _():
            held_ref[:half] = far_ref[half:]
            held_ref[half:] = far_near_ref[half:]

    return held_ref[...]


def other_core(ref, step):
    value = ref[...].astype(F32)
    half = value.shape[0] // 2
    turned = jnp.concatenate([value[half:], value[:half]], axis=0)
    return jnp.where(step == 2, turned, value)


def other_pair(step):
    return jnp.where(step == 2, 2, 1 - step)


def mlp_kernel(
    x0, x1, x2, x3, own_ref, other_ref, b0, b1, b2, b3, vec_ref, upb_own, upb_far, up_own, up_far, dn_own, dn_far,
    rstd_ref, mid_ref, act_ref, hg_ref, out_ref, give_ref, midin_ref, upbg_ref, bg_ref, held_ref,
):
    step = pl.program_id(0)
    proj_bias, gain, shift = vec_ref[0:1, :], vec_ref[1:2, :], vec_ref[2:3, :]
    residual = two_blocks(step, (x0, x1, x2, x3), held_ref).astype(F32) + own_ref[...].astype(F32)
    residual = residual + other_core(other_ref, step) + proj_bias
    centered = residual - jnp.mean(residual, axis=-1, keepdims=True)
    variance = jnp.mean(centered * centered, axis=-1, keepdims=True)
    rstd = lax.rsqrt(variance + NORM_EPS)
    rstd_ref[...] = jnp.broadcast_to(rstd, rstd_ref.shape)
    mid = (centered * rstd * gain + shift).astype(BF)
    mid_ref[...] = mid
    bg = two_blocks(step, (b0, b1, b2, b3), bg_ref)

    @pl.when(step == 0)
    def _():
        upbg_ref[...] = jnp.zeros_like(upbg_ref)

    out = None
    midin = None
    weights = ((up_own[...], dn_own[...], upb_own[...]), (up_far[0], dn_far[0], upb_far[...]))
    for part, (up_w, dn_w, up_bias) in enumerate(weights):
        hidden = nn(mid, up_w) + up_bias[1:2].astype(F32)
        act_grad = nt(bg, dn_w)
        square = hidden * hidden
        bent = jnp.tanh(GELU_C * (hidden + GELU_A * hidden * square))
        half = 0.5 * (1.0 + bent)
        act = (hidden * half).astype(BF)
        slope = half + 0.5 * hidden * (1.0 - bent * bent) * (GELU_C + 3.0 * GELU_C * GELU_A * square)
        grad = (act_grad * slope).astype(BF)
        act_ref[part] = act
        hg_ref[part] = grad
        upbg_ref[part : part + 1, :] += jnp.sum(grad.astype(F32), axis=0, keepdims=True)
        out_part = nn(act, dn_w)
        midin_part = nt(grad, up_w)
        out = out_part if out is None else out + out_part
        midin = midin_part if midin is None else midin + midin_part
    midin_ref[...] = midin.astype(BF)
    size = out.shape[0] // 2

    @pl.when(step == 0)
    def _():
        out_ref[: 2 * size] = out + residual + vec_ref[3:4, :]

    @pl.when(step == 1)
    def _():
        give_ref[: 2 * size] = out.astype(BF)

    @pl.when(step == 2)
    def _():
        out_ref[2 * size :] = (out + residual)[:size] + vec_ref[3:4, :]
        give_ref[2 * size :] = out[size:].astype(BF)


def mlp(tokens, own, other, bg, vectors, qkv_own, qkv_far, up_own, down_own, far, size):
    rows, width = own.shape
    inner = up_own.shape[1]
    block = pl.BlockSpec((2 * size, width), lambda i: (i, 0))
    wide = pl.BlockSpec((2, 2 * size, inner), lambda i: (0, i, 0))
    half = pl.BlockSpec((rows // 2, width), lambda i: (0, 0))
    return pl.pallas_call(
        mlp_kernel,
        grid=(3,),
        in_specs=[fixed((2 * size, width))] * 4
        + [
            block,
            pl.BlockSpec((2 * size, width), lambda i: (other_pair(i), 0)),
        ]
        + [fixed(value.shape) for value in bg]
        + [
            fixed((8, width)),
            pl.BlockSpec((16, width), lambda i: (9 * HEAD_DIM // 16, 0)),
            pl.BlockSpec((16, width), lambda i: (9 * HEAD_DIM // 16, 0)),
            fixed((width, inner)),
            pl.BlockSpec((1, width, inner), lambda i: (0, 0, 0), pipeline_mode=pl.Buffered(1)),
            fixed((inner, width)),
            pl.BlockSpec((1, inner, width), lambda i: (1, 0, 0), pipeline_mode=pl.Buffered(1)),
        ],
        out_specs=[
            pl.BlockSpec((2 * size, 128), lambda i: (i, 0)),
            block, wide, wide, half, half, block,
            pl.BlockSpec((8, inner), lambda i: (0, 0)),
            block,
        ],
        out_shape=[
            jax.ShapeDtypeStruct((rows, 128), F32),
            jax.ShapeDtypeStruct((rows, width), BF),
            jax.ShapeDtypeStruct((2, rows, inner), BF),
            jax.ShapeDtypeStruct((2, rows, inner), BF),
            jax.ShapeDtypeStruct((rows // 2, width), F32),
            jax.ShapeDtypeStruct((rows // 2, width), BF),
            jax.ShapeDtypeStruct((rows, width), BF),
            jax.ShapeDtypeStruct((8, inner), F32),
            jax.ShapeDtypeStruct((rows, width), BF),
        ],
        scratch_shapes=[pltpu.VMEM((2 * size, width), BF)],
        compiler_params=params(),
        cost_estimate=SMALL_COST,
        name="mlp",
    )(*tokens, own, other, *bg, vectors, qkv_own, qkv_far, up_own, far, down_own, far)


def sum_tokens_kernel(rows, has_extra, left_ref, right_ref, *refs):
    left = left_ref[0] if len(left_ref.shape) == 3 else left_ref[...]
    right = right_ref[0] if len(right_ref.shape) == 3 else right_ref[...]
    total = tn(left, right)[:rows]
    if has_extra:
        total = total + refs[0][...].astype(F32)
    refs[-1][...] = total.astype(refs[-1].dtype)


def sum_tokens(
    left, right, extra=None, dtype=BF, part=0, parts=1, rows=256, first=0, count=None, room=0, into=None
):
    block = 256
    blocks = left.shape[-1] // block
    count = count or parts * blocks
    tokens, width = right.shape[-2:]

    def spec(value, lanes, at):
        if value.ndim == 3 and parts > 1:
            return pl.BlockSpec((1, tokens, lanes), lambda i: (i // blocks, 0, i % blocks))
        if value.ndim == 3:
            return pl.BlockSpec((1, tokens, lanes), lambda i: (part, 0, at(i)))
        return pl.BlockSpec((tokens, lanes), lambda i: (0, at(i)))

    base = 0 if into is None else into.shape[0] // rows - count
    out = pl.BlockSpec((rows, width), lambda i: (base + i, 0))
    specs = [spec(left, block, lambda i: first + i), spec(right, width, lambda i: 0)]
    operands = [left, right]
    if extra is not None:
        specs.append(pl.BlockSpec((rows, width), lambda i: (i, 0)))
        operands.append(extra)
    aliases = {}
    shape = jax.ShapeDtypeStruct((count * rows + room, width), dtype)
    if into is not None:
        specs.append(pl.BlockSpec(memory_space=pl.ANY))
        aliases = {len(operands): 0}
        operands.append(into)
        shape = jax.ShapeDtypeStruct(into.shape, into.dtype)
    return pl.pallas_call(
        functools.partial(sum_tokens_kernel, rows, extra is not None),
        grid=(count,),
        in_specs=specs,
        out_specs=out,
        out_shape=shape,
        input_output_aliases=aliases,
        compiler_params=params(),
        cost_estimate=SMALL_COST,
        name="sum_tokens",
    )(*operands)


def project_kernel(heads_ref, far_w, own_w, out_ref):
    lanes = 4 * HEAD_DIM
    feats = far_w.shape[0]
    total = nn(heads_ref[:, :feats], far_w[...])
    out_ref[...] = (total + nn(heads_ref[:, lanes : lanes + feats], own_w[...])).astype(BF)


def project(heads, far_w, own_w, size):
    rows, lanes = heads.shape
    width = far_w.shape[1]
    return pl.pallas_call(
        project_kernel,
        grid=(3,),
        in_specs=[
            pl.BlockSpec((2 * size, lanes), lambda i: (i, 0)), fixed(far_w.shape), fixed(own_w.shape)
        ],
        out_specs=pl.BlockSpec((2 * size, width), lambda i: (i, 0)),
        out_shape=jax.ShapeDtypeStruct((rows, width), BF),
        compiler_params=params(),
        cost_estimate=SMALL_COST,
        name="project",
    )(heads, far_w, own_w)


def mid_backward_kernel(
    mid_ref, rstd_ref, own_ref, other_ref, bg_ref, vec_ref, far_w, own_w,
    rg_ref, ag_ref, atg_ref, sum_ref,
):
    step = pl.program_id(0)
    gain, shift = vec_ref[1:2, :], vec_ref[2:3, :]
    rstd = rstd_ref[:, 0:1]
    xhat = (mid_ref[...].astype(F32) - shift) * (1.0 / gain)
    mid_in = own_ref[...].astype(F32) + other_core(other_ref, step)
    gy = mid_in * gain
    through = rstd * (
        gy
        - jnp.mean(gy, axis=-1, keepdims=True)
        - xhat * jnp.mean(gy * xhat, axis=-1, keepdims=True)
    )
    total = bg_ref[...].astype(F32) + through
    low = total.astype(BF)
    ag_ref[...] = low
    lanes = 4 * HEAD_DIM
    feats = far_w.shape[0]
    for shard, w_ref in enumerate((far_w, own_w)):
        atg_ref[:, shard * lanes : shard * lanes + feats] = nt(low, w_ref[...]).astype(BF)
        atg_ref[:, shard * lanes + feats : (shard + 1) * lanes] = jnp.zeros(
            (low.shape[0], lanes - feats), BF
        )
    size = total.shape[0] // 2

    @pl.when(step == 0)
    def _():
        rg_ref[: 2 * size] = total
        sum_ref[...] = jnp.zeros_like(sum_ref)

    @pl.when(step == 2)
    def _():
        rg_ref[2 * size :] = total[:size]

    sum_ref[0:1, :] += jnp.sum(mid_in * xhat, axis=0, keepdims=True)
    sum_ref[1:2, :] += jnp.sum(mid_in, axis=0, keepdims=True)
    sum_ref[2:3, :] += jnp.sum(low.astype(F32), axis=0, keepdims=True)
    sum_ref[3:4, :] += jnp.sum(bg_ref[...].astype(F32), axis=0, keepdims=True)


def mid_backward(mid, rstd, own, other, bg, vectors, far_w, own_w, size):
    rows, width = own.shape
    lanes = 8 * HEAD_DIM
    block = pl.BlockSpec((2 * size, width), lambda i: (i, 0))
    return pl.pallas_call(
        mid_backward_kernel,
        grid=(3,),
        in_specs=[
            block,
            pl.BlockSpec((2 * size, 128), lambda i: (i, 0)),
            block,
            pl.BlockSpec((2 * size, width), lambda i: (other_pair(i), 0)),
            block,
            fixed((8, width)),
            fixed(far_w.shape),
            fixed(own_w.shape),
        ],
        out_specs=[
            pl.BlockSpec((rows // 2, width), lambda i: (0, 0)),
            block,
            pl.BlockSpec((2 * size, lanes), lambda i: (i, 0)),
            pl.BlockSpec((8, width), lambda i: (0, 0)),
        ],
        out_shape=[
            jax.ShapeDtypeStruct((rows // 2, width), F32),
            jax.ShapeDtypeStruct((rows, width), BF),
            jax.ShapeDtypeStruct((rows, lanes), BF),
            jax.ShapeDtypeStruct((8, width), F32),
        ],
        compiler_params=params(),
        cost_estimate=SMALL_COST,
        name="mid_backward",
    )(mid, rstd, own, other, bg, vectors, far_w, own_w)


def bias_row(ref):
    return ref[9 * HEAD_DIM : 9 * HEAD_DIM + 1].astype(F32)


def pad_heads(w_ref, padded_ref):
    lanes, feats = 4 * HEAD_DIM, 3 * HEAD_DIM
    for i in range(3):
        padded_ref[i * lanes : i * lanes + feats] = w_ref[i * feats : (i + 1) * feats]
        padded_ref[i * lanes + feats : (i + 1) * lanes] = jnp.zeros(
            (lanes - feats, w_ref.shape[1]), BF
        )


def first_kernel(x0, x1, x2, x3, vec_ref, far_ref, own_ref, normed_ref, qkv_ref, far_w, own_w, held_ref):
    @pl.when(pl.program_id(0) == 0)
    def _():
        pad_heads(far_ref, far_w)
        pad_heads(own_ref, own_w)

    stream = two_blocks(pl.program_id(0), (x0, x1, x2, x3), held_ref).astype(F32)
    centered = stream - jnp.mean(stream, axis=-1, keepdims=True)
    variance = jnp.mean(centered * centered, axis=-1, keepdims=True)
    normed = (
        centered * lax.rsqrt(variance + NORM_EPS) * vec_ref[4:5, :] + vec_ref[5:6, :]
    ).astype(BF)
    normed_ref[...] = normed
    third = far_w.shape[0]
    qkv_ref[:, :third] = (nt(normed, far_w[...]) + bias_row(far_ref)).astype(BF)
    qkv_ref[:, third:] = (nt(normed, own_w[...]) + bias_row(own_ref)).astype(BF)


def first(tokens, vectors, far, own, size):
    width = tokens[0].shape[1]
    rows = 8 * size
    outs = 6 * 4 * HEAD_DIM
    block = pl.BlockSpec((2 * size, width), lambda i: (i, 0))
    return pl.pallas_call(
        first_kernel,
        grid=(4,),
        in_specs=[fixed((2 * size, width))] * 4
        + [fixed((8, width)), fixed(far.shape), fixed(own.shape)],
        out_specs=[block, pl.BlockSpec((2 * size, outs), lambda i: (i, 0))],
        out_shape=[
            jax.ShapeDtypeStruct((rows, width), BF),
            jax.ShapeDtypeStruct((rows, outs), BF),
        ],
        scratch_shapes=[pltpu.VMEM((outs // 2, width), BF)] * 2
        + [pltpu.VMEM((2 * size, width), BF)],
        compiler_params=params(),
        cost_estimate=SMALL_COST,
        name="first_norm_qkv",
    )(*tokens, vectors, far, own)


def first_in_kernel(far_d, own_d, far_ref, own_w_ref, own_ref, give_ref, far_w, own_w):
    step = pl.program_id(0)
    half = far_d.shape[0] // 2

    @pl.when(step == 0)
    def _():
        pad_heads(far_ref, far_w)
        pad_heads(own_w_ref, own_w)

    total = (nn(far_d[...], far_w[...]) + nn(own_d[...], own_w[...])).astype(BF)

    @pl.when(step == 0)
    def _():
        own_ref[: 2 * half] = total

    @pl.when(step == 1)
    def _():
        give_ref[: 2 * half] = total

    @pl.when(step == 2)
    def _():
        own_ref[2 * half : 3 * half] = total[:half]
        give_ref[2 * half : 3 * half] = total[half:]

    @pl.when(step == 3)
    def _():
        own_ref[3 * half :] = total[:half]
        give_ref[3 * half :] = total[half:]


def first_in(far_grad, own_grad, far, own, size):
    rows, lanes = far_grad.shape
    width = far.shape[1]
    block = pl.BlockSpec((2 * size, lanes), lambda i: (i, 0))
    whole = pl.BlockSpec((rows // 2, width), lambda i: (0, 0))
    return pl.pallas_call(
        first_in_kernel,
        grid=(4,),
        in_specs=[block, block, fixed(far.shape), fixed(own.shape)],
        out_specs=[whole, whole],
        out_shape=[jax.ShapeDtypeStruct((rows // 2, width), BF)] * 2,
        scratch_shapes=[pltpu.VMEM((lanes, width), BF)] * 2,
        compiler_params=params(),
        cost_estimate=SMALL_COST,
        name="first_in",
    )(far_grad, own_grad, far, own)


def first_backward_kernel(home_ref, away_ref, own_ref, got_ref, rg_ref, vec_ref, *refs):
    extra_ref, (in_ref, sum_ref) = (refs[0] if len(refs) == 3 else None), refs[-2:]
    stream = jnp.where(pl.program_id(0) == 0, home_ref[...], away_ref[...]).astype(F32)
    centered = stream - jnp.mean(stream, axis=-1, keepdims=True)
    rstd = lax.rsqrt(jnp.mean(centered * centered, axis=-1, keepdims=True) + NORM_EPS)
    xhat = centered * rstd
    grad = own_ref[...].astype(F32) + got_ref[...].astype(F32)
    if extra_ref is not None:
        grad = grad + extra_ref[...].astype(F32)
    gy = grad * vec_ref[4:5, :]
    through = rstd * (
        gy
        - jnp.mean(gy, axis=-1, keepdims=True)
        - xhat * jnp.mean(gy * xhat, axis=-1, keepdims=True)
    )
    in_ref[...] = (rg_ref[...] + through).astype(BF)

    @pl.when(pl.program_id(0) == 0)
    def _():
        sum_ref[...] = jnp.zeros_like(sum_ref)

    sum_ref[0:1, :] += jnp.sum(grad * xhat, axis=0, keepdims=True)
    sum_ref[1:2, :] += jnp.sum(grad, axis=0, keepdims=True)


def first_backward(tokens, own, got, residual_grad, vectors, extra, size, owned):
    width = tokens[0].shape[1]
    stride = owned[1] - owned[0] if len(owned) > 1 else 1
    block = pl.BlockSpec((size, width), lambda i: (owned[0] + stride * i, 0))
    home = pl.BlockSpec((size, width), lambda i: (owned[0], 0))
    away = pl.BlockSpec((size, width), lambda i: (0, 0))
    more = () if extra is None else (extra,)
    return pl.pallas_call(
        first_backward_kernel,
        grid=(len(owned),),
        in_specs=[home, away, block, block, block, fixed((8, width))]
        + [pl.BlockSpec((size, width), lambda i: (0, 0))] * len(more),
        out_specs=[
            pl.BlockSpec((size, width), lambda i: (i, 0)),
            pl.BlockSpec((8, width), lambda i: (0, 0)),
        ],
        out_shape=[
            jax.ShapeDtypeStruct((len(owned) * size, width), BF),
            jax.ShapeDtypeStruct((8, width), F32),
        ],
        compiler_params=params(),
        cost_estimate=SMALL_COST,
        name="first_backward",
    )(tokens[0], tokens[2], own, got, residual_grad, vectors, *more)


def dp_partners(count, bit):
    return [(d, d ^ bit) for d in range(count)]


def dp_bits():
    return [1 << i for i in range(lax.axis_size("dp").bit_length() - 1)]


def dp_swap(value, bit):
    return lax.ppermute(value, "dp", dp_partners(lax.axis_size("dp"), bit))


def upper(bit):
    return (lax.axis_index("dp") & bit) != 0


def in_order(value, got, bit, axis=0):
    return jnp.where(
        upper(bit),
        jnp.concatenate([got, value], axis=axis),
        jnp.concatenate([value, got], axis=axis),
    )


def double(value, bit, axis=0):
    return in_order(value, dp_swap(value, bit), bit, axis)


def dp_part(value, axis):
    bits = dp_bits()
    place = sum(jnp.where(upper(bit), value.shape[axis] // (2 * bit), 0) for bit in bits)
    return lax.dynamic_slice_in_dim(value, place, value.shape[axis] // (2 * bits[-1]), axis)


def dp_stages():
    bits = dp_bits()
    return [bits[:1]] + [bits[i : i + 2] for i in range(1, len(bits), 2)]


def masks(bits):
    if len(bits) == 1:
        return [bits[0]]
    return [bits[1], bits[0], bits[0] | bits[1]]


def member(bits):
    place = jnp.where(upper(bits[-1]), 1, 0)
    return place if len(bits) == 1 else place + jnp.where(upper(bits[0]), 2, 0)


class Step:
    def whole(self, value):
        with jax.named_scope(self.name):
            kept, give = self.split(value)
            return self.join(kept, [dp_swap(x, mask) for x, mask in zip(give, self.masks)])


class Scatter(Step):
    def __init__(self, name, bits):
        self.name, self.masks = name, masks(bits)
        self.bits = bits

    def piece(self, value, distance):
        axis = value.ndim - 2
        rows = value.shape[axis] // (2 ** len(self.bits))
        return lax.dynamic_slice_in_dim(value, (member(self.bits) ^ distance) * rows, rows, axis)

    def split(self, value):
        give = range(1, 2 ** len(self.bits))
        return value, [self.piece(value, distance).astype(BF) for distance in give]

    def join(self, kept, got):
        total = self.piece(kept, 0).astype(F32)
        for piece in got:
            total = total + piece.astype(F32)
        return total


class Gather(Step):
    def __init__(self, name, bits):
        self.name, self.masks = name, masks(bits)
        self.bits = bits

    def split(self, value):
        value = value.astype(BF)
        return value, [value] * len(self.masks)

    def join(self, kept, got):
        if len(self.bits) == 1:
            return in_order(kept, got[0], self.bits[0])
        low = in_order(kept, got[0], self.bits[1])
        return in_order(low, in_order(got[1], got[2], self.bits[1]), self.bits[0])


class GatherAndAdd(Gather):
    def split(self, value):
        pieces, total = value
        rows = -(-total.shape[0] // 16) * 16
        total_low = jnp.pad(total.astype(BF), ((0, rows - total.shape[0]), (0, 0)))
        message = jnp.concatenate([total_low, pieces], axis=0)
        return (pieces, total), [message] * len(self.masks)

    def join(self, kept, got):
        pieces, total = kept
        rows = -(-total.shape[0] // 16) * 16
        for message in got:
            total = total + message[: total.shape[0]].astype(F32)
        return super().join(pieces, [message[rows:] for message in got]), total


def exchange(values, steps, *held):
    values, held = lax.optimization_barrier((tuple(values), held))
    halves = []
    for value, step in zip(values, steps):
        with jax.named_scope(step.name):
            halves.append(step.split(value))
    halves, held = lax.optimization_barrier((halves, held))
    joined = []
    for (kept, give), step in zip(halves, steps):
        with jax.named_scope(step.name):
            got = [dp_swap(piece, mask) for piece, mask in zip(give, step.masks)]
            joined.append((kept, got))

    def finish(*late):
        gots = [got for _, got in joined]
        gots, _ = lax.optimization_barrier((gots, late))
        out = []
        for (kept, _), got, step in zip(joined, gots, steps):
            with jax.named_scope(step.name):
                out.append(step.join(kept, got))
        return out

    return finish, held


def sum_over_tensor(value):
    return value + core_swap(value) + x_swap(value) + lax.ppermute(value, "tensor", DIAGONAL)


def after(value, *earlier):
    return lax.optimization_barrier((value,) + earlier)[0]


def body(
    hidden_in,
    doc_ids,
    first_gain,
    first_shift,
    qkv_weight,
    qv_bias,
    proj_weight,
    proj_bias,
    second_gain,
    second_shift,
    up_weight,
    up_bias,
    down_weight,
    down_bias,
    out_grad,
):
    size, rows_dev, width = hidden_in.shape
    length = doc_ids.shape[0]
    place = lax.axis_index("tensor")
    right = place >= 2
    feats = qkv_weight.shape[2]
    inner = up_weight.shape[1]

    def split_rows(value):
        first, mid, last = value[:, 0], value[:, 1], value[:, 2]
        return jnp.where(right, last, first), mid, jnp.where(right, first, last)

    def join_rows(main, mid, other):
        return jnp.stack(
            [jnp.where(right, other, main), mid, jnp.where(right, main, other)], axis=1
        )

    def head_sums(sums_own, sums_far, up_sums):
        slots = []
        for own, away in (
            (up_sums[0:1], up_sums[1:2]),
            (sums_own[:2, :feats].reshape(1, -1), sums_far[:2, :feats].reshape(1, -1)),
        ):
            index = lax.broadcasted_iota(jnp.int32, (4, own.shape[1]), 0)
            value = jnp.where(index == place, own, jnp.where(index == place ^ 2, away, 0.0))
            slots.append(value.reshape(-1, width))
        return slots

    pieces = jnp.stack([dp_part(up_weight, 0), dp_part(down_weight, 0)])
    with jax.named_scope("mlp_weights_x"):
        far_mlp = x_swap(pieces)

    space = jnp.zeros((4 * HEAD_DIM - feats,), BF)
    biases = jnp.concatenate(
        [qv_bias[0], space, jnp.zeros((4 * HEAD_DIM,), BF), qv_bias[1], space, up_bias]
    ).reshape(2, width)
    qkv_own = jnp.concatenate(
        [
            jnp.transpose(qkv_weight, (1, 2, 0)).reshape(3 * feats, width),
            jnp.pad(biases, ((0, 14), (0, 0))),
        ],
        axis=0,
    )

    main, mid, away = split_rows(hidden_in)
    home = jnp.concatenate([main, mid], axis=0)
    with jax.named_scope("tokens"):
        far = x_swap(jnp.concatenate([away, mid], axis=0))
        near = core_swap(home)
        far_near = core_swap(far)
    tokens = (home, near, far, far_near)

    with jax.named_scope("qkv_weights_x"):
        qkv_far = x_swap(qkv_own)
    local_ids = lax.dynamic_slice_in_dim(doc_ids, place * size, size, 0)
    cot = jnp.where((local_ids >= 0)[:, :, None], out_grad, jnp.zeros_like(out_grad))
    g_main, g_mid, g_away = split_rows(cot)
    g_home = jnp.concatenate([g_main, g_mid], axis=0)
    start_rows, table, vectors = prepare(
        doc_ids,
        place,
        (proj_bias, second_gain, second_shift, down_bias, first_gain, first_shift),
        size,
    )

    with jax.named_scope("mlp_weights_dp"):
        far_mlp, qkv_own, g_home, g_away = lax.optimization_barrier(
            (far_mlp, qkv_own, g_home, g_away)
        )
        for bit in reversed(dp_bits()[1:]):
            far_mlp, table, start_rows, vectors = lax.optimization_barrier(
                (double(far_mlp, bit, 1), table, start_rows, vectors)
            )
        far_mlp, held, tokens = lax.optimization_barrier((far_mlp, qkv_far, tokens))
        got_mlp = dp_swap(far_mlp, dp_bits()[0])

    with jax.named_scope("cotangent"):
        g_near = core_swap(g_home)
        g_far = x_swap(after(g_away, held))
        g_far_near = lax.ppermute(after(g_away, held), "tensor", DIAGONAL)

    with jax.named_scope("proj_weight_x"):
        proj_far = x_swap(after(proj_weight, held))
    normed, qkv = first(tokens, vectors, held, qkv_own, size)
    attended, lse = attend_forward(qkv, table, start_rows, size)
    attn_part = project(after(attended, g_far, g_near, g_far_near, got_mlp), proj_far, proj_weight, size)
    with jax.named_scope("attn_core"):
        attn_other = core_swap(attn_part)
    far_mlp = in_order(far_mlp, got_mlp, dp_bits()[0], 1)

    mid_rstd, normed_mid, act, hidden_grad, out_own, out_give, mid_part, up_sums, branch_grad = mlp(
        tokens, attn_part, attn_other, (g_home, g_near, g_far, g_far_near), vectors, qkv_own, held,
        up_weight, down_weight, far_mlp, size,
    )

    stages = dp_stages()
    first_stage, high_stages = stages[0], stages[1:]

    d, u, t = "down_grad_dp", "up_proj_grad_dp", "qkv_grad_dp"
    singles = [[bit] for bit in dp_bits()[1:]]

    with jax.named_scope("mid_core"):
        mid_other = core_swap(mid_part)
    up_away = sum_tokens(normed_mid, hidden_grad, part=1)
    with jax.named_scope("up_grad_x"):
        up_got = x_swap(up_away)

    down = sum_tokens(act, after(branch_grad, up_away), parts=2).reshape(2, inner, width)
    finish, (mid_rstd, mid_part, attended, hidden_grad, out_give) = exchange(
        [down], [Scatter(d, first_stage)], mid_rstd, mid_part, attended, hidden_grad, out_give
    )
    residual_grad, attn_grad, attended_grad, mid_sums = mid_backward(
        normed_mid, mid_rstd, mid_part, mid_other, branch_grad, vectors,
        proj_far, proj_weight, size,
    )
    proj_away = sum_tokens(attended, attn_grad, rows=feats, count=1)
    with jax.named_scope("proj_grad_x"):
        proj_got = x_swap(proj_away)
    d_far, sums_far = attend_backward(
        qkv, attended, after(attended_grad, proj_away), lse, table, start_rows, size, 0
    )
    qkv_away = sum_tokens(d_far, normed, rows=feats)
    with jax.named_scope("qkv_grad_x"):
        qkv_got = x_swap(qkv_away)
    (down,) = finish(qkv_away)

    finish, (attended_grad, out_give) = exchange(
        [down], [Scatter(d, singles[0])], after(attended_grad, qkv_away), out_give
    )
    with jax.named_scope("block_out"):
        out_got = core_swap(out_give)
    d_own, sums_own = attend_backward(
        qkv, attended, attended_grad, lse, table, start_rows, size, 1
    )
    (down,) = finish(d_own)

    finish, (d_own, up_got, out_got, hidden_grad) = exchange(
        [down], [Scatter(d, singles[1])], d_own, up_got, out_got, hidden_grad
    )
    up = sum_tokens(normed_mid, hidden_grad, up_got, room=feats)
    up, qkv_got, proj_got = lax.optimization_barrier((up, qkv_got, proj_got))
    up = sum_tokens(
        attended, attn_grad, proj_got, rows=feats, first=1, count=1, into=up
    )
    (down,) = finish(up)
    for bits in singles[2:]:
        finish, _ = exchange([down], [Scatter(d, bits)])
        (down,) = finish()
    down_own, down_away = down[0], down[1].astype(BF)

    finish_up, (d_own, qkv_got, down_own, down_away) = exchange(
        [up], [Scatter(u, first_stage)], d_own, qkv_got, down_own, down_away
    )
    with jax.named_scope("down_grad_x"):
        down_got = x_swap(down_away)
    tail = sum_tokens(d_own, normed, qkv_got, rows=feats)
    down_got, tail = lax.optimization_barrier((down_got, tail))
    down = down_own + down_got.astype(F32)

    down_gathers = [Gather(d, bits) for bits in reversed(singles)] + [Gather(d, first_stage)]
    for step in down_gathers[:-3]:
        finish, _ = exchange([down], [step])
        (down,) = finish()
    steps = [Scatter(t, first_stage), down_gathers[-3]]
    finish, (d_own, out_got) = exchange([tail, down], steps, d_own, out_got)
    own_in, give_in = first_in(d_far, d_own, held, qkv_own, size)
    with jax.named_scope("block_out"):
        out_full = (out_own + out_got.astype(F32)).astype(BF)
        out_away = x_swap(out_full[2 * size :])
    (up,) = finish_up(own_in, out_away)

    finish_high, (own_in, give_in) = exchange(
        [up], [Scatter(u, high_stages[0])], own_in, give_in
    )
    tail, down = finish()
    finish, (own_in, give_in) = exchange([down], [down_gathers[-2]], own_in, give_in)
    with jax.named_scope("first_core"):
        got_in = core_swap(give_in)
    mid_sum = (own_in[3 * size :].astype(F32) + got_in[3 * size :].astype(F32)).astype(BF)
    with jax.named_scope("first_mid_x"):
        extra = x_swap(mid_sum)
    in_main, sums_main = first_backward(
        tokens, own_in, got_in, residual_grad, vectors, None, size, (0, 2)
    )
    (up,) = finish_high(in_main)
    (down,) = finish(in_main)
    for bits in high_stages[1:]:
        finish, _ = exchange([up], [Scatter(u, bits)])
        (up,) = finish()

    up_gathers = [Gather(u, bits) for bits in reversed(singles)] + [Gather(u, first_stage)]
    for step in up_gathers[:-3]:
        finish, _ = exchange([up], [step])
        (up,) = finish()
    steps = [Scatter(t, high_stages[0]), up_gathers[-3], down_gathers[-1]]
    finish, (in_main, extra, out_full, out_away) = exchange(
        [tail, up, down], steps, in_main, extra, out_full, out_away
    )
    block_out = join_rows(out_full[:size], out_full[size : 2 * size], out_away)
    in_mid, sums_mid = first_backward(
        tokens, own_in, got_in, residual_grad, vectors, extra, size, (1,)
    )
    tail, up, down = finish(in_mid, block_out)
    for bits in high_stages[1:]:
        finish, _ = exchange([tail], [Scatter(t, bits)])
        (tail,) = finish()
    small = jnp.concatenate(
        [(sums_main + sums_mid)[:2], 0.5 * mid_sums[:4], *head_sums(sums_own, sums_far, up_sums)],
        axis=0,
    )

    steps = [Gather(t, first_stage), up_gathers[-2]]
    finish, (small, in_main, down) = exchange([tail, up], steps, small, in_main, down)
    with jax.named_scope("small_sums"):
        small = sum_over_tensor(small)
        small = small + dp_swap(small, first_stage[0])
    with jax.named_scope("in_grad_x"):
        in_away = x_swap(after(in_main[size:], small))
    down = down.astype(F32)
    tail, up = finish(small, down)

    last = high_stages[-1] if len(high_stages[-1]) == 2 else high_stages[-2]
    for bits in reversed([bits for bits in high_stages if bits is not last]):
        finish, _ = exchange([(tail, small)], [GatherAndAdd(t, bits)])
        ((tail, small),) = finish()
    finish_up, (tail, small) = exchange([up], [up_gathers[-1]], tail, small)
    finish, _ = exchange([(tail, small)], [GatherAndAdd(t, last)])
    (up,) = finish_up()
    up_weight_grad, proj_weight_grad = up[:inner].astype(F32), up[inner:].astype(F32)
    ((tail, small),) = finish(up_weight_grad, proj_weight_grad)
    tail = tail.reshape(-1, 2, tail.shape[0] // (2 ** len(dp_bits())), width)
    tail = jnp.transpose(tail, (1, 0, 2, 3)).reshape(3 * feats, width)

    in_grad = join_rows(in_main[:size], in_mid, in_away)

    up_bias_grad = lax.dynamic_slice_in_dim(small, 6 + place, 1, 0)[0]
    qv_all = small[10:].reshape(4, 2, feats)
    qv_bias_grad = lax.dynamic_slice_in_dim(qv_all, place, 1, 0)[0]

    qkv_weight_grad = jnp.transpose(
        tail.reshape(3, feats, width), (2, 0, 1)
    ).astype(F32)
    return (
        block_out,
        in_grad,
        small[0],
        small[1],
        qkv_weight_grad,
        qv_bias_grad,
        proj_weight_grad,
        small[4],
        small[2],
        small[3],
        up_weight_grad,
        up_bias_grad,
        down,
        small[5],
    )


def solution(mesh):
    in_specs = (
        P("tensor", "dp", None),
        P(None, "dp"),
        P(),
        P(),
        P(None, None, "tensor"),
        P(None, "tensor"),
        P("tensor", None),
        P(),
        P(),
        P(),
        P(None, "tensor"),
        P("tensor"),
        P("tensor", None),
        P(),
        P("tensor", "dp", None),
    )
    out_specs = (
        P("tensor", "dp", None),
        P("tensor", "dp", None),
        P(),
        P(),
        P(None, None, "tensor"),
        P(None, "tensor"),
        P("tensor", None),
        P(),
        P(),
        P(),
        P(None, "tensor"),
        P("tensor"),
        P("tensor", None),
        P(),
    )
    return jax.shard_map(body, mesh=mesh, in_specs=in_specs, out_specs=out_specs, check_vma=False)
```
